32 devices in a mesh: ctx: 4 (over y, x), exp: 8 (over z, core).
Axes of the slice: x: 2, y: 2, z: 4, core: 2. Of those that a mesh axis runs over, the one named last changes fastest.
Arguments:
- residual: bfloat16 [512, 4096], P('ctx'), may hold values from -4 to 4
- ssm_input: bfloat16 [512, 8192], P('ctx', 'exp'), may hold values from -16 to 16
- ssm_gate: bfloat16 [512, 8192], P('ctx', 'exp'), may hold values from -5 to 5
- write_vectors: bfloat16 [512, 128], P('ctx'), may hold values from -1.75 to 1.75
- read_vectors: bfloat16 [512, 128], P('ctx'), may hold values from -1.75 to 1.75
- step_logits: float32 [128, 512], P('exp', 'ctx'), may hold values from -2 to 1536
- decay_log: float32 [128], P('exp'), may hold values from -12 to -2
- skip_gain: float32 [128], P('exp'), may hold values from 0.5 to 3
- norm_gain: float32 [8192], P('exp'), may hold values from 0.1 to 1.9
- out_weight: bfloat16 [8192, 4096], P('exp', 'ctx'), may hold values from -0.09375 to 0.09375
- moe_gain: float32 [4096], replicated, may hold values from 0.1 to 1.9
- gate_weight: bfloat16 [8, 4096, 12288], P('exp', None, 'ctx'), may hold values from -0.09375 to 0.09375
- up_weight: bfloat16 [8, 4096, 12288], P('exp', None, 'ctx'), may hold values from -0.09375 to 0.09375
- down_weight: bfloat16 [8, 12288, 4096], P('exp', 'ctx'), may hold values from -0.0546875 to 0.0546875
- expert_ids: int32 [512, 2], P('ctx'), may hold values from 0 to 7, all different within a row; in each aligned block of 128 rows (0 to 127, 128 to 255, ...) at most 64 rows name the same one
- route_weight: float32 [512, 2], P('ctx'), may hold values from 0.5 to 1.5
Outputs:
- layer_out: bfloat16 [512, 4096], P('ctx', 'exp')
The draws below stay inside these ranges and needn't reach their ends.
Inputs may be any that keep to these rules, and one draw needn't show every extreme that they name: `expert_ids`: each row names 2 different experts. Among the 128 rows of one index of ctx no expert is named by more than 64 rows, and in every draw some expert is named by exactly 64 of them.
All inputs are finite; a program needn't handle non-finite values.
Results may differ from the reference program's by a relative error of at most 0.023.
Values may be sent and summed in bfloat16 or wider, within the bound.
A program may use at most 192 MiB of HBM per device.

```python
import math
import jax
import jax.numpy as jnp
import numpy as np
from jax import lax

D = 4096
SSM_HEADS = 128
HEAD_DIM = 64
STATE = 128
SPAN = 128
NORM_GROUP = 512
EXPERTS = 8
FF = 12288
TOP = 2
TOK_CTX = 128
WINDOW_TOKENS = 512
INNER = 8192
PIECES = 8
FF_PART = 12288
CAP = 64
N_CTX = 4
N_EXP = 8


def spike_positions(key):
    return jax.random.randint(jax.random.fold_in(key, 29), (2,), 0, WINDOW_TOKENS)


def spike_token_rows(key):
    token_positions = spike_positions(key)
    return jnp.any(jnp.arange(WINDOW_TOKENS)[:, None] == token_positions[None, :], axis=1)


def scaled_field(key, row_count, col_count):
    key_rows, key_cols, key_vals = jax.random.split(key, 3)
    row_scale = 10.0 ** jax.random.uniform(key_rows, (row_count, 1), jnp.float32, -0.5, 0.5)
    col_scale = 10.0 ** jax.random.uniform(key_cols, (1, col_count), jnp.float32, -0.5, 0.5)
    values = 0.5 * jnp.clip(jax.random.normal(key_vals, (row_count, col_count), jnp.float32), -3.0, 3.0)
    return values * row_scale * col_scale


def decay_plan(key):
    key_kind, key_slow, key_fast = jax.random.split(jax.random.fold_in(key, 17), 3)
    slow_share = 0.5
    slow_head_mask = jax.random.uniform(key_kind, (SSM_HEADS,), jnp.float32) < slow_share
    slow_rate = jax.random.uniform(key_slow, (SSM_HEADS,), jnp.float32, 0.2, 0.9) / WINDOW_TOKENS
    fast_rate = 1.0 / jax.random.uniform(key_fast, (SSM_HEADS,), jnp.float32, 20.0, 40.0)
    return (jnp.where(slow_head_mask, slow_rate, fast_rate), slow_head_mask)


def draw_residual(key, part):
    return (0.25 * scaled_field(jax.random.fold_in(key, 3), WINDOW_TOKENS, D)).astype(jnp.bfloat16)


def draw_ssm_input(key, part):
    signal_field_values = scaled_field(jax.random.fold_in(key, 5), WINDOW_TOKENS, INNER)
    token_at_spike = spike_token_rows(key)
    return jnp.where(token_at_spike[:, None], signal_field_values / WINDOW_TOKENS, signal_field_values).astype(jnp.bfloat16)


def draw_decay_log(key, part):
    decay_rate_by_head = decay_plan(key)[0]
    return jnp.log(decay_rate_by_head).astype(jnp.float32)


def draw_step_logits(key, part):
    decay_rate_by_head, slow_head_mask = decay_plan(key)
    key_base, key_phase, key_loss = jax.random.split(jax.random.fold_in(key, 23), 3)
    base_step = 10.0 ** jax.random.uniform(key_base, (SSM_HEADS, WINDOW_TOKENS), jnp.float32, -0.4, 0.2)
    phase_shift = jax.random.uniform(key_phase, (SSM_HEADS, 1), jnp.float32, 0.0, 1.0)
    position_ramp = jnp.arange(WINDOW_TOKENS, dtype=jnp.float32)[None, :] / WINDOW_TOKENS
    wave_factor = jnp.exp(0.6 * jnp.sin(6.283185307 * (position_ramp + phase_shift)))
    steady_level = base_step * wave_factor
    balance_loss_share = jax.random.uniform(key_loss, (SSM_HEADS, 1), jnp.float32, 0.22, 0.51)
    spike_step_size = jnp.where(slow_head_mask[:, None], balance_loss_share / decay_rate_by_head[:, None], 3.0)
    token_at_spike = spike_token_rows(key)
    step_size_value = jnp.where(token_at_spike[None, :], spike_step_size, steady_level)
    return (step_size_value + jnp.log(-jnp.expm1(-step_size_value))).astype(jnp.float32)


def raised(result, rng, source, target, blocks, factor):
    def block_of(position):
        return (jnp.arange(result.shape[position]) // (result.shape[position] // blocks)).reshape((-1,) + (1,) * (result.ndim - 1 - position))

    first = jax.random.permutation(rng, blocks)[block_of(target)]
    far = (block_of(target) + blocks // 2) % blocks
    return jnp.where((block_of(source) == first) | (block_of(source) == far), factor * result, result)


def level_of(key, dims, cuts, smallest, high):
    gain = 1.0
    for axis_at, parts in cuts:
        steps = jax.random.uniform(jax.random.fold_in(jax.random.fold_in(key, 6), axis_at), (parts,), jnp.float32, smallest / len(cuts), high / len(cuts))
        gain = gain * jnp.repeat(jnp.exp(steps), dims[axis_at] // parts).reshape((-1,) + (1,) * (len(dims) - 1 - axis_at))
    return gain


def assign_block(own_key, own, number, rows, count, top, limit, slope):
    order = jax.random.permutation(own_key, count)
    packed, usual = portions_of(count, rows * top, limit, slope, True), portions_of(count, rows * top, limit, slope, False)
    places = jnp.arange(count)

    def named(sizes, offset_by):
        used = int((sizes > 0).sum())
        fixed = max(1, used // 4)
        passed = fixed + (places - fixed + offset_by * (used - fixed)) % max(1, count - fixed)
        return jnp.zeros((count,), jnp.int32).at[order[jnp.where(places < fixed, places, passed)]].set(jnp.asarray(sizes, jnp.int32))

    sizes = jnp.where(number % 4 == 0, named(packed, number // 4), named(usual, number - number // 4 - 1))
    mixed = jax.random.permutation(jax.random.fold_in(own, 3), count)
    source_of, taker = mixed[0:count // 2 * 2:2], mixed[1:count // 2 * 2:2]
    slack = jnp.minimum(sizes[source_of] - 1, limit - sizes[taker]) // 2
    slack = jnp.where((source_of == order[0]) | (taker == order[0]) | (sizes[taker] == 0), 0, jnp.maximum(slack, 0))
    passed = jax.random.randint(jax.random.fold_in(own, 4), (count // 2,), 0, 1 << 20) % (slack + 1)
    sizes = sizes.at[source_of].add(-passed).at[taker].add(passed)
    members = jnp.searchsorted(jnp.cumsum(sizes), jnp.arange(rows * top), side="right").astype(jnp.int32)
    grid = members.reshape(top, rows).T
    grid = grid[jax.random.permutation(jax.random.fold_in(own, 1), rows)]
    offset_by = jax.random.randint(jax.random.fold_in(own, 2), (rows, 1), 0, top)
    return jnp.take_along_axis(grid, (jnp.arange(top)[None, :] + offset_by) % top, axis=1)


def portions_of(number_of, total, reach, slope, full):
    loads = [(1 << 20) // math.isqrt(grade ** slope) + 1 for grade in range(1, number_of + 1)]
    largest = reach if full else min(reach, max(-(-total // number_of), total * loads[0] // sum(loads)))
    least = 1 if total - largest >= number_of - 1 else 0
    counts, spare = [largest] + [least] * (number_of - 1), total - largest - least * (number_of - 1)
    while spare > 0:
        free = [i for i in range(1, number_of) if counts[i] < largest] or [i for i in range(1, number_of) if counts[i] < reach]
        pool, remaining = sum([loads[i] for i in free]), spare
        for i in free:
            extra = min(reach - counts[i], max(1, remaining * loads[i] // pool), spare)
            counts[i] = counts[i] + extra
            spare = spare - extra
    return np.array(counts)


def centred(key, dims, scale, most, cuts=(), kind=jnp.bfloat16):
    entries = jax.random.normal(key, dims, jnp.float32) * scale
    if len(cuts) > 0:
        entries = level_of(key, dims, cuts, -0.22, 0.18) * entries
    return jnp.clip(entries, min=-most, max=most).astype(kind)


def gaussian_with(key, extent, spread, bound, pieces, heavy, kind=jnp.bfloat16):
    array = spread * jax.random.normal(key, extent, jnp.float32)
    if pieces:
        array = array * level_of(key, extent, pieces, -0.22, 0.18)
    return jnp.clip(raised(array, jax.random.fold_in(key, 3), *heavy), -bound, bound).astype(kind)


def setup_inputs(seed: int = 0) -> dict:
    arg_keys = jax.random.split(jax.random.key(seed), 17)
    residual = draw_residual(jax.random.fold_in(arg_keys[16], 71), 0)
    ssm_input = draw_ssm_input(jax.random.fold_in(arg_keys[16], 71), 0)
    ssm_gate = centred(arg_keys[2], (WINDOW_TOKENS, INNER), 1.0, 5.0, ((0, 4), (1, 8)))
    write_vectors = centred(arg_keys[3], (WINDOW_TOKENS, STATE), 0.3, 1.75, ((0, 4),))
    read_vectors = centred(arg_keys[4], (WINDOW_TOKENS, STATE), 0.3, 1.75, ((0, 4),))
    step_logits = draw_step_logits(jax.random.fold_in(arg_keys[16], 71), 0)
    decay_log = draw_decay_log(jax.random.fold_in(arg_keys[16], 71), 0)
    skip_gain = jnp.clip(0.5 + 2.5 * jax.random.uniform(arg_keys[7], (SSM_HEADS,), jnp.float32) ** level_of(arg_keys[7], (SSM_HEADS,), ((0, 8),), -0.2, 0.2), 0.5, 3.0)
    norm_gain = jnp.clip(1.0 + 0.18 * jax.random.normal(arg_keys[8], (INNER,), jnp.float32), 0.1, 1.9)
    out_weight = gaussian_with(arg_keys[9], (INNER, D), INNER ** -0.5, 0.09375, ((0, 8), (1, 4)), (0, 1, 8, 2.0))
    moe_gain = jnp.clip(1.0 + 0.18 * jax.random.normal(arg_keys[10], (D,), jnp.float32), 0.1, 1.9)
    gate_weight = centred(arg_keys[11], (PIECES, D, FF_PART), D ** -0.5, 0.09375, ((0, 8), (2, 4)))
    up_weight = centred(arg_keys[12], (PIECES, D, FF_PART), D ** -0.5, 0.09375, ((0, 8), (2, 4)))
    down_weight = centred(arg_keys[13], (PIECES, FF_PART, D), FF ** -0.5, 0.0546875, ((0, 8), (1, 4)))
    expert_ids_keys = jax.random.split(jax.random.fold_in(arg_keys[14], 1), WINDOW_TOKENS // TOK_CTX)
    expert_ids_turns = jax.random.permutation(jax.random.fold_in(arg_keys[14], 3), WINDOW_TOKENS // TOK_CTX)
    expert_ids = jax.vmap(lambda own, number: assign_block(jax.random.fold_in(arg_keys[14], 2), own, number, TOK_CTX, EXPERTS, TOP, CAP, 2))(expert_ids_keys, expert_ids_turns).reshape((WINDOW_TOKENS, TOP))
    route_weight = jnp.clip(0.5 + 1.0 * jax.random.uniform(arg_keys[15], (WINDOW_TOKENS, TOP), jnp.float32) ** level_of(arg_keys[15], (WINDOW_TOKENS, TOP), ((0, 4),), -0.2, 0.2), 0.5, 1.5)
    return {"residual": residual, "ssm_input": ssm_input, "ssm_gate": ssm_gate, "write_vectors": write_vectors, "read_vectors": read_vectors, "step_logits": step_logits, "decay_log": decay_log, "skip_gain": skip_gain, "norm_gain": norm_gain, "out_weight": out_weight, "moe_gain": moe_gain, "gate_weight": gate_weight, "up_weight": up_weight, "down_weight": down_weight, "expert_ids": expert_ids, "route_weight": route_weight}


EPSILON = 1e-05

def slot_tables(block_ids):
    expert_range = jnp.arange(EXPERTS, dtype=jnp.int32)
    hit_table = lax.optimization_barrier(jnp.sum((block_ids[:, :, None] == expert_range[None, None, :]).astype(jnp.int32), axis=1))
    ranking = jnp.cumsum(hit_table, axis=0).astype(jnp.int32) - 1
    slot_range = jnp.arange(CAP, dtype=jnp.int32)
    matches = (hit_table.T[:, None, :] == 1) & (ranking.T[:, None, :] == slot_range[None, :, None])
    row_count = block_ids.shape[0]
    row_range = jnp.arange(row_count, dtype=jnp.int32)
    chosen = lax.optimization_barrier(jnp.sum(jnp.where(matches, row_range[None, None, :], 0), axis=2)).astype(jnp.int32)
    filled = jnp.any(matches, axis=2)
    token_of_slot = jnp.where(filled, chosen, row_count).astype(jnp.int32)
    pick_rank = jnp.take_along_axis(ranking, block_ids, axis=1).astype(jnp.int32)
    return (token_of_slot, pick_rank)

def head_scan(cumulative, step_blocks, input_blocks, scores, write_blocks, read_wide, skip_value):
    causal = jnp.arange(SPAN)[:, None] >= jnp.arange(SPAN)[None, :]
    log_gaps = cumulative[:, :, None] - cumulative[:, None, :]
    mixing = jnp.where(causal[None], scores * jnp.exp(jnp.where(causal[None], log_gaps, 0.0)) * step_blocks[:, None, :], 0.0).astype(jnp.bfloat16)
    input_wide = input_blocks.astype(jnp.float32)
    intra_out = jnp.einsum('kts,ksp->ktp', mixing.astype(jnp.float32), input_wide, precision=lax.Precision.HIGHEST)
    end_weight = jnp.exp(cumulative[:, -1:] - cumulative) * step_blocks
    loaded = (end_weight[:, :, None] * write_blocks.astype(jnp.float32)).astype(jnp.bfloat16)
    block_state = jnp.einsum('ksp,ksn->kpn', input_wide, loaded.astype(jnp.float32), precision=lax.Precision.HIGHEST)
    block_decay = jnp.exp(cumulative[:, -1])

    def advance(carried, inputs):
        decay_now, state_now = inputs
        return (decay_now * carried + state_now, carried)
    zero_state = jnp.zeros(block_state.shape[1:], jnp.float32)
    entering = lax.scan(advance, zero_state, (block_decay, block_state))[1]
    inter_out = jnp.exp(cumulative)[:, :, None] * jnp.einsum('ktn,kpn->ktp', read_wide, entering, precision=lax.Precision.HIGHEST)
    return intra_out + inter_out + skip_value * input_wide

def reference(residual, ssm_input, ssm_gate, write_vectors, read_vectors, step_logits, decay_log, skip_gain, norm_gain, out_weight, moe_gain, gate_weight, up_weight, down_weight, expert_ids, route_weight):
    span_count = WINDOW_TOKENS // SPAN
    step_size = jax.nn.softplus(step_logits)
    log_step = step_size * (-jnp.exp(decay_log))[:, None]
    cumulative = jnp.cumsum(log_step.reshape(SSM_HEADS, span_count, SPAN), axis=2)
    step_blocks = step_size.reshape(SSM_HEADS, span_count, SPAN)
    input_heads = jnp.transpose(ssm_input.reshape(span_count, SPAN, SSM_HEADS, HEAD_DIM), (2, 0, 1, 3))
    write_blocks = write_vectors.reshape(span_count, SPAN, STATE)
    read_wide = read_vectors.reshape(span_count, SPAN, STATE).astype(jnp.float32)
    scores = jnp.einsum('ktn,ksn->kts', read_wide, write_blocks.astype(jnp.float32), precision=lax.Precision.HIGHEST)

    def per_head(items):
        return head_scan(items[0], items[1], items[2], scores, write_blocks, read_wide, items[3])
    head_outs = lax.map(per_head, (cumulative, step_blocks, input_heads, skip_gain))
    scan_out = jnp.transpose(head_outs, (1, 2, 0, 3)).reshape(WINDOW_TOKENS, INNER)
    gated_out = scan_out * jax.nn.silu(ssm_gate.astype(jnp.float32))
    grouped = gated_out.reshape(WINDOW_TOKENS, INNER // NORM_GROUP, NORM_GROUP)
    scale_inv = lax.rsqrt(lax.optimization_barrier(jnp.mean(grouped * grouped, axis=2, keepdims=True)) + EPSILON)
    normed = ((grouped * scale_inv).reshape(WINDOW_TOKENS, INNER) * norm_gain).astype(jnp.bfloat16)
    ssm_out = jnp.dot(normed, out_weight, preferred_element_type=jnp.float32)
    stream = (residual.astype(jnp.float32) + ssm_out).astype(jnp.bfloat16)
    stream_wide = stream.astype(jnp.float32)
    moe_scale = lax.rsqrt(lax.optimization_barrier(jnp.mean(stream_wide * stream_wide, axis=1, keepdims=True)) + EPSILON)
    moe_in = (stream_wide * moe_scale * moe_gain).astype(jnp.bfloat16)
    split_count = N_EXP // EXPERTS
    piece_width = FF_PART // N_CTX
    token_of_slot, pick_rank = jax.vmap(slot_tables)(expert_ids.reshape(N_CTX, TOK_CTX, TOP))
    padded = jnp.concatenate([moe_in.reshape(N_CTX, TOK_CTX, D), jnp.zeros((N_CTX, 1, D), jnp.bfloat16)], axis=1)
    gathered = jax.vmap(lambda table_rows, slot_index: jnp.take(table_rows, slot_index, axis=0))(padded, token_of_slot)
    expert_rows = jnp.transpose(gathered, (1, 0, 2, 3)).reshape(EXPERTS, N_CTX * CAP, D)

    def piece_out(piece_index):
        piece_rows = lax.dynamic_index_in_dim(expert_rows, piece_index // split_count, 0, keepdims=False).astype(jnp.float32)
        gate_piece = lax.dynamic_index_in_dim(gate_weight, piece_index, 0, keepdims=False)
        up_piece = lax.dynamic_index_in_dim(up_weight, piece_index, 0, keepdims=False)
        down_piece = lax.dynamic_index_in_dim(down_weight, piece_index, 0, keepdims=False)

        def add_block(total, ctx_index):
            first_col = (ctx_index * piece_width).astype(jnp.int32)
            gate_cols = lax.dynamic_slice_in_dim(gate_piece, first_col, piece_width, 1).astype(jnp.float32)
            up_cols = lax.dynamic_slice_in_dim(up_piece, first_col, piece_width, 1).astype(jnp.float32)
            down_rows = lax.dynamic_slice_in_dim(down_piece, first_col, piece_width, 0).astype(jnp.float32)
            gate_val = jnp.dot(piece_rows, gate_cols, precision=lax.Precision.HIGHEST, preferred_element_type=jnp.float32)
            up_val = jnp.dot(piece_rows, up_cols, precision=lax.Precision.HIGHEST, preferred_element_type=jnp.float32)
            hidden = (jax.nn.silu(gate_val) * up_val).astype(jnp.bfloat16)
            piece_term = jnp.dot(hidden.astype(jnp.float32), down_rows, precision=lax.Precision.HIGHEST, preferred_element_type=jnp.float32)
            piece_term = lax.optimization_barrier(piece_term.astype(jnp.bfloat16)).astype(jnp.float32)
            return (total + piece_term, None)
        return lax.scan(add_block, jnp.zeros((N_CTX * CAP, D), jnp.float32), jnp.arange(N_CTX, dtype=jnp.int32))[0]
    pieces_out = lax.map(piece_out, jnp.arange(N_EXP, dtype=jnp.int32))
    block_of = jnp.arange(WINDOW_TOKENS, dtype=jnp.int32) // TOK_CTX
    row_index = (block_of[:, None] * CAP + pick_rank.reshape(WINDOW_TOKENS, TOP)).astype(jnp.int32)
    piece_index = (expert_ids[:, :, None] * split_count + jnp.arange(split_count, dtype=jnp.int32)[None, None, :]).astype(jnp.int32)
    picked = pieces_out[piece_index, row_index[:, :, None]]
    moe_out = lax.optimization_barrier(jnp.sum(route_weight[:, :, None] * lax.optimization_barrier(jnp.sum(picked, axis=2)), axis=1))
    return (stream_wide + moe_out).astype(jnp.bfloat16)
```

```python
import functools
import math

import jax
import jax.numpy as jnp
from jax import lax
from jax.experimental import pallas as pl
from jax.experimental.pallas import tpu as pltpu
from jax.sharding import PartitionSpec as P

SPAN = 128
NORM_GROUP = 512
EXPERTS = 8
CAP = 64


EPSILON = 1e-05


MESH = pl.DeviceIdType.MESH


def send_kernel(axis, count, pair, spread, n_arrays, *refs):
    sources, targets = refs[:n_arrays], refs[n_arrays : 2 * n_arrays]
    local_sem, send_sem, recv_sem = refs[2 * n_arrays :]
    index = lax.axis_index(axis)
    group, lane = index // pair, lax.rem(index, pair)
    barrier = pltpu.get_barrier_semaphore()
    peers = [lax.rem(group + d, count) for d in range(1, count)]
    for peer in peers:
        pl.semaphore_signal(
            barrier, inc=1, device_id={axis: peer * pair + lane}, device_id_type=MESH
        )
    pl.semaphore_wait(barrier, count - 1)
    copies = []
    for d, peer in enumerate(peers):
        for i in range(n_arrays):
            copy = pltpu.make_async_remote_copy(
                src_ref=sources[i] if spread else sources[i].at[peer],
                dst_ref=targets[i].at[group],
                send_sem=send_sem.at[d, i],
                recv_sem=recv_sem.at[d, i],
                device_id={axis: peer * pair + lane},
                device_id_type=MESH,
            )
            copy.start()
            copies.append(copy)
    for i in range(n_arrays):
        own = pltpu.make_async_copy(
            sources[i] if spread else sources[i].at[group],
            targets[i].at[group],
            local_sem.at[i],
        )
        own.start()
        copies.append(own)
    for copy in copies:
        copy.wait()


def sent(arrays, axis, number, spread, pair=1):
    count = lax.axis_size(axis) // pair
    n_arrays = len(arrays)
    shapes = [
        jax.ShapeDtypeStruct((count,) + a.shape if spread else a.shape, a.dtype) for a in arrays
    ]
    size = sum(math.prod(shape.shape) * shape.dtype.itemsize for shape in shapes)
    return pl.pallas_call(
        functools.partial(send_kernel, axis, count, pair, spread, n_arrays),
        out_shape=shapes,
        in_specs=[pl.BlockSpec(memory_space=pl.ANY)] * n_arrays,
        out_specs=[pl.BlockSpec(memory_space=pl.ANY)] * n_arrays,
        scratch_shapes=[
            pltpu.SemaphoreType.DMA((n_arrays,)),
            pltpu.SemaphoreType.DMA((count - 1, n_arrays)),
            pltpu.SemaphoreType.DMA((count - 1, n_arrays)),
        ],
        compiler_params=pltpu.CompilerParams(collective_id=number, has_side_effects=True),
        cost_estimate=pl.CostEstimate(flops=0, bytes_accessed=2 * size, transcendentals=0),
    )(*arrays)


def gather_pairs_kernel(axis, groups, x_ref, out_ref, local_sem, send_sem, recv_sem, pass_send, pass_recv):
    index = lax.axis_index(axis)
    group, lane = index // 2, lax.rem(index, 2)
    sibling = group * 2 + 1 - lane
    barrier = pltpu.get_barrier_semaphore()
    peers = [lax.rem(group + d, groups) for d in range(1, groups)]
    for peer in [p * 2 + lane for p in peers] + [sibling]:
        pl.semaphore_signal(barrier, inc=1, device_id={axis: peer}, device_id_type=MESH)
    pl.semaphore_wait(barrier, groups)
    copies = []
    for d, peer in enumerate(peers):
        copy = pltpu.make_async_remote_copy(
            src_ref=x_ref,
            dst_ref=out_ref.at[index],
            send_sem=send_sem.at[d],
            recv_sem=recv_sem.at[d],
            device_id={axis: peer * 2 + lane},
            device_id_type=MESH,
        )
        copy.start()
        copies.append(copy)
    own = pltpu.make_async_copy(x_ref, out_ref.at[index], local_sem)
    own.start()
    passed = [
        pltpu.make_async_remote_copy(
            src_ref=x_ref,
            dst_ref=out_ref.at[index],
            send_sem=pass_send.at[0],
            recv_sem=pass_recv.at[0],
            device_id={axis: sibling},
            device_id_type=MESH,
        )
    ]
    passed[0].start()
    for d in range(1, groups):
        copies[d - 1].wait_recv()
        block = lax.rem(group + groups - d, groups) * 2 + lane
        copy = pltpu.make_async_remote_copy(
            src_ref=out_ref.at[block],
            dst_ref=out_ref.at[block],
            send_sem=pass_send.at[d],
            recv_sem=pass_recv.at[d],
            device_id={axis: sibling},
            device_id_type=MESH,
        )
        copy.start()
        passed.append(copy)
    for copy in copies:
        copy.wait_send()
    own.wait()
    for copy in passed:
        copy.wait()


def gather_pairs(x, axis, number):
    count = lax.axis_size(axis)
    return pl.pallas_call(
        functools.partial(gather_pairs_kernel, axis, count // 2),
        out_shape=jax.ShapeDtypeStruct((count,) + x.shape, x.dtype),
        in_specs=[pl.BlockSpec(memory_space=pl.ANY)],
        out_specs=pl.BlockSpec(memory_space=pl.ANY),
        scratch_shapes=[
            pltpu.SemaphoreType.DMA,
            pltpu.SemaphoreType.DMA((count // 2 - 1,)),
            pltpu.SemaphoreType.DMA((count // 2 - 1,)),
            pltpu.SemaphoreType.DMA((count // 2,)),
            pltpu.SemaphoreType.DMA((count // 2,)),
        ],
        compiler_params=pltpu.CompilerParams(collective_id=number, has_side_effects=True),
        cost_estimate=pl.CostEstimate(
            flops=0, bytes_accessed=2 * count * x.size * x.dtype.itemsize, transcendentals=0
        ),
    )(x)


def pair_sum(halves, number):
    lane = lax.rem(lax.axis_index("exp"), 2)
    both = pair_send(halves, number)
    own = lax.dynamic_index_in_dim(halves, lane, 0, keepdims=False)
    return (own.astype(jnp.float32) + both.astype(jnp.float32)).astype(jnp.bfloat16)


def pair_kernel(x_ref, out_ref, send_sem, recv_sem):
    index = lax.axis_index("exp")
    lane = lax.rem(index, 2)
    sibling = index + 1 - 2 * lane
    barrier = pltpu.get_barrier_semaphore()
    pl.semaphore_signal(barrier, inc=1, device_id={"exp": sibling}, device_id_type=MESH)
    pl.semaphore_wait(barrier, 1)
    copy = pltpu.make_async_remote_copy(
        src_ref=x_ref.at[1 - lane],
        dst_ref=out_ref,
        send_sem=send_sem,
        recv_sem=recv_sem,
        device_id={"exp": sibling},
        device_id_type=MESH,
    )
    copy.start()
    copy.wait()


def pair_send(halves, number):
    return pl.pallas_call(
        pair_kernel,
        out_shape=jax.ShapeDtypeStruct(halves.shape[1:], halves.dtype),
        in_specs=[pl.BlockSpec(memory_space=pl.ANY)],
        out_specs=pl.BlockSpec(memory_space=pl.ANY),
        scratch_shapes=[pltpu.SemaphoreType.DMA, pltpu.SemaphoreType.DMA],
        compiler_params=pltpu.CompilerParams(collective_id=number, has_side_effects=True),
        cost_estimate=pl.CostEstimate(
            flops=0, bytes_accessed=halves.size * 2, transcendentals=0
        ),
    )(halves)


def expert_kernel(x_ref, gate_ref, up_ref, down_ref, out_ref, total):
    step = pl.program_id(1)
    gate_val = jnp.dot(x_ref[...], gate_ref[...], preferred_element_type=jnp.float32)
    up_val = jnp.dot(x_ref[...], up_ref[...], preferred_element_type=jnp.float32)
    hidden = (gate_val / (1.0 + jnp.exp(-gate_val)) * up_val).astype(jnp.bfloat16)
    columns = down_ref.shape[1] // 4

    def add(first):
        for c in range(4):
            part = slice(c * columns, (c + 1) * columns)
            term = jnp.dot(hidden, down_ref[:, part], preferred_element_type=jnp.float32)
            total[:, part] = term if first else total[:, part] + term

    pl.when(step == 0)(lambda: add(True))
    pl.when(step > 0)(lambda: add(False))

    @pl.when(step == pl.num_programs(1) - 1)
    def _():
        out_ref[...] = total[...].astype(out_ref.dtype)


def expert_terms(rows, gate, up, down):
    count, width = rows.shape
    units = gate.shape[1]
    block = 256 if units % 256 == 0 else 128
    tall = 256 if count % 256 == 0 else count
    return pl.pallas_call(
        expert_kernel,
        out_shape=jax.ShapeDtypeStruct((count, width), jnp.bfloat16),
        grid=(count // tall, units // block),
        in_specs=[
            pl.BlockSpec((tall, width), lambda r, i: (r, 0)),
            pl.BlockSpec((width, block), lambda r, i: (0, i)),
            pl.BlockSpec((width, block), lambda r, i: (0, i)),
            pl.BlockSpec((block, width), lambda r, i: (i, 0)),
        ],
        out_specs=pl.BlockSpec((tall, width), lambda r, i: (r, 0)),
        scratch_shapes=[pltpu.VMEM((tall, width), jnp.float32)],
        compiler_params=pltpu.CompilerParams(vmem_limit_bytes=48 * 1024 * 1024),
        cost_estimate=pl.CostEstimate(
            flops=6 * count * width * units,
            bytes_accessed=6 * width * units,
            transcendentals=count * units,
        ),
    )(rows, gate, up, down)


def slot_tables(block_ids):
    expert_range = jnp.arange(EXPERTS, dtype=jnp.int32)
    hit_table = jnp.sum(
        (block_ids[:, :, None] == expert_range[None, None, :]).astype(jnp.int32), axis=1
    )
    lower = jnp.tril(jnp.ones((block_ids.shape[0],) * 2, jnp.bfloat16))
    ranking = (
        jnp.dot(lower, hit_table.astype(jnp.bfloat16), preferred_element_type=jnp.float32)
    ).astype(jnp.int32) - 1
    slot_range = jnp.arange(CAP, dtype=jnp.int32)
    matches = (hit_table.T[:, None, :] == 1) & (ranking.T[:, None, :] == slot_range[None, :, None])
    row_count = block_ids.shape[0]
    row_range = jnp.arange(row_count, dtype=jnp.int32)
    chosen = jnp.sum(jnp.where(matches, row_range[None, None, :], 0), axis=2)
    filled = jnp.any(matches, axis=2)
    token_of_slot = jnp.where(filled, chosen, row_count)
    pick_rank = jnp.take_along_axis(ranking, block_ids, axis=1)
    return (token_of_slot, pick_rank)


def normalize(stream_rows, moe_gain):
    values = stream_rows.astype(jnp.float32)
    scale_inv = lax.rsqrt(jnp.mean(values * values, axis=-1, keepdims=True) + EPSILON)
    return (values * scale_inv * moe_gain).astype(jnp.bfloat16)


def handshake(peers):
    barrier = pltpu.get_barrier_semaphore()
    for peer in peers:
        pl.semaphore_signal(barrier, inc=1, device_id=peer, device_id_type=MESH)
    pl.semaphore_wait(barrier, len(peers))


def remote(src, dst, send_sem, recv_sem, device):
    return pltpu.make_async_remote_copy(
        src_ref=src,
        dst_ref=dst,
        send_sem=send_sem,
        recv_sem=recv_sem,
        device_id=device,
        device_id_type=MESH,
    )


def xor(a, s):
    low = lax.rem(a, 2)
    low = 1 - low if s % 2 else low
    high = a // 2
    high = 1 - high if s // 2 else high
    return high * 2 + low


def ssm_kernel(
    x_ref,
    z_ref,
    write_ref,
    read_ref,
    logit_ref,
    decay_ref,
    skip_ref,
    gain_ref,
    residual_ref,
    weight_hbm,
    part_ref,
    weight,
    states,
    decays,
    entered,
    scan,
    normed,
    terms,
    paired,
    sums,
    arrived,
    rest,
    local_sem,
    state_send,
    state_recv,
    norm_send,
    norm_recv,
    pair_send_sem,
    pair_recv_sem,
    sum_send,
    sum_recv,
    rest_send,
    rest_recv,
):
    f32, bf16 = jnp.float32, jnp.bfloat16
    n_ctx, n_exp = 4, 8
    groups = n_exp // 2
    ctx, e = lax.axis_index("ctx"), lax.axis_index("exp")
    group, lane = e // 2, lax.rem(e, 2)
    sibling = group * 2 + 1 - lane
    tokens, channels = x_ref.shape
    heads = logit_ref.shape[0]
    wide = 2 * (channels // heads)
    own_rows = tokens // n_exp
    cols = weight.shape[1]
    others = [xor(ctx, s) for s in range(n_ctx)]
    chips = [lax.rem(group + d, groups) for d in range(groups)]

    load = pltpu.make_async_copy(weight_hbm, weight, local_sem)
    load.start()

    step = jnp.maximum(logit_ref[...], 0.0) + jnp.log1p(jnp.exp(-jnp.abs(logit_ref[...])))
    diagonal = lax.broadcasted_iota(jnp.int32, (heads, heads), 0) == lax.broadcasted_iota(
        jnp.int32, (heads, heads), 1
    )

    def column(row):
        return jnp.sum(
            jnp.where(diagonal, jnp.broadcast_to(row, (heads, heads)), 0.0), axis=1, keepdims=True
        )

    head_of = lax.broadcasted_iota(jnp.int32, (heads, channels), 1) // (channels // heads)
    own_head = head_of == lax.broadcasted_iota(jnp.int32, (heads, channels), 0)

    def spread_row(col):
        return jnp.sum(
            jnp.where(own_head, jnp.broadcast_to(col, (heads, channels)), 0.0),
            axis=0,
            keepdims=True,
        )

    log_step = step * (-jnp.exp(column(decay_ref[...])))
    row_i = lax.broadcasted_iota(jnp.int32, (tokens, tokens), 0)
    col_i = lax.broadcasted_iota(jnp.int32, (tokens, tokens), 1)
    upper = (row_i <= col_i).astype(f32)
    cumulative = jnp.dot(
        log_step, upper, precision=lax.Precision.HIGHEST, preferred_element_type=f32
    )
    last = cumulative[:, tokens - 1 : tokens]
    end_weight = jnp.exp(last - cumulative) * step
    stacked = jnp.concatenate(
        [
            cumulative,
            jnp.exp(cumulative),
            end_weight,
            jnp.zeros((tokens - 3 * heads, tokens), f32),
        ],
        axis=0,
    ).T
    first_half = lax.broadcasted_iota(jnp.int32, (tokens, wide), 1) < wide // 2

    def pair_columns(first, q):
        return jnp.where(
            first_half,
            stacked[:, first + 2 * q : first + 2 * q + 1],
            stacked[:, first + 2 * q + 1 : first + 2 * q + 2],
        )

    write_t = write_ref[...].astype(f32).T.astype(bf16)
    for q in range(heads // 2):
        part = slice(q * wide, (q + 1) * wide)
        weighted = (pair_columns(2 * heads, q) * x_ref[:, part].astype(f32)).astype(bf16)
        states[ctx, :, part] = jnp.dot(
            write_t, weighted, preferred_element_type=f32
        ).astype(bf16)
    decays[ctx] = jnp.broadcast_to(jnp.exp(last), (heads, tokens))

    handshake(
        [{"ctx": others[s], "exp": e} for s in range(1, n_ctx)]
        + [{"ctx": ctx, "exp": chips[d] * 2 + lane} for d in range(1, groups)]
        + [{"ctx": ctx, "exp": sibling}]
    )

    def state_copies(d, device_ctx, slot):
        return [
            remote(
                buf.at[slot],
                buf.at[slot],
                state_send.at[d - 1, i],
                state_recv.at[d - 1, i],
                {"ctx": device_ctx, "exp": e},
            )
            for i, buf in enumerate((states, decays))
        ]

    for d in range(1, n_ctx):

        @pl.when(ctx + d < n_ctx)
        def _(d=d):
            for copy in state_copies(d, ctx + d, ctx):
                copy.start()

    rest_copies = [
        remote(
            residual_ref.at[pl.ds(e * own_rows, own_rows), pl.ds(others[s] * cols, cols)],
            rest.at[s],
            rest_send.at[s - 1],
            rest_recv.at[s - 1],
            {"ctx": others[s], "exp": e},
        )
        for s in range(1, n_ctx)
    ]
    for copy in rest_copies:
        copy.start()
    rest[0] = residual_ref[pl.ds(pl.multiple_of(e * own_rows, 16), own_rows), pl.ds(pl.multiple_of(ctx * cols, 128), cols)]

    causal = row_i >= col_i
    scores = lax.dot_general(
        read_ref[...], write_ref[...], (((1,), (1,)), ((), ())), preferred_element_type=f32
    )
    for q in range(heads // 2):
        part = slice(q * wide, (q + 1) * wide)
        x_pair = x_ref[:, part]
        outs = []
        for h in (2 * q, 2 * q + 1):
            gap = stacked[:, h : h + 1] - cumulative[h : h + 1, :]
            decayed = jnp.exp(jnp.where(causal, gap, 0.0)) * step[h : h + 1, :]
            mixing = jnp.where(causal, scores * decayed, 0.0).astype(bf16)
            outs.append(jnp.dot(mixing, x_pair, preferred_element_type=f32))
        scan[:, part] = jnp.where(first_half, outs[0], outs[1])

    entered[...] = jnp.zeros_like(entered)
    for d in range(n_ctx - 1, 0, -1):

        @pl.when(ctx >= d)
        def _(d=d):
            source = ctx - d
            for copy in state_copies(d, ctx, source):
                copy.wait_recv()
            entered[...] = spread_row(decays[source][:, :1]) * entered[...] + states[
                source
            ].astype(f32)

    high = entered[...].astype(bf16)
    low = (entered[...] - high.astype(f32)).astype(bf16)
    reads = read_ref[...]
    skip = spread_row(column(skip_ref[...]))
    for q in range(heads // 2):
        part = slice(q * wide, (q + 1) * wide)
        inter = jnp.dot(reads, high[:, part], preferred_element_type=f32) + jnp.dot(
            reads, low[:, part], preferred_element_type=f32
        )
        value = (
            scan[:, part]
            + pair_columns(heads, q) * inter
            + skip[:, part] * x_ref[:, part].astype(f32)
        )
        gate = z_ref[:, part].astype(f32)
        scan[:, part] = value * (gate / (1.0 + jnp.exp(-gate)))
    for n in range(channels // NORM_GROUP):
        part = slice(n * NORM_GROUP, (n + 1) * NORM_GROUP)
        value = scan[:, part]
        scale = lax.rsqrt(jnp.mean(value * value, axis=1, keepdims=True) + EPSILON)
        normed[ctx, :, part] = (value * scale * gain_ref[:, part]).astype(bf16)

    half = tokens // 2

    def norm_copy(s, source, rows, number):
        where = normed.at[source] if rows is None else normed.at[source, pl.ds(rows, half)]
        return remote(
            where, where, norm_send.at[number], norm_recv.at[number], {"ctx": others[s], "exp": e}
        )

    norm_copies = [norm_copy(1, ctx, None, 0), norm_copy(2, ctx, None, 1)]
    for copy in norm_copies:
        copy.start()
    load.wait()

    def project(s):
        value = jnp.dot(
            normed[others[s]], weight[...], preferred_element_type=f32
        ).astype(bf16)
        for owner in range(n_exp):
            terms[s, owner % 2, owner // 2] = value[owner * own_rows : (owner + 1) * own_rows]

    def pair_copy(s):
        return remote(
            terms.at[s, 1 - lane],
            paired.at[s],
            pair_send_sem.at[s],
            pair_recv_sem.at[s],
            {"ctx": ctx, "exp": sibling},
        )

    def sum_copy(s, d):
        return remote(
            sums.at[s, chips[d]],
            arrived.at[s, d - 1],
            sum_send.at[s, d - 1],
            sum_recv.at[s, d - 1],
            {"ctx": ctx, "exp": chips[d] * 2 + lane},
        )

    def add_pair(s):
        pair_copy(s).wait_recv()
        sums[s] = (terms[s, lane].astype(f32) + paired[s].astype(f32)).astype(bf16)
        for d in range(1, groups):
            sum_copy(s, d).start()

    project(0)
    pair_copy(0).start()
    norm_copies[0].wait_recv()
    norm_copies.append(norm_copy(2, others[1], 0, 2))
    norm_copies[2].start()
    norm_copies[1].wait_recv()
    norm_copies.append(norm_copy(1, others[2], half, 3))
    norm_copies[3].start()
    add_pair(0)
    project(1)
    pair_copy(1).start()
    project(2)
    pair_copy(2).start()
    add_pair(1)
    add_pair(2)
    norm_copies[2].wait_recv()
    norm_copies[3].wait_recv()
    project(3)
    pair_copy(3).start()
    add_pair(3)
    for copy in rest_copies:
        copy.wait()
    for s in range(n_ctx):
        total = sums[s, group].astype(f32)
        for d in range(1, groups):
            sum_copy(s, d).wait_recv()
            total = total + arrived[s, d - 1].astype(f32)
        total = total.astype(bf16).astype(f32) + rest[s].astype(f32)
        part_ref[pl.ds(pl.multiple_of(others[s] * own_rows, 16), own_rows), :] = total.astype(bf16)

    for copy in norm_copies:
        copy.wait_send()
    for s in range(n_ctx):
        pair_copy(s).wait_send()
        for d in range(1, groups):
            sum_copy(s, d).wait_send()
    for d in range(1, n_ctx):

        @pl.when(ctx + d < n_ctx)
        def _(d=d):
            for copy in state_copies(d, ctx + d, ctx):
                copy.wait_send()


def ssm_stage(
    x, z, write, read, logits, decay_log, skip_gain, norm_gain, residual, out_weight, number
):
    n_ctx, n_exp = lax.axis_size("ctx"), lax.axis_size("exp")
    tokens, channels = x.shape
    heads = logits.shape[0]
    cols = out_weight.shape[1]
    own_rows = tokens // n_exp
    groups = n_exp // 2
    bf16, dma = jnp.bfloat16, pltpu.SemaphoreType.DMA
    vmem = pl.BlockSpec(memory_space=pltpu.VMEM)
    return pl.pallas_call(
        ssm_kernel,
        out_shape=jax.ShapeDtypeStruct((n_ctx * own_rows, cols), bf16),
        in_specs=[vmem] * 9 + [pl.BlockSpec(memory_space=pl.ANY)],
        out_specs=vmem,
        scratch_shapes=[
            pltpu.VMEM(out_weight.shape, bf16),
            pltpu.VMEM((n_ctx, write.shape[1], channels), bf16),
            pltpu.VMEM((n_ctx, heads, tokens), jnp.float32),
            pltpu.VMEM((write.shape[1], channels), jnp.float32),
            pltpu.VMEM((tokens, channels), jnp.float32),
            pltpu.VMEM((n_ctx, tokens, channels), bf16),
            pltpu.VMEM((n_ctx, 2, groups, own_rows, cols), bf16),
            pltpu.VMEM((n_ctx, groups, own_rows, cols), bf16),
            pltpu.VMEM((n_ctx, groups, own_rows, cols), bf16),
            pltpu.VMEM((n_ctx, groups - 1, own_rows, cols), bf16),
            pltpu.VMEM((n_ctx, own_rows, cols), bf16),
            dma,
            dma((n_ctx - 1, 2)),
            dma((n_ctx - 1, 2)),
            dma((4,)),
            dma((4,)),
            dma((n_ctx,)),
            dma((n_ctx,)),
            dma((n_ctx, groups - 1)),
            dma((n_ctx, groups - 1)),
            dma((n_ctx - 1,)),
            dma((n_ctx - 1,)),
        ],
        compiler_params=pltpu.CompilerParams(
            collective_id=number, has_side_effects=True, vmem_limit_bytes=40 * 1024 * 1024
        ),
        cost_estimate=pl.CostEstimate(
            flops=2 * n_ctx * tokens * channels * cols,
            bytes_accessed=2 * channels * cols,
            transcendentals=heads * tokens * tokens,
        ),
    )(
        x,
        z,
        write,
        read,
        logits,
        decay_log.reshape(1, -1),
        skip_gain.reshape(1, -1),
        norm_gain.reshape(1, -1),
        residual,
        out_weight,
    )


TILE = 1024
SLOTS = 18


def moe_kernel(
    part_ref,
    ids_ref,
    route_ref,
    gain_ref,
    gate_hbm,
    up_hbm,
    down_hbm,
    out_ref,
    stream,
    tiles,
    gate_sum,
    up_sum,
    rows,
    hidden,
    term,
    came,
    mine,
    outs,
    ids_all,
    combine,
    tile_sem,
    z_send,
    z_recv,
    xy_send,
    xy_recv,
    fwd_send,
    fwd_recv,
    pass_send,
    pass_recv,
    ids_send,
    ids_recv,
    term_send,
    term_recv,
    out_send,
    out_recv,
    sib_send,
    sib_recv,
):
    f32, bf16 = jnp.float32, jnp.bfloat16
    n_ctx, n_exp = 4, 8
    groups = n_exp // 2
    ctx, e = lax.axis_index("ctx"), lax.axis_index("exp")
    group, lane = e // 2, lax.rem(e, 2)
    sibling = group * 2 + 1 - lane
    others = [xor(ctx, s) for s in range(n_ctx)]
    chips = [lax.rem(group + d, groups) for d in range(groups)]
    back = [lax.rem(group + groups - d, groups) for d in range(groups)]
    blocks = hidden.shape[1] // TILE
    n_rows = n_ctx * CAP

    order = [
        (kind, s, n) for s in range(n_ctx) for n in range(blocks) for kind in ("gate", "up")
    ] + [("down", m, f) for m in range(groups) for f in range(blocks)]
    turn = [lax.rem(group + 1 + i, groups) for i in range(groups)]

    def tile_copy(i):
        kind, outer, inner = order[i]
        fixed = pl.ds(inner * TILE, TILE)
        if kind == "down":
            moving = pl.ds(pl.multiple_of(turn[outer] * TILE, TILE), TILE)
            src = down_hbm.at[0, fixed, moving]
        else:
            moving = pl.ds(pl.multiple_of(others[outer] * TILE, TILE), TILE)
            src = (gate_hbm if kind == "gate" else up_hbm).at[0, moving, fixed]
        return pltpu.make_async_copy(src, tiles.at[i % SLOTS], tile_sem.at[i % SLOTS])

    def use_tile(i):
        tile_copy(i).wait()
        return tiles.at[i % SLOTS]

    def done_tile(i):
        if i + SLOTS < len(order):
            tile_copy(i + SLOTS).start()

    for i in range(SLOTS):
        tile_copy(i).start()

    stream[ctx, e] = part_ref[...]
    row_i = lax.broadcasted_iota(jnp.int32, (128, 128), 0)
    col_i = lax.broadcasted_iota(jnp.int32, (128, 128), 1)

    def as_row(ref, k):
        return jnp.broadcast_to(ref[:, k : k + 1].astype(f32), (128, 128)).T

    ids_rows = [as_row(ids_ref, k) for k in range(2)]
    ids_all[ctx] = jnp.where(row_i[:8] == 0, ids_rows[0][:8], ids_rows[1][:8])

    handshake(
        [{"ctx": others[s], "exp": e} for s in range(1, n_ctx)]
        + [{"ctx": ctx, "exp": lax.rem(e + d, n_exp)} for d in range(1, n_exp)]
    )

    def block(ref, source, b):
        return ref.at[source, back[b] * 2 + lane]

    def z_copy(d, b=0):
        where = block(stream, ctx, b)
        return remote(
            where,
            where,
            z_send.at[d - 1],
            z_recv.at[d - 1],
            {"ctx": ctx, "exp": chips[d] * 2 + lane},
        )

    def xy_copy(s, b, source):
        where = block(stream, source, b)
        return remote(
            where,
            where,
            xy_send.at[s - 1, b],
            xy_recv.at[s - 1, b],
            {"ctx": others[s], "exp": e},
        )

    half = part_ref.shape[0] // 2

    def fwd_copy(s, b, source):
        where = stream.at[source, back[b] * 2 + lane, pl.ds((2 - s) * half, half)]
        return remote(
            where,
            where,
            fwd_send.at[s - 1, b],
            fwd_recv.at[s - 1, b],
            {"ctx": others[s], "exp": e},
        )

    def pass_copy(s, b, which=None):
        where = stream.at[others[s], back[b] * 2 + (lane if which is None else which)]
        return remote(
            where, where, pass_send.at[s, b], pass_recv.at[s, b], {"ctx": ctx, "exp": sibling}
        )

    def ids_copy(s, source):
        where = ids_all.at[source]
        return remote(
            where, where, ids_send.at[s - 1], ids_recv.at[s - 1], {"ctx": others[s], "exp": e}
        )

    def forward(b):
        xy_copy(1, b, others[1]).wait_recv()
        fwd_copy(2, b, others[1]).start()
        pass_copy(1, b).start()
        xy_copy(2, b, others[2]).wait_recv()
        fwd_copy(1, b, others[2]).start()
        pass_copy(2, b).start()

    def diagonal(b):
        fwd_copy(1, b, others[3]).wait_recv()
        fwd_copy(2, b, others[3]).wait_recv()
        pass_copy(3, b).start()

    for s in range(1, n_ctx):
        ids_copy(s, ctx).start()
    for d in range(1, groups):
        z_copy(d).start()
    for s in (1, 2):
        xy_copy(s, 0, ctx).start()
    pass_copy(0, 0).start()

    upper = (row_i <= col_i).astype(bf16)
    slot_i = lax.broadcasted_iota(jnp.int32, (CAP, 128), 0).astype(f32)

    def slots_of(first, second, expert):
        hit = jnp.where((first == expert) | (second == expert), 1.0, 0.0)
        rank = jnp.dot(hit.astype(bf16), upper, preferred_element_type=f32) - 1.0
        return jnp.where((hit > 0.0) & (rank == slot_i), 1.0, 0.0)

    own_ids = [r[:CAP] for r in ids_rows]
    own_route = [as_row(route_ref, k)[:CAP] for k in range(2)]
    for pair in range(n_exp // 2):
        both = []
        for x in (2 * pair, 2 * pair + 1):
            weight = jnp.where(own_ids[0] == float(x), own_route[0], own_route[1])
            both.append(slots_of(own_ids[0], own_ids[1], float(x)) * weight)
        back_table = jnp.concatenate(both, axis=0).T
        high = back_table.astype(bf16)
        part = slice(pair * 128, (pair + 1) * 128)
        combine[0, :, part] = high
        combine[1, :, part] = (back_table - high.astype(f32)).astype(bf16)

    for s in range(1, n_ctx):
        ids_copy(s, others[s]).wait_recv()
    my_expert = e.astype(f32)
    picks = []
    for j in range(n_ctx):
        first = jnp.broadcast_to(ids_all[j][0:1], (CAP, 128))
        second = jnp.broadcast_to(ids_all[j][1:2], (CAP, 128))
        picks.append(slots_of(first, second, my_expert).astype(bf16))

    for b in range(1, groups):
        z_copy(b, b).wait_recv()
        for s in (1, 2):
            xy_copy(s, b, ctx).start()
        pass_copy(0, b).start()
        forward(b - 1)

    squares = jnp.zeros((n_rows, 1), f32)
    own = part_ref.shape[0] // n_ctx

    for s in range(n_ctx):
        if s > 0:
            if s == 1:
                forward(groups - 1)
            if s == 2:
                for b in range(groups):
                    diagonal(b)
        for b in range(groups):
            pass_copy(s, b, 1 - lane).wait_recv()
        source = others[s]
        added = []
        gain = gain_ref[:, pl.ds(pl.multiple_of(source * TILE, TILE), TILE)]
        for j in range(n_ctx):
            dense = stream[source, :, j * own : (j + 1) * own, :].reshape(n_exp * own, TILE)
            picked = jnp.dot(picks[j], dense, preferred_element_type=f32)
            added.append(jnp.sum(picked * picked, axis=1, keepdims=True))
            rows[j * CAP : (j + 1) * CAP, :] = (picked * gain).astype(bf16)
        squares = squares + jnp.concatenate(added, axis=0)
        for n in range(blocks):
            for kind, total in (("gate", gate_sum), ("up", up_sum)):
                i = order.index((kind, s, n))
                tile = use_tile(i)

                def add(q, carry, tile=tile, total=total, n=n, s=s):
                    at = pl.ds(pl.multiple_of(q * 256, 256), 256)
                    to = pl.ds(pl.multiple_of(n * TILE + q * 256, 256), 256)
                    value = jnp.dot(rows[...], tile[:, at], preferred_element_type=f32)
                    total[:, to] = value if s == 0 else total[:, to] + value
                    return carry

                lax.fori_loop(0, TILE // 256, add, 0)
                done_tile(i)

    scale = lax.rsqrt(squares / float(n_ctx * TILE) + EPSILON)
    for n in range(hidden.shape[1] // 256):
        part = slice(n * 256, (n + 1) * 256)
        gate = gate_sum[:, part] * scale
        hidden[:, part] = (gate / (1.0 + jnp.exp(-gate)) * (up_sum[:, part] * scale)).astype(bf16)

    def term_copy(i, s):
        return remote(
            term.at[i, others[s]],
            came.at[i, s - 1],
            term_send.at[i, s - 1],
            term_recv.at[i, s - 1],
            {"ctx": others[s], "exp": e},
        )

    width = TILE // 2

    def out_copy(i, to, number):
        return remote(
            mine.at[i, to],
            outs.at[e],
            out_send.at[i, to],
            out_recv.at[i, number],
            {"ctx": ctx, "exp": turn[i] * 2 + to},
        )

    def sib_copy():
        return remote(
            mine.at[groups - 1, 1 - lane],
            outs.at[e],
            sib_send,
            sib_recv,
            {"ctx": ctx, "exp": sibling},
        )

    def reduce(i):
        total = term[i, ctx].astype(f32)
        for s in range(1, n_ctx):
            term_copy(i, s).wait_recv()
            total = total + came[i, s - 1].astype(f32)
        total = total.astype(bf16)
        for to in range(2):
            mine[i, to] = total[:, to * width : (to + 1) * width]
        if i < groups - 1:
            for to in range(2):
                out_copy(i, to, lane).start()
        else:
            sib_copy().start()
            outs[e] = mine[i, lane]

    for i in range(groups):
        for q in range(TILE // 256):
            at = slice(q * 256, (q + 1) * 256)
            value = jnp.zeros((n_rows, 256), f32)
            for f in range(blocks):
                number = order.index(("down", i, f))
                tile = use_tile(number) if q == 0 else tiles.at[number % SLOTS]
                value = value + jnp.dot(
                    hidden[:, f * TILE : (f + 1) * TILE],
                    tile[:, at],
                    preferred_element_type=f32,
                )
            for j in range(n_ctx):
                term[i, j, :, at] = value[j * CAP : (j + 1) * CAP].astype(bf16)
        for f in range(blocks):
            done_tile(order.index(("down", i, f)))
        for s in (3, 1, 2):
            term_copy(i, s).start()
    for i in range(groups):
        reduce(i)

    for i in range(groups - 1):
        for number in range(2):
            out_copy(i, 0, number).wait_recv()
    sib_copy().wait_recv()
    lot = outs[...].reshape(n_exp * CAP, width)
    value = jnp.dot(combine[0], lot, preferred_element_type=f32) + jnp.dot(
        combine[1], lot, preferred_element_type=f32
    )
    base = stream[
        group,
        :,
        pl.ds(pl.multiple_of(ctx * own, 16), own),
        pl.ds(pl.multiple_of(lane * width, 128), width),
    ].reshape(n_exp * own, width)
    out_ref[...] = (base.astype(f32) + value).astype(bf16)

    for s in range(1, n_ctx):
        ids_copy(s, ctx).wait_send()
        for i in range(groups):
            term_copy(i, s).wait_send()
    for d in range(1, groups):
        z_copy(d).wait_send()
    for b in range(groups):
        for s in (1, 2):
            xy_copy(s, b, ctx).wait_send()
            fwd_copy(s, b, others[3 - s]).wait_send()
        for s in range(n_ctx):
            pass_copy(s, b).wait_send()
    for i in range(groups - 1):
        for to in range(2):
            out_copy(i, to, lane).wait_send()
    sib_copy().wait_send()


def moe_stage(part, ids, route, moe_gain, gate, up, down, number):
    n_ctx, n_exp = lax.axis_size("ctx"), lax.axis_size("exp")
    groups = n_exp // 2
    own, cols = part.shape
    units = gate.shape[2]
    width = cols // 2
    n_rows = n_ctx * CAP
    f32, bf16, dma = jnp.float32, jnp.bfloat16, pltpu.SemaphoreType.DMA
    vmem, hbm = pl.BlockSpec(memory_space=pltpu.VMEM), pl.BlockSpec(memory_space=pl.ANY)
    return pl.pallas_call(
        moe_kernel,
        out_shape=jax.ShapeDtypeStruct((ids.shape[0], width), bf16),
        in_specs=[vmem] * 4 + [hbm] * 3,
        out_specs=vmem,
        scratch_shapes=[
            pltpu.VMEM((n_ctx, n_exp, own, cols), bf16),
            pltpu.VMEM((SLOTS, TILE, TILE), bf16),
            pltpu.VMEM((n_rows, units), f32),
            pltpu.VMEM((n_rows, units), f32),
            pltpu.VMEM((n_rows, TILE), bf16),
            pltpu.VMEM((n_rows, units), bf16),
            pltpu.VMEM((groups, n_ctx, CAP, TILE), bf16),
            pltpu.VMEM((groups, n_ctx - 1, CAP, TILE), bf16),
            pltpu.VMEM((groups, 2, CAP, width), bf16),
            pltpu.VMEM((n_exp, CAP, width), bf16),
            pltpu.VMEM((n_ctx, 8, 128), f32),
            pltpu.VMEM((2, ids.shape[0], n_exp * CAP), bf16),
            dma((SLOTS,)),
            dma((groups - 1,)),
            dma((groups - 1,)),
            dma((2, groups)),
            dma((2, groups)),
            dma((2, groups)),
            dma((2, groups)),
            dma((n_ctx, groups)),
            dma((n_ctx, groups)),
            dma((n_ctx - 1,)),
            dma((n_ctx - 1,)),
            dma((groups, n_ctx - 1)),
            dma((groups, n_ctx - 1)),
            dma((groups - 1, 2)),
            dma((groups - 1, 2)),
            dma,
            dma,
        ],
        compiler_params=pltpu.CompilerParams(
            collective_id=number, has_side_effects=True, vmem_limit_bytes=60 * 1024 * 1024
        ),
        cost_estimate=pl.CostEstimate(
            flops=6 * n_rows * n_ctx * TILE * units,
            bytes_accessed=6 * n_ctx * TILE * units,
            transcendentals=n_rows * units,
        ),
    )(part, ids, route, moe_gain.reshape(1, -1), gate, up, down)


def body(
    residual,
    ssm_input,
    ssm_gate,
    write_vectors,
    read_vectors,
    step_logits,
    decay_log,
    skip_gain,
    norm_gain,
    out_weight,
    moe_gain,
    gate_weight,
    up_weight,
    down_weight,
    expert_ids,
    route_weight,
):
    sizes = (lax.axis_size("ctx"), lax.axis_size("exp"), step_logits.shape[1], out_weight.shape[1])
    if sizes == (4, 8, SPAN, TILE) and gate_weight.shape[2] % TILE == 0:
        part = ssm_stage(
            ssm_input,
            ssm_gate,
            write_vectors,
            read_vectors,
            step_logits,
            decay_log,
            skip_gain,
            norm_gain,
            residual,
            out_weight,
            1,
        )
        return moe_stage(
            part, expert_ids, route_weight, moe_gain, gate_weight, up_weight, down_weight, 2
        )
    heads_dev = step_logits.shape[0]
    tok_rows = step_logits.shape[1]
    head_width = ssm_input.shape[1] // heads_dev
    span_count = tok_rows // SPAN
    step_size = jax.nn.softplus(step_logits)
    log_step = step_size * (-jnp.exp(decay_log))[:, None]
    cumulative = jnp.einsum(
        "hks,st->hkt",
        log_step.reshape(heads_dev, span_count, SPAN),
        jnp.triu(jnp.ones((SPAN, SPAN), jnp.float32)),
        precision=lax.Precision.HIGHEST,
    )
    step_blocks = step_size.reshape(heads_dev, span_count, SPAN)
    input_blocks = ssm_input.reshape(span_count, SPAN, heads_dev, head_width)
    write_blocks = write_vectors.reshape(span_count, SPAN, -1)
    read_blocks = read_vectors.reshape(span_count, SPAN, -1)
    scores = jnp.einsum(
        "ktn,ksn->kts", read_blocks, write_blocks, preferred_element_type=jnp.float32
    )
    causal = jnp.arange(SPAN)[:, None] >= jnp.arange(SPAN)[None, :]
    log_gaps = cumulative[:, :, :, None] - cumulative[:, :, None, :]
    mixing = jnp.where(
        causal,
        scores[None] * jnp.exp(jnp.where(causal, log_gaps, 0.0)) * step_blocks[:, :, None, :],
        0.0,
    ).astype(jnp.bfloat16)
    intra_out = jnp.einsum(
        "hkts,kshp->kthp", mixing, input_blocks, preferred_element_type=jnp.float32
    )
    end_weight = jnp.exp(cumulative[:, :, -1:] - cumulative) * step_blocks
    loaded = (end_weight[:, :, :, None] * write_blocks.astype(jnp.float32)[None]).astype(
        jnp.bfloat16
    )
    block_state = jnp.einsum(
        "kshp,hksn->hkpn", input_blocks, loaded, preferred_element_type=jnp.float32
    )
    block_decay = jnp.exp(cumulative[:, :, -1])
    running = jnp.zeros_like(block_state[:, 0])
    decay_run = jnp.ones_like(block_decay[:, 0])
    entering_list = [running]
    reach_list = [decay_run]
    running = block_decay[:, 0, None, None] * running + block_state[:, 0]
    decay_run = decay_run * block_decay[:, 0]
    device_state = running
    device_decay = decay_run

    all_states, all_decays = sent(
        [
            device_state.astype(jnp.bfloat16),
            jnp.broadcast_to(device_decay[:, None], (heads_dev, 128)),
        ],
        "ctx",
        1,
        True,
    )
    ctx_index = lax.axis_index("ctx")
    device_in = jnp.zeros_like(device_state)
    for j in range(lax.axis_size("ctx") - 1):
        device_in = jnp.where(
            j < ctx_index,
            all_decays[j, :, :1, None] * device_in + all_states[j].astype(jnp.float32),
            device_in,
        )
    entering = jnp.stack(entering_list, axis=1)
    reach = jnp.stack(reach_list, axis=1)
    states = entering + reach[:, :, None, None] * device_in[:, None]
    inter_out = jnp.transpose(jnp.exp(cumulative), (1, 2, 0))[:, :, :, None] * jnp.einsum(
        "ktn,hkpn->kthp", read_blocks.astype(jnp.float32), states, precision=lax.Precision.HIGHEST
    )
    scan_out = (
        intra_out + inter_out + skip_gain[None, None, :, None] * input_blocks.astype(jnp.float32)
    )
    scan_out = scan_out.reshape(tok_rows, heads_dev * head_width)
    gated_out = scan_out * jax.nn.silu(ssm_gate.astype(jnp.float32))
    grouped = gated_out.reshape(tok_rows, -1, NORM_GROUP)
    group_scale = lax.rsqrt(jnp.mean(grouped * grouped, axis=2, keepdims=True) + EPSILON)
    normed = ((grouped * group_scale).reshape(tok_rows, -1) * norm_gain).astype(jnp.bfloat16)
    ctx_count = lax.axis_size("ctx")
    exp_count = lax.axis_size("exp")
    exp_index = lax.axis_index("exp")
    width = residual.shape[1]
    slice_width = width // exp_count
    split_count = exp_count // EXPERTS
    own_rows = tok_rows // exp_count
    normed_all = sent([normed], "ctx", 2, True)[0].reshape(ctx_count * tok_rows, -1)
    ssm_terms = jnp.dot(normed_all, out_weight, preferred_element_type=jnp.float32).astype(
        jnp.bfloat16
    )
    groups = exp_count // 2
    by_owner = jnp.transpose(
        ssm_terms.reshape(ctx_count, groups, 2, own_rows, -1), (2, 1, 0, 3, 4)
    ).reshape(2, groups * ctx_count * own_rows, -1)
    halves = pair_sum(by_owner, 3)
    chips = sent([halves.reshape(groups, ctx_count * own_rows, -1)], "exp", 4, False, 2)[0]
    ssm_part = jnp.sum(chips.astype(jnp.float32), axis=0).astype(jnp.bfloat16)
    ssm_rows = sent([ssm_part.reshape(ctx_count, own_rows, -1)], "ctx", 5, False)[0]
    ssm_rows = jnp.transpose(ssm_rows, (1, 0, 2)).reshape(own_rows, width)
    own_residual = lax.dynamic_slice_in_dim(residual, exp_index * own_rows, own_rows, 0)
    stream_rows = (own_residual.astype(jnp.float32) + ssm_rows.astype(jnp.float32)).astype(
        jnp.bfloat16
    )
    token_of_slot, pick_rank = slot_tables(expert_ids)
    stream_full = gather_pairs(stream_rows, "exp", 6).reshape(tok_rows, width)
    stream_slice = lax.dynamic_slice_in_dim(stream_full, exp_index * slice_width, slice_width, 1)
    padded = jnp.concatenate(
        [stream_full, jnp.zeros((1, stream_full.shape[1]), jnp.bfloat16)], axis=0
    )
    my_slots = lax.dynamic_index_in_dim(token_of_slot, exp_index // split_count, 0, keepdims=False)
    picked = normalize(jnp.take(padded, my_slots, axis=0), moe_gain)
    normed_rows = sent([picked], "ctx", 7, True)[0].reshape(ctx_count * CAP, width)
    terms = expert_terms(normed_rows, gate_weight[0], up_weight[0], down_weight[0])
    arrived_terms = sent([terms.reshape(ctx_count, CAP, width)], "ctx", 8, False)[0]
    sums_mine = jnp.sum(arrived_terms.astype(jnp.float32), axis=0).astype(jnp.bfloat16)
    by_slice = jnp.transpose(sums_mine.reshape(CAP, exp_count, slice_width), (1, 0, 2))
    arrived = sent([by_slice], "exp", 9, False)[0].reshape(exp_count * CAP, slice_width)
    piece_expert = jnp.arange(exp_count, dtype=jnp.int32) // split_count
    slot_range = jnp.arange(CAP, dtype=jnp.int32)
    moe_slice = jnp.zeros((tok_rows, slice_width), jnp.float32)
    for k in range(expert_ids.shape[1]):
        hit_expert = expert_ids[:, k, None] == piece_expert[None, :]
        hit_slot = pick_rank[:, k, None] == slot_range[None, :]
        hits = (hit_expert[:, :, None] & hit_slot[:, None, :]).astype(jnp.bfloat16)
        picked_out = jnp.dot(
            hits.reshape(tok_rows, exp_count * CAP), arrived, preferred_element_type=jnp.float32
        )
        moe_slice = moe_slice + route_weight[:, k, None] * picked_out
    return (stream_slice.astype(jnp.float32) + moe_slice).astype(jnp.bfloat16)


def solution(mesh):
    placed = (
        P("ctx", None),
        P("ctx", "exp"),
        P("ctx", "exp"),
        P("ctx", None),
        P("ctx", None),
        P("exp", "ctx"),
        P("exp"),
        P("exp"),
        P("exp"),
        P("exp", "ctx"),
        P(),
        P("exp", None, "ctx"),
        P("exp", None, "ctx"),
        P("exp", "ctx", None),
        P("ctx", None),
        P("ctx", None),
    )
    return jax.shard_map(
        body, mesh=mesh, in_specs=placed, out_specs=P("ctx", "exp"), check_vma=False
    )
```

```python
import functools
import math

import jax
import jax.numpy as jnp
from jax import lax
from jax.experimental import pallas as pl
from jax.experimental.pallas import tpu as pltpu
from jax.sharding import PartitionSpec as P

SPAN = 128
NORM_GROUP = 512
EXPERTS = 8
CAP = 64


EPSILON = 1e-05


MESH = pl.DeviceIdType.MESH


def send_kernel(axis, count, pair, spread, n_arrays, *refs):
    sources, targets = refs[:n_arrays], refs[n_arrays : 2 * n_arrays]
    local_sem, send_sem, recv_sem = refs[2 * n_arrays :]
    index = lax.axis_index(axis)
    group, lane = index // pair, lax.rem(index, pair)
    barrier = pltpu.get_barrier_semaphore()
    peers = [lax.rem(group + d, count) for d in range(1, count)]
    for peer in peers:
        pl.semaphore_signal(
            barrier, inc=1, device_id={axis: peer * pair + lane}, device_id_type=MESH
        )
    pl.semaphore_wait(barrier, count - 1)
    copies = []
    for d, peer in enumerate(peers):
        for i in range(n_arrays):
            copy = pltpu.make_async_remote_copy(
                src_ref=sources[i] if spread else sources[i].at[peer],
                dst_ref=targets[i].at[group],
                send_sem=send_sem.at[d, i],
                recv_sem=recv_sem.at[d, i],
                device_id={axis: peer * pair + lane},
                device_id_type=MESH,
            )
            copy.start()
            copies.append(copy)
    for i in range(n_arrays):
        own = pltpu.make_async_copy(
            sources[i] if spread else sources[i].at[group],
            targets[i].at[group],
            local_sem.at[i],
        )
        own.start()
        copies.append(own)
    for copy in copies:
        copy.wait()


def sent(arrays, axis, number, spread, pair=1):
    count = lax.axis_size(axis) // pair
    n_arrays = len(arrays)
    shapes = [
        jax.ShapeDtypeStruct((count,) + a.shape if spread else a.shape, a.dtype) for a in arrays
    ]
    size = sum(math.prod(shape.shape) * shape.dtype.itemsize for shape in shapes)
    return pl.pallas_call(
        functools.partial(send_kernel, axis, count, pair, spread, n_arrays),
        out_shape=shapes,
        in_specs=[pl.BlockSpec(memory_space=pl.ANY)] * n_arrays,
        out_specs=[pl.BlockSpec(memory_space=pl.ANY)] * n_arrays,
        scratch_shapes=[
            pltpu.SemaphoreType.DMA((n_arrays,)),
            pltpu.SemaphoreType.DMA((count - 1, n_arrays)),
            pltpu.SemaphoreType.DMA((count - 1, n_arrays)),
        ],
        compiler_params=pltpu.CompilerParams(collective_id=number, has_side_effects=True),
        cost_estimate=pl.CostEstimate(flops=0, bytes_accessed=2 * size, transcendentals=0),
    )(*arrays)


def gather_pairs_kernel(axis, groups, x_ref, out_ref, local_sem, send_sem, recv_sem, pass_send, pass_recv):
    index = lax.axis_index(axis)
    group, lane = index // 2, lax.rem(index, 2)
    sibling = group * 2 + 1 - lane
    barrier = pltpu.get_barrier_semaphore()
    peers = [lax.rem(group + d, groups) for d in range(1, groups)]
    for peer in [p * 2 + lane for p in peers] + [sibling]:
        pl.semaphore_signal(barrier, inc=1, device_id={axis: peer}, device_id_type=MESH)
    pl.semaphore_wait(barrier, groups)
    copies = []
    for d, peer in enumerate(peers):
        copy = pltpu.make_async_remote_copy(
            src_ref=x_ref,
            dst_ref=out_ref.at[index],
            send_sem=send_sem.at[d],
            recv_sem=recv_sem.at[d],
            device_id={axis: peer * 2 + lane},
            device_id_type=MESH,
        )
        copy.start()
        copies.append(copy)
    own = pltpu.make_async_copy(x_ref, out_ref.at[index], local_sem)
    own.start()
    passed = [
        pltpu.make_async_remote_copy(
            src_ref=x_ref,
            dst_ref=out_ref.at[index],
            send_sem=pass_send.at[0],
            recv_sem=pass_recv.at[0],
            device_id={axis: sibling},
            device_id_type=MESH,
        )
    ]
    passed[0].start()
    for d in range(1, groups):
        copies[d - 1].wait_recv()
        block = lax.rem(group + groups - d, groups) * 2 + lane
        copy = pltpu.make_async_remote_copy(
            src_ref=out_ref.at[block],
            dst_ref=out_ref.at[block],
            send_sem=pass_send.at[d],
            recv_sem=pass_recv.at[d],
            device_id={axis: sibling},
            device_id_type=MESH,
        )
        copy.start()
        passed.append(copy)
    for copy in copies:
        copy.wait_send()
    own.wait()
    for copy in passed:
        copy.wait()


def gather_pairs(x, axis, number):
    count = lax.axis_size(axis)
    return pl.pallas_call(
        functools.partial(gather_pairs_kernel, axis, count // 2),
        out_shape=jax.ShapeDtypeStruct((count,) + x.shape, x.dtype),
        in_specs=[pl.BlockSpec(memory_space=pl.ANY)],
        out_specs=pl.BlockSpec(memory_space=pl.ANY),
        scratch_shapes=[
            pltpu.SemaphoreType.DMA,
            pltpu.SemaphoreType.DMA((count // 2 - 1,)),
            pltpu.SemaphoreType.DMA((count // 2 - 1,)),
            pltpu.SemaphoreType.DMA((count // 2,)),
            pltpu.SemaphoreType.DMA((count // 2,)),
        ],
        compiler_params=pltpu.CompilerParams(collective_id=number, has_side_effects=True),
        cost_estimate=pl.CostEstimate(
            flops=0, bytes_accessed=2 * count * x.size * x.dtype.itemsize, transcendentals=0
        ),
    )(x)


def pair_sum(halves, number):
    lane = lax.rem(lax.axis_index("exp"), 2)
    both = pair_send(halves, number)
    own = lax.dynamic_index_in_dim(halves, lane, 0, keepdims=False)
    return (own.astype(jnp.float32) + both.astype(jnp.float32)).astype(jnp.bfloat16)


def pair_kernel(x_ref, out_ref, send_sem, recv_sem):
    index = lax.axis_index("exp")
    lane = lax.rem(index, 2)
    sibling = index + 1 - 2 * lane
    barrier = pltpu.get_barrier_semaphore()
    pl.semaphore_signal(barrier, inc=1, device_id={"exp": sibling}, device_id_type=MESH)
    pl.semaphore_wait(barrier, 1)
    copy = pltpu.make_async_remote_copy(
        src_ref=x_ref.at[1 - lane],
        dst_ref=out_ref,
        send_sem=send_sem,
        recv_sem=recv_sem,
        device_id={"exp": sibling},
        device_id_type=MESH,
    )
    copy.start()
    copy.wait()


def pair_send(halves, number):
    return pl.pallas_call(
        pair_kernel,
        out_shape=jax.ShapeDtypeStruct(halves.shape[1:], halves.dtype),
        in_specs=[pl.BlockSpec(memory_space=pl.ANY)],
        out_specs=pl.BlockSpec(memory_space=pl.ANY),
        scratch_shapes=[pltpu.SemaphoreType.DMA, pltpu.SemaphoreType.DMA],
        compiler_params=pltpu.CompilerParams(collective_id=number, has_side_effects=True),
        cost_estimate=pl.CostEstimate(
            flops=0, bytes_accessed=halves.size * 2, transcendentals=0
        ),
    )(halves)


def expert_kernel(x_ref, gate_ref, up_ref, down_ref, out_ref, total):
    step = pl.program_id(1)
    gate_val = jnp.dot(x_ref[...], gate_ref[...], preferred_element_type=jnp.float32)
    up_val = jnp.dot(x_ref[...], up_ref[...], preferred_element_type=jnp.float32)
    hidden = (gate_val / (1.0 + jnp.exp(-gate_val)) * up_val).astype(jnp.bfloat16)
    columns = down_ref.shape[1] // 4

    def add(first):
        for c in range(4):
            part = slice(c * columns, (c + 1) * columns)
            term = jnp.dot(hidden, down_ref[:, part], preferred_element_type=jnp.float32)
            total[:, part] = term if first else total[:, part] + term

    pl.when(step == 0)(lambda: add(True))
    pl.when(step > 0)(lambda: add(False))

    @pl.when(step == pl.num_programs(1) - 1)
    def _():
        out_ref[...] = total[...].astype(out_ref.dtype)


def expert_terms(rows, gate, up, down):
    count, width = rows.shape
    units = gate.shape[1]
    block = 256 if units % 256 == 0 else 128
    tall = 256 if count % 256 == 0 else count
    return pl.pallas_call(
        expert_kernel,
        out_shape=jax.ShapeDtypeStruct((count, width), jnp.bfloat16),
        grid=(count // tall, units // block),
        in_specs=[
            pl.BlockSpec((tall, width), lambda r, i: (r, 0)),
            pl.BlockSpec((width, block), lambda r, i: (0, i)),
            pl.BlockSpec((width, block), lambda r, i: (0, i)),
            pl.BlockSpec((block, width), lambda r, i: (i, 0)),
        ],
        out_specs=pl.BlockSpec((tall, width), lambda r, i: (r, 0)),
        scratch_shapes=[pltpu.VMEM((tall, width), jnp.float32)],
        compiler_params=pltpu.CompilerParams(vmem_limit_bytes=48 * 1024 * 1024),
        cost_estimate=pl.CostEstimate(
            flops=6 * count * width * units,
            bytes_accessed=6 * width * units,
            transcendentals=count * units,
        ),
    )(rows, gate, up, down)


def slot_tables(block_ids):
    expert_range = jnp.arange(EXPERTS, dtype=jnp.int32)
    hit_table = jnp.sum(
        (block_ids[:, :, None] == expert_range[None, None, :]).astype(jnp.int32), axis=1
    )
    lower = jnp.tril(jnp.ones((block_ids.shape[0],) * 2, jnp.bfloat16))
    ranking = (
        jnp.dot(lower, hit_table.astype(jnp.bfloat16), preferred_element_type=jnp.float32)
    ).astype(jnp.int32) - 1
    slot_range = jnp.arange(CAP, dtype=jnp.int32)
    matches = (hit_table.T[:, None, :] == 1) & (ranking.T[:, None, :] == slot_range[None, :, None])
    row_count = block_ids.shape[0]
    row_range = jnp.arange(row_count, dtype=jnp.int32)
    chosen = jnp.sum(jnp.where(matches, row_range[None, None, :], 0), axis=2)
    filled = jnp.any(matches, axis=2)
    token_of_slot = jnp.where(filled, chosen, row_count)
    pick_rank = jnp.take_along_axis(ranking, block_ids, axis=1)
    return (token_of_slot, pick_rank)


def normalize(stream_rows, moe_gain):
    values = stream_rows.astype(jnp.float32)
    scale_inv = lax.rsqrt(jnp.mean(values * values, axis=-1, keepdims=True) + EPSILON)
    return (values * scale_inv * moe_gain).astype(jnp.bfloat16)


def remote(src, dst, send_sem, recv_sem, device):
    return pltpu.make_async_remote_copy(
        src_ref=src,
        dst_ref=dst,
        send_sem=send_sem,
        recv_sem=recv_sem,
        device_id=device,
        device_id_type=MESH,
    )


def xor(a, s):
    low = lax.rem(a, 2)
    low = 1 - low if s % 2 else low
    high = a // 2
    high = 1 - high if s // 2 else high
    return high * 2 + low


TILE = 1024
SLOTS = 14


def layer_kernel(
    x_hbm,
    z_hbm,
    write_hbm,
    read_hbm,
    logit_hbm,
    decay_hbm,
    skip_hbm,
    norm_gain_hbm,
    residual_hbm,
    weight_hbm,
    ids_hbm,
    route_hbm,
    moe_gain_hbm,
    gate_hbm,
    up_hbm,
    down_hbm,
    out_ref,
    x_ref,
    z_ref,
    write_ref,
    read_ref,
    logit_ref,
    decay_ref,
    skip_ref,
    norm_gain_ref,
    residual_ref,
    weight,
    ids_ref,
    route_ref,
    moe_gain_ref,
    states,
    decays,
    entered,
    scan,
    normed,
    terms,
    paired,
    sums,
    arrived,
    rest,
    stream,
    tiles,
    gate_sum,
    up_sum,
    rows,
    hidden,
    term,
    came,
    mine,
    outs,
    ids_all,
    combine,
    load_sem,
    state_send,
    state_recv,
    norm_send,
    norm_recv,
    pair_send_sem,
    pair_recv_sem,
    sum_send,
    sum_recv,
    rest_send,
    rest_recv,
    tile_sem,
    z_send,
    z_recv,
    xy_send,
    xy_recv,
    fwd_send,
    fwd_recv,
    pass_send,
    pass_recv,
    ids_send,
    ids_recv,
    term_send,
    term_recv,
    out_send,
    out_recv,
    sib_send,
    sib_recv,
):
    f32, bf16 = jnp.float32, jnp.bfloat16
    n_ctx, n_exp = 4, 8
    groups = n_exp // 2
    ctx, e = lax.axis_index("ctx"), lax.axis_index("exp")
    group, lane = e // 2, lax.rem(e, 2)
    sibling = group * 2 + 1 - lane
    tokens, channels = x_ref.shape
    heads = logit_ref.shape[0]
    wide = 2 * (channels // heads)
    own_rows = tokens // n_exp
    cols = weight.shape[1]
    blocks = hidden.shape[1] // TILE
    n_rows = n_ctx * CAP
    others = [xor(ctx, s) for s in range(n_ctx)]
    chips = [lax.rem(group + d, groups) for d in range(groups)]

    back = [lax.rem(group + groups - d, groups) for d in range(groups)]
    turn = [lax.rem(group + 1 + i, groups) for i in range(groups)]
    barrier = pltpu.get_barrier_semaphore()
    peers = [{"ctx": others[s], "exp": e} for s in range(1, n_ctx)] + [
        {"ctx": ctx, "exp": lax.rem(e + d, n_exp)} for d in range(1, n_exp)
    ]
    for peer in peers:
        pl.semaphore_signal(barrier, inc=1, device_id=peer, device_id_type=MESH)

    loads = [
        pltpu.make_async_copy(src, dst, load_sem.at[i])
        for i, (src, dst) in enumerate(
            (
                (logit_hbm, logit_ref),
                (decay_hbm, decay_ref),
                (write_hbm, write_ref),
                (x_hbm, x_ref),
                (read_hbm, read_ref),
                (skip_hbm, skip_ref),
                (z_hbm, z_ref),
                (norm_gain_hbm, norm_gain_ref),
                (ids_hbm, ids_ref),
                (route_hbm, route_ref),
                (moe_gain_hbm, moe_gain_ref),
                (residual_hbm.at[pl.ds(pl.multiple_of(e * own_rows, 16), own_rows)], residual_ref),
                (weight_hbm, weight),
            )
        )
    ]
    for load in loads:
        load.start()

    order = [
        (kind, s, n) for s in range(n_ctx) for n in range(blocks) for kind in ("gate", "up")
    ] + [("down", m, f) for m in range(groups) for f in range(blocks)]

    def tile_copy(i):
        kind, outer, inner = order[i]
        fixed = pl.ds(inner * TILE, TILE)
        if kind == "down":
            moving = pl.ds(pl.multiple_of(turn[outer] * TILE, TILE), TILE)
            src = down_hbm.at[0, fixed, moving]
        else:
            moving = pl.ds(pl.multiple_of(others[outer] * TILE, TILE), TILE)
            src = (gate_hbm if kind == "gate" else up_hbm).at[0, moving, fixed]
        return pltpu.make_async_copy(src, tiles.at[i % SLOTS], tile_sem.at[i % SLOTS])

    def use_tile(i):
        tile_copy(i).wait()
        return tiles.at[i % SLOTS]

    def done_tile(i):
        if i + SLOTS < len(order):
            tile_copy(i + SLOTS).start()

    for load in loads[:-1]:
        load.wait()

    step = jnp.maximum(logit_ref[...], 0.0) + jnp.log1p(jnp.exp(-jnp.abs(logit_ref[...])))
    diagonal = lax.broadcasted_iota(jnp.int32, (heads, heads), 0) == lax.broadcasted_iota(
        jnp.int32, (heads, heads), 1
    )

    def column(row):
        return jnp.sum(
            jnp.where(diagonal, jnp.broadcast_to(row, (heads, heads)), 0.0), axis=1, keepdims=True
        )

    head_of = lax.broadcasted_iota(jnp.int32, (heads, channels), 1) // (channels // heads)
    own_head = head_of == lax.broadcasted_iota(jnp.int32, (heads, channels), 0)

    def spread_row(col):
        return jnp.sum(
            jnp.where(own_head, jnp.broadcast_to(col, (heads, channels)), 0.0),
            axis=0,
            keepdims=True,
        )

    log_step = step * (-jnp.exp(column(decay_ref[...])))
    row_i = lax.broadcasted_iota(jnp.int32, (tokens, tokens), 0)
    col_i = lax.broadcasted_iota(jnp.int32, (tokens, tokens), 1)
    upper = (row_i <= col_i).astype(f32)
    cumulative = jnp.dot(
        log_step, upper, precision=lax.Precision.HIGHEST, preferred_element_type=f32
    )
    last = cumulative[:, tokens - 1 : tokens]
    end_weight = jnp.exp(last - cumulative) * step
    stacked = jnp.concatenate(
        [
            cumulative,
            jnp.exp(cumulative),
            end_weight,
            jnp.zeros((tokens - 3 * heads, tokens), f32),
        ],
        axis=0,
    ).T
    first_half = lax.broadcasted_iota(jnp.int32, (tokens, wide), 1) < wide // 2

    def pair_columns(first, q):
        return jnp.where(
            first_half,
            stacked[:, first + 2 * q : first + 2 * q + 1],
            stacked[:, first + 2 * q + 1 : first + 2 * q + 2],
        )

    write_t = write_ref[...].astype(f32).T.astype(bf16)
    for q in range(heads // 2):
        part = slice(q * wide, (q + 1) * wide)
        weighted = (pair_columns(2 * heads, q) * x_ref[:, part].astype(f32)).astype(bf16)
        states[ctx, :, part] = jnp.dot(
            write_t, weighted, preferred_element_type=f32
        ).astype(bf16)
    decays[ctx] = jnp.broadcast_to(jnp.exp(last), (heads, tokens))

    pl.semaphore_wait(barrier, len(peers))

    def state_copies(d, device_ctx, slot):
        return [
            remote(
                buf.at[slot],
                buf.at[slot],
                state_send.at[d - 1, i],
                state_recv.at[d - 1, i],
                {"ctx": device_ctx, "exp": e},
            )
            for i, buf in enumerate((states, decays))
        ]

    for d in range(1, n_ctx):

        @pl.when(ctx + d < n_ctx)
        def _(d=d):
            for copy in state_copies(d, ctx + d, ctx):
                copy.start()

    rest_copies = [
        remote(
            residual_ref.at[:, pl.ds(pl.multiple_of(others[s] * cols, cols), cols)],
            rest.at[s],
            rest_send.at[s - 1],
            rest_recv.at[s - 1],
            {"ctx": others[s], "exp": e},
        )
        for s in range(1, n_ctx)
    ]
    for copy in rest_copies:
        copy.start()
    rest[0] = residual_ref[:, pl.ds(pl.multiple_of(ctx * cols, cols), cols)]

    for i in range(SLOTS):
        tile_copy(i).start()

    causal = row_i >= col_i
    scores = lax.dot_general(
        read_ref[...], write_ref[...], (((1,), (1,)), ((), ())), preferred_element_type=f32
    )
    for q in range(heads // 2):
        part = slice(q * wide, (q + 1) * wide)
        x_pair = x_ref[:, part]
        pair_outs = []
        for h in (2 * q, 2 * q + 1):
            gap = stacked[:, h : h + 1] - cumulative[h : h + 1, :]
            decayed = jnp.exp(jnp.where(causal, gap, 0.0)) * step[h : h + 1, :]
            mixing = jnp.where(causal, scores * decayed, 0.0).astype(bf16)
            pair_outs.append(jnp.dot(mixing, x_pair, preferred_element_type=f32))
        scan[:, part] = jnp.where(first_half, pair_outs[0], pair_outs[1])

    entered[...] = jnp.zeros_like(entered)
    for d in range(n_ctx - 1, 0, -1):

        @pl.when(ctx >= d)
        def _(d=d):
            source = ctx - d
            for copy in state_copies(d, ctx, source):
                copy.wait_recv()
            entered[...] = spread_row(decays[source][:, :1]) * entered[...] + states[
                source
            ].astype(f32)

    high = entered[...].astype(bf16)
    low = (entered[...] - high.astype(f32)).astype(bf16)
    reads = read_ref[...]
    skip = spread_row(column(skip_ref[...]))
    for q in range(heads // 2):
        part = slice(q * wide, (q + 1) * wide)
        inter = jnp.dot(reads, high[:, part], preferred_element_type=f32) + jnp.dot(
            reads, low[:, part], preferred_element_type=f32
        )
        value = (
            scan[:, part]
            + pair_columns(heads, q) * inter
            + skip[:, part] * x_ref[:, part].astype(f32)
        )
        gate = z_ref[:, part].astype(f32)
        scan[:, part] = value * (gate / (1.0 + jnp.exp(-gate)))
    for n in range(channels // NORM_GROUP):
        part = slice(n * NORM_GROUP, (n + 1) * NORM_GROUP)
        value = scan[:, part]
        scale = lax.rsqrt(jnp.mean(value * value, axis=1, keepdims=True) + EPSILON)
        normed[ctx, :, part] = (value * scale * norm_gain_ref[:, part]).astype(bf16)

    norm_half = tokens // 2

    def norm_copy(s, source, rows, number):
        where = normed.at[source] if rows is None else normed.at[source, pl.ds(rows, norm_half)]
        return remote(
            where, where, norm_send.at[number], norm_recv.at[number], {"ctx": others[s], "exp": e}
        )

    norm_copies = [norm_copy(1, ctx, None, 0), norm_copy(2, ctx, None, 1)]
    for copy in norm_copies:
        copy.start()
    loads[-1].wait()

    def project(s):
        value = jnp.dot(
            normed[others[s]], weight[...], preferred_element_type=f32
        ).astype(bf16)
        for owner in range(n_exp):
            terms[s, owner % 2, owner // 2] = value[owner * own_rows : (owner + 1) * own_rows]

    def pair_copy(s):
        return remote(
            terms.at[s, 1 - lane],
            paired.at[s],
            pair_send_sem.at[s],
            pair_recv_sem.at[s],
            {"ctx": ctx, "exp": sibling},
        )

    def sum_copy(s, d):
        return remote(
            sums.at[s, chips[d]],
            arrived.at[s, d - 1],
            sum_send.at[s, d - 1],
            sum_recv.at[s, d - 1],
            {"ctx": ctx, "exp": chips[d] * 2 + lane},
        )

    def add_pair(s):
        pair_copy(s).wait_recv()
        sums[s] = (terms[s, lane].astype(f32) + paired[s].astype(f32)).astype(bf16)
        for d in range(1, groups):
            sum_copy(s, d).start()

    project(0)
    pair_copy(0).start()
    norm_copies[0].wait_recv()
    norm_copies.append(norm_copy(2, others[1], 0, 2))
    norm_copies[2].start()
    norm_copies[1].wait_recv()
    norm_copies.append(norm_copy(1, others[2], norm_half, 3))
    norm_copies[3].start()
    add_pair(0)
    project(1)
    pair_copy(1).start()
    project(2)
    pair_copy(2).start()
    add_pair(1)
    add_pair(2)
    norm_copies[2].wait_recv()
    norm_copies[3].wait_recv()
    project(3)
    pair_copy(3).start()
    add_pair(3)
    for copy in rest_copies:
        copy.wait()
    for s in range(n_ctx):
        total = sums[s, group].astype(f32)
        for d in range(1, groups):
            sum_copy(s, d).wait_recv()
            total = total + arrived[s, d - 1].astype(f32)
        total = total.astype(bf16).astype(f32) + rest[s].astype(f32)
        stream[ctx, e, pl.ds(pl.multiple_of(others[s] * own_rows, 16), own_rows), :] = total.astype(bf16)

    ids_rows = [jnp.broadcast_to(ids_ref[k : k + 1, :].astype(f32), (CAP, tokens)) for k in range(2)]
    ids_all[ctx] = jnp.where(row_i[:8] == 0, ids_rows[0][:8], ids_rows[1][:8])

    def block(ref, source, b):
        return ref.at[source, back[b] * 2 + lane]

    def z_copy(d, b=0):
        where = block(stream, ctx, b)
        return remote(
            where,
            where,
            z_send.at[d - 1],
            z_recv.at[d - 1],
            {"ctx": ctx, "exp": chips[d] * 2 + lane},
        )

    def xy_copy(s, b, source):
        where = block(stream, source, b)
        return remote(
            where,
            where,
            xy_send.at[s - 1, b],
            xy_recv.at[s - 1, b],
            {"ctx": others[s], "exp": e},
        )

    half = stream.shape[2] // 2

    def fwd_copy(s, b, source):
        where = stream.at[source, back[b] * 2 + lane, pl.ds((2 - s) * half, half)]
        return remote(
            where,
            where,
            fwd_send.at[s - 1, b],
            fwd_recv.at[s - 1, b],
            {"ctx": others[s], "exp": e},
        )

    def pass_copy(s, b, which=None):
        where = stream.at[others[s], back[b] * 2 + (lane if which is None else which)]
        return remote(
            where, where, pass_send.at[s, b], pass_recv.at[s, b], {"ctx": ctx, "exp": sibling}
        )

    def ids_copy(s, source):
        where = ids_all.at[source]
        return remote(
            where, where, ids_send.at[s - 1], ids_recv.at[s - 1], {"ctx": others[s], "exp": e}
        )

    def forward(b):
        xy_copy(1, b, others[1]).wait_recv()
        fwd_copy(2, b, others[1]).start()
        pass_copy(1, b).start()
        xy_copy(2, b, others[2]).wait_recv()
        fwd_copy(1, b, others[2]).start()
        pass_copy(2, b).start()

    def diagonal(b):
        fwd_copy(1, b, others[3]).wait_recv()
        fwd_copy(2, b, others[3]).wait_recv()
        pass_copy(3, b).start()

    for s in range(1, n_ctx):
        ids_copy(s, ctx).start()
    for d in range(1, groups):
        z_copy(d).start()
    for s in (1, 2):
        xy_copy(s, 0, ctx).start()
    pass_copy(0, 0).start()

    upper = upper.astype(bf16)
    slot_i = lax.broadcasted_iota(jnp.int32, (CAP, 128), 0).astype(f32)

    def slots_of(first, second, expert):
        hit = jnp.where((first == expert) | (second == expert), 1.0, 0.0)
        rank = jnp.dot(hit.astype(bf16), upper, preferred_element_type=f32) - 1.0
        return jnp.where((hit > 0.0) & (rank == slot_i), 1.0, 0.0)

    own_ids = ids_rows
    own_route = [jnp.broadcast_to(route_ref[k : k + 1, :], (CAP, tokens)) for k in range(2)]
    for pair in range(n_exp // 2):
        both = []
        for x in (2 * pair, 2 * pair + 1):
            weight = jnp.where(own_ids[0] == float(x), own_route[0], own_route[1])
            both.append(slots_of(own_ids[0], own_ids[1], float(x)) * weight)
        back_table = jnp.concatenate(both, axis=0).T
        high = back_table.astype(bf16)
        part = slice(pair * 128, (pair + 1) * 128)
        combine[0, :, part] = high
        combine[1, :, part] = (back_table - high.astype(f32)).astype(bf16)

    for s in range(1, n_ctx):
        ids_copy(s, others[s]).wait_recv()
    my_expert = e.astype(f32)
    picks = []
    for j in range(n_ctx):
        first = jnp.broadcast_to(ids_all[j][0:1], (CAP, 128))
        second = jnp.broadcast_to(ids_all[j][1:2], (CAP, 128))
        picks.append(slots_of(first, second, my_expert).astype(bf16))

    for b in range(1, groups):
        z_copy(b, b).wait_recv()
        for s in (1, 2):
            xy_copy(s, b, ctx).start()
        pass_copy(0, b).start()
        forward(b - 1)

    squares = jnp.zeros((n_rows, 1), f32)
    own = own_rows

    for s in range(n_ctx):
        if s > 0:
            if s == 1:
                forward(groups - 1)
            if s == 2:
                for b in range(groups):
                    diagonal(b)
        for b in range(groups):
            pass_copy(s, b, 1 - lane).wait_recv()
        source = others[s]
        added = []
        gain = moe_gain_ref[:, pl.ds(pl.multiple_of(source * TILE, TILE), TILE)]
        for j in range(n_ctx):
            dense = stream[source, :, j * own : (j + 1) * own, :].reshape(n_exp * own, TILE)
            picked = jnp.dot(picks[j], dense, preferred_element_type=f32)
            added.append(jnp.sum(picked * picked, axis=1, keepdims=True))
            rows[j * CAP : (j + 1) * CAP, :] = (picked * gain).astype(bf16)
        squares = squares + jnp.concatenate(added, axis=0)
        for number in range(s * 2 * blocks, (s + 1) * 2 * blocks):
            tile_copy(number).wait()

        def step_of(n, carry, s=s):
            to = pl.ds(pl.multiple_of(n * TILE, TILE), TILE)
            for kind, total in enumerate((gate_sum, up_sum)):
                slot = lax.rem(s * 2 * blocks + 2 * n + kind, SLOTS)
                value = jnp.dot(rows[...], tiles[slot], preferred_element_type=f32)
                total[:, to] = value if s == 0 else total[:, to] + value
            return carry

        lax.fori_loop(0, blocks, step_of, 0)
        for number in range(s * 2 * blocks, (s + 1) * 2 * blocks):
            done_tile(number)

    scale = lax.rsqrt(squares / float(n_ctx * TILE) + EPSILON)
    for n in range(hidden.shape[1] // 256):
        part = slice(n * 256, (n + 1) * 256)
        gate = gate_sum[:, part] * scale
        hidden[:, part] = (gate / (1.0 + jnp.exp(-gate)) * (up_sum[:, part] * scale)).astype(bf16)

    def term_copy(i, s):
        return remote(
            term.at[i, others[s]],
            came.at[i, s - 1],
            term_send.at[i, s - 1],
            term_recv.at[i, s - 1],
            {"ctx": others[s], "exp": e},
        )

    width = TILE // 2

    def out_copy(i, to, number):
        return remote(
            mine.at[i, to],
            outs.at[e],
            out_send.at[i, to],
            out_recv.at[i, number],
            {"ctx": ctx, "exp": turn[i] * 2 + to},
        )

    def sib_copy():
        return remote(
            mine.at[groups - 1, 1 - lane],
            outs.at[e],
            sib_send,
            sib_recv,
            {"ctx": ctx, "exp": sibling},
        )

    def reduce(i):
        total = term[i, ctx].astype(f32)
        for s in range(1, n_ctx):
            term_copy(i, s).wait_recv()
            total = total + came[i, s - 1].astype(f32)
        total = total.astype(bf16)
        for to in range(2):
            mine[i, to] = total[:, to * width : (to + 1) * width]
        if i < groups - 1:
            for to in range(2):
                out_copy(i, to, lane).start()
        else:
            sib_copy().start()
            outs[e] = mine[i, lane]

    for i in range(groups):
        value = None
        for f in range(blocks):
            tile = use_tile(order.index(("down", i, f)))
            more = jnp.dot(
                hidden[:, f * TILE : (f + 1) * TILE], tile[...], preferred_element_type=f32
            )
            value = more if value is None else value + more
        for j in range(n_ctx):
            term[i, j] = value[j * CAP : (j + 1) * CAP].astype(bf16)
        for f in range(blocks):
            done_tile(order.index(("down", i, f)))
        for s in (3, 1, 2):
            term_copy(i, s).start()
    for i in range(groups):
        reduce(i)

    for i in range(groups - 1):
        for number in range(2):
            out_copy(i, 0, number).wait_recv()
    sib_copy().wait_recv()
    lot = outs[...].reshape(n_exp * CAP, width)
    value = jnp.dot(combine[0], lot, preferred_element_type=f32) + jnp.dot(
        combine[1], lot, preferred_element_type=f32
    )
    base = stream[
        group,
        :,
        pl.ds(pl.multiple_of(ctx * own, 16), own),
        pl.ds(pl.multiple_of(lane * width, 128), width),
    ].reshape(n_exp * own, width)
    out_ref[...] = (base.astype(f32) + value).astype(bf16)

    for s in range(1, n_ctx):
        ids_copy(s, ctx).wait_send()
        for i in range(groups):
            term_copy(i, s).wait_send()
    for d in range(1, groups):
        z_copy(d).wait_send()
    for b in range(groups):
        for s in (1, 2):
            xy_copy(s, b, ctx).wait_send()
            fwd_copy(s, b, others[3 - s]).wait_send()
        for s in range(n_ctx):
            pass_copy(s, b).wait_send()
    for i in range(groups - 1):
        for to in range(2):
            out_copy(i, to, lane).wait_send()
    sib_copy().wait_send()


    for copy in norm_copies:
        copy.wait_send()
    for s in range(n_ctx):
        pair_copy(s).wait_send()
        for d in range(1, groups):
            sum_copy(s, d).wait_send()
    for d in range(1, n_ctx):

        @pl.when(ctx + d < n_ctx)
        def _(d=d):
            for copy in state_copies(d, ctx + d, ctx):
                copy.wait_send()


def layer(
    x, z, write, read, logits, decay_log, skip_gain, norm_gain, residual, out_weight, ids, route,
    moe_gain, gate, up, down, number,
):
    n_ctx, n_exp = lax.axis_size("ctx"), lax.axis_size("exp")
    tokens, channels = x.shape
    heads = logits.shape[0]
    cols = out_weight.shape[1]
    own_rows = tokens // n_exp
    groups = n_exp // 2
    units = gate.shape[2]
    width = cols // 2
    n_rows = n_ctx * CAP
    size = write.shape[1]
    f32, bf16, dma = jnp.float32, jnp.bfloat16, pltpu.SemaphoreType.DMA
    vmem = pltpu.VMEM
    inputs = (
        x,
        z,
        write,
        read,
        logits,
        decay_log.reshape(1, -1),
        skip_gain.reshape(1, -1),
        norm_gain.reshape(1, -1),
        residual,
        out_weight,
        ids.T,
        route.T,
        moe_gain.reshape(1, -1),
        gate,
        up,
        down,
    )
    held = [vmem(a.shape, a.dtype) for a in inputs[:13]]
    held[8] = vmem((own_rows, residual.shape[1]), bf16)
    return pl.pallas_call(
        layer_kernel,
        out_shape=jax.ShapeDtypeStruct((tokens, width), bf16),
        in_specs=[pl.BlockSpec(memory_space=pl.ANY)] * len(inputs),
        out_specs=pl.BlockSpec(memory_space=pltpu.VMEM),
        scratch_shapes=held
        + [
            vmem((n_ctx, size, channels), bf16),
            vmem((n_ctx, heads, tokens), f32),
            vmem((size, channels), f32),
            vmem((tokens, channels), f32),
            vmem((n_ctx, tokens, channels), bf16),
            vmem((n_ctx, 2, groups, own_rows, cols), bf16),
            vmem((n_ctx, groups, own_rows, cols), bf16),
            vmem((n_ctx, groups, own_rows, cols), bf16),
            vmem((n_ctx, groups - 1, own_rows, cols), bf16),
            vmem((n_ctx, own_rows, cols), bf16),
            vmem((n_ctx, n_exp, n_ctx * own_rows, cols), bf16),
            vmem((SLOTS, TILE, TILE), bf16),
            vmem((n_rows, units), f32),
            vmem((n_rows, units), f32),
            vmem((n_rows, TILE), bf16),
            vmem((n_rows, units), bf16),
            vmem((groups, n_ctx, CAP, TILE), bf16),
            vmem((groups, n_ctx - 1, CAP, TILE), bf16),
            vmem((groups, 2, CAP, width), bf16),
            vmem((n_exp, CAP, width), bf16),
            vmem((n_ctx, 8, 128), f32),
            vmem((2, tokens, n_exp * CAP), bf16),
            dma((13,)),
            dma((n_ctx - 1, 2)),
            dma((n_ctx - 1, 2)),
            dma((4,)),
            dma((4,)),
            dma((n_ctx,)),
            dma((n_ctx,)),
            dma((n_ctx, groups - 1)),
            dma((n_ctx, groups - 1)),
            dma((n_ctx - 1,)),
            dma((n_ctx - 1,)),
            dma((SLOTS,)),
            dma((groups - 1,)),
            dma((groups - 1,)),
            dma((2, groups)),
            dma((2, groups)),
            dma((2, groups)),
            dma((2, groups)),
            dma((n_ctx, groups)),
            dma((n_ctx, groups)),
            dma((n_ctx - 1,)),
            dma((n_ctx - 1,)),
            dma((groups, n_ctx - 1)),
            dma((groups, n_ctx - 1)),
            dma((groups - 1, 2)),
            dma((groups - 1, 2)),
            dma,
            dma,
        ],
        compiler_params=pltpu.CompilerParams(
            collective_id=number, has_side_effects=True, vmem_limit_bytes=62 * 1024 * 1024
        ),
        cost_estimate=pl.CostEstimate(
            flops=6 * n_rows * n_ctx * TILE * units,
            bytes_accessed=6 * n_ctx * TILE * units,
            transcendentals=n_rows * units,
        ),
    )(*inputs)


def body(
    residual,
    ssm_input,
    ssm_gate,
    write_vectors,
    read_vectors,
    step_logits,
    decay_log,
    skip_gain,
    norm_gain,
    out_weight,
    moe_gain,
    gate_weight,
    up_weight,
    down_weight,
    expert_ids,
    route_weight,
):
    sizes = (lax.axis_size("ctx"), lax.axis_size("exp"), step_logits.shape[1], out_weight.shape[1])
    if sizes == (4, 8, SPAN, TILE) and gate_weight.shape[2] % TILE == 0:
        return layer(
            ssm_input,
            ssm_gate,
            write_vectors,
            read_vectors,
            step_logits,
            decay_log,
            skip_gain,
            norm_gain,
            residual,
            out_weight,
            expert_ids,
            route_weight,
            moe_gain,
            gate_weight,
            up_weight,
            down_weight,
            1,
        )
    heads_dev = step_logits.shape[0]
    tok_rows = step_logits.shape[1]
    head_width = ssm_input.shape[1] // heads_dev
    span_count = tok_rows // SPAN
    step_size = jax.nn.softplus(step_logits)
    log_step = step_size * (-jnp.exp(decay_log))[:, None]
    cumulative = jnp.einsum(
        "hks,st->hkt",
        log_step.reshape(heads_dev, span_count, SPAN),
        jnp.triu(jnp.ones((SPAN, SPAN), jnp.float32)),
        precision=lax.Precision.HIGHEST,
    )
    step_blocks = step_size.reshape(heads_dev, span_count, SPAN)
    input_blocks = ssm_input.reshape(span_count, SPAN, heads_dev, head_width)
    write_blocks = write_vectors.reshape(span_count, SPAN, -1)
    read_blocks = read_vectors.reshape(span_count, SPAN, -1)
    scores = jnp.einsum(
        "ktn,ksn->kts", read_blocks, write_blocks, preferred_element_type=jnp.float32
    )
    causal = jnp.arange(SPAN)[:, None] >= jnp.arange(SPAN)[None, :]
    log_gaps = cumulative[:, :, :, None] - cumulative[:, :, None, :]
    mixing = jnp.where(
        causal,
        scores[None] * jnp.exp(jnp.where(causal, log_gaps, 0.0)) * step_blocks[:, :, None, :],
        0.0,
    ).astype(jnp.bfloat16)
    intra_out = jnp.einsum(
        "hkts,kshp->kthp", mixing, input_blocks, preferred_element_type=jnp.float32
    )
    end_weight = jnp.exp(cumulative[:, :, -1:] - cumulative) * step_blocks
    loaded = (end_weight[:, :, :, None] * write_blocks.astype(jnp.float32)[None]).astype(
        jnp.bfloat16
    )
    block_state = jnp.einsum(
        "kshp,hksn->hkpn", input_blocks, loaded, preferred_element_type=jnp.float32
    )
    block_decay = jnp.exp(cumulative[:, :, -1])
    running = jnp.zeros_like(block_state[:, 0])
    decay_run = jnp.ones_like(block_decay[:, 0])
    entering_list = [running]
    reach_list = [decay_run]
    running = block_decay[:, 0, None, None] * running + block_state[:, 0]
    decay_run = decay_run * block_decay[:, 0]
    device_state = running
    device_decay = decay_run

    all_states, all_decays = sent(
        [
            device_state.astype(jnp.bfloat16),
            jnp.broadcast_to(device_decay[:, None], (heads_dev, 128)),
        ],
        "ctx",
        1,
        True,
    )
    ctx_index = lax.axis_index("ctx")
    device_in = jnp.zeros_like(device_state)
    for j in range(lax.axis_size("ctx") - 1):
        device_in = jnp.where(
            j < ctx_index,
            all_decays[j, :, :1, None] * device_in + all_states[j].astype(jnp.float32),
            device_in,
        )
    entering = jnp.stack(entering_list, axis=1)
    reach = jnp.stack(reach_list, axis=1)
    states = entering + reach[:, :, None, None] * device_in[:, None]
    inter_out = jnp.transpose(jnp.exp(cumulative), (1, 2, 0))[:, :, :, None] * jnp.einsum(
        "ktn,hkpn->kthp", read_blocks.astype(jnp.float32), states, precision=lax.Precision.HIGHEST
    )
    scan_out = (
        intra_out + inter_out + skip_gain[None, None, :, None] * input_blocks.astype(jnp.float32)
    )
    scan_out = scan_out.reshape(tok_rows, heads_dev * head_width)
    gated_out = scan_out * jax.nn.silu(ssm_gate.astype(jnp.float32))
    grouped = gated_out.reshape(tok_rows, -1, NORM_GROUP)
    group_scale = lax.rsqrt(jnp.mean(grouped * grouped, axis=2, keepdims=True) + EPSILON)
    normed = ((grouped * group_scale).reshape(tok_rows, -1) * norm_gain).astype(jnp.bfloat16)
    ctx_count = lax.axis_size("ctx")
    exp_count = lax.axis_size("exp")
    exp_index = lax.axis_index("exp")
    width = residual.shape[1]
    slice_width = width // exp_count
    split_count = exp_count // EXPERTS
    own_rows = tok_rows // exp_count
    normed_all = sent([normed], "ctx", 2, True)[0].reshape(ctx_count * tok_rows, -1)
    ssm_terms = jnp.dot(normed_all, out_weight, preferred_element_type=jnp.float32).astype(
        jnp.bfloat16
    )
    groups = exp_count // 2
    by_owner = jnp.transpose(
        ssm_terms.reshape(ctx_count, groups, 2, own_rows, -1), (2, 1, 0, 3, 4)
    ).reshape(2, groups * ctx_count * own_rows, -1)
    halves = pair_sum(by_owner, 3)
    chips = sent([halves.reshape(groups, ctx_count * own_rows, -1)], "exp", 4, False, 2)[0]
    ssm_part = jnp.sum(chips.astype(jnp.float32), axis=0).astype(jnp.bfloat16)
    ssm_rows = sent([ssm_part.reshape(ctx_count, own_rows, -1)], "ctx", 5, False)[0]
    ssm_rows = jnp.transpose(ssm_rows, (1, 0, 2)).reshape(own_rows, width)
    own_residual = lax.dynamic_slice_in_dim(residual, exp_index * own_rows, own_rows, 0)
    stream_rows = (own_residual.astype(jnp.float32) + ssm_rows.astype(jnp.float32)).astype(
        jnp.bfloat16
    )
    token_of_slot, pick_rank = slot_tables(expert_ids)
    stream_full = gather_pairs(stream_rows, "exp", 6).reshape(tok_rows, width)
    stream_slice = lax.dynamic_slice_in_dim(stream_full, exp_index * slice_width, slice_width, 1)
    padded = jnp.concatenate(
        [stream_full, jnp.zeros((1, stream_full.shape[1]), jnp.bfloat16)], axis=0
    )
    my_slots = lax.dynamic_index_in_dim(token_of_slot, exp_index // split_count, 0, keepdims=False)
    picked = normalize(jnp.take(padded, my_slots, axis=0), moe_gain)
    normed_rows = sent([picked], "ctx", 7, True)[0].reshape(ctx_count * CAP, width)
    terms = expert_terms(normed_rows, gate_weight[0], up_weight[0], down_weight[0])
    arrived_terms = sent([terms.reshape(ctx_count, CAP, width)], "ctx", 8, False)[0]
    sums_mine = jnp.sum(arrived_terms.astype(jnp.float32), axis=0).astype(jnp.bfloat16)
    by_slice = jnp.transpose(sums_mine.reshape(CAP, exp_count, slice_width), (1, 0, 2))
    arrived = sent([by_slice], "exp", 9, False)[0].reshape(exp_count * CAP, slice_width)
    piece_expert = jnp.arange(exp_count, dtype=jnp.int32) // split_count
    slot_range = jnp.arange(CAP, dtype=jnp.int32)
    moe_slice = jnp.zeros((tok_rows, slice_width), jnp.float32)
    for k in range(expert_ids.shape[1]):
        hit_expert = expert_ids[:, k, None] == piece_expert[None, :]
        hit_slot = pick_rank[:, k, None] == slot_range[None, :]
        hits = (hit_expert[:, :, None] & hit_slot[:, None, :]).astype(jnp.bfloat16)
        picked_out = jnp.dot(
            hits.reshape(tok_rows, exp_count * CAP), arrived, preferred_element_type=jnp.float32
        )
        moe_slice = moe_slice + route_weight[:, k, None] * picked_out
    return (stream_slice.astype(jnp.float32) + moe_slice).astype(jnp.bfloat16)


def solution(mesh):
    placed = (
        P("ctx", None),
        P("ctx", "exp"),
        P("ctx", "exp"),
        P("ctx", None),
        P("ctx", None),
        P("exp", "ctx"),
        P("exp"),
        P("exp"),
        P("exp"),
        P("exp", "ctx"),
        P(),
        P("exp", None, "ctx"),
        P("exp", None, "ctx"),
        P("exp", "ctx", None),
        P("ctx", None),
        P("ctx", None),
    )
    return jax.shard_map(
        body, mesh=mesh, in_specs=placed, out_specs=P("ctx", "exp"), check_vma=False
    )
```

```python
import functools
import math

import jax
import jax.numpy as jnp
from jax import lax
from jax.experimental import pallas as pl
from jax.experimental.pallas import tpu as pltpu
from jax.sharding import PartitionSpec as P

SPAN = 128
NORM_GROUP = 512
EXPERTS = 8
CAP = 64


EPSILON = 1e-05


MESH = pl.DeviceIdType.MESH


def send_kernel(axis, count, pair, spread, n_arrays, *refs):
    sources, targets = refs[:n_arrays], refs[n_arrays : 2 * n_arrays]
    local_sem, send_sem, recv_sem = refs[2 * n_arrays :]
    index = lax.axis_index(axis)
    group, lane = index // pair, lax.rem(index, pair)
    barrier = pltpu.get_barrier_semaphore()
    peers = [lax.rem(group + d, count) for d in range(1, count)]
    for peer in peers:
        pl.semaphore_signal(
            barrier, inc=1, device_id={axis: peer * pair + lane}, device_id_type=MESH
        )
    pl.semaphore_wait(barrier, count - 1)
    copies = []
    for d, peer in enumerate(peers):
        for i in range(n_arrays):
            copy = pltpu.make_async_remote_copy(
                src_ref=sources[i] if spread else sources[i].at[peer],
                dst_ref=targets[i].at[group],
                send_sem=send_sem.at[d, i],
                recv_sem=recv_sem.at[d, i],
                device_id={axis: peer * pair + lane},
                device_id_type=MESH,
            )
            copy.start()
            copies.append(copy)
    for i in range(n_arrays):
        own = pltpu.make_async_copy(
            sources[i] if spread else sources[i].at[group],
            targets[i].at[group],
            local_sem.at[i],
        )
        own.start()
        copies.append(own)
    for copy in copies:
        copy.wait()


def sent(arrays, axis, number, spread, pair=1):
    count = lax.axis_size(axis) // pair
    n_arrays = len(arrays)
    shapes = [
        jax.ShapeDtypeStruct((count,) + a.shape if spread else a.shape, a.dtype) for a in arrays
    ]
    size = sum(math.prod(shape.shape) * shape.dtype.itemsize for shape in shapes)
    return pl.pallas_call(
        functools.partial(send_kernel, axis, count, pair, spread, n_arrays),
        out_shape=shapes,
        in_specs=[pl.BlockSpec(memory_space=pl.ANY)] * n_arrays,
        out_specs=[pl.BlockSpec(memory_space=pl.ANY)] * n_arrays,
        scratch_shapes=[
            pltpu.SemaphoreType.DMA((n_arrays,)),
            pltpu.SemaphoreType.DMA((count - 1, n_arrays)),
            pltpu.SemaphoreType.DMA((count - 1, n_arrays)),
        ],
        compiler_params=pltpu.CompilerParams(collective_id=number, has_side_effects=True),
        cost_estimate=pl.CostEstimate(flops=0, bytes_accessed=2 * size, transcendentals=0),
    )(*arrays)


def gather_pairs_kernel(axis, groups, x_ref, out_ref, local_sem, send_sem, recv_sem, pass_send, pass_recv):
    index = lax.axis_index(axis)
    group, lane = index // 2, lax.rem(index, 2)
    sibling = group * 2 + 1 - lane
    barrier = pltpu.get_barrier_semaphore()
    peers = [lax.rem(group + d, groups) for d in range(1, groups)]
    for peer in [p * 2 + lane for p in peers] + [sibling]:
        pl.semaphore_signal(barrier, inc=1, device_id={axis: peer}, device_id_type=MESH)
    pl.semaphore_wait(barrier, groups)
    copies = []
    for d, peer in enumerate(peers):
        copy = pltpu.make_async_remote_copy(
            src_ref=x_ref,
            dst_ref=out_ref.at[index],
            send_sem=send_sem.at[d],
            recv_sem=recv_sem.at[d],
            device_id={axis: peer * 2 + lane},
            device_id_type=MESH,
        )
        copy.start()
        copies.append(copy)
    own = pltpu.make_async_copy(x_ref, out_ref.at[index], local_sem)
    own.start()
    passed = [
        pltpu.make_async_remote_copy(
            src_ref=x_ref,
            dst_ref=out_ref.at[index],
            send_sem=pass_send.at[0],
            recv_sem=pass_recv.at[0],
            device_id={axis: sibling},
            device_id_type=MESH,
        )
    ]
    passed[0].start()
    for d in range(1, groups):
        copies[d - 1].wait_recv()
        block = lax.rem(group + groups - d, groups) * 2 + lane
        copy = pltpu.make_async_remote_copy(
            src_ref=out_ref.at[block],
            dst_ref=out_ref.at[block],
            send_sem=pass_send.at[d],
            recv_sem=pass_recv.at[d],
            device_id={axis: sibling},
            device_id_type=MESH,
        )
        copy.start()
        passed.append(copy)
    for copy in copies:
        copy.wait_send()
    own.wait()
    for copy in passed:
        copy.wait()


def gather_pairs(x, axis, number):
    count = lax.axis_size(axis)
    return pl.pallas_call(
        functools.partial(gather_pairs_kernel, axis, count // 2),
        out_shape=jax.ShapeDtypeStruct((count,) + x.shape, x.dtype),
        in_specs=[pl.BlockSpec(memory_space=pl.ANY)],
        out_specs=pl.BlockSpec(memory_space=pl.ANY),
        scratch_shapes=[
            pltpu.SemaphoreType.DMA,
            pltpu.SemaphoreType.DMA((count // 2 - 1,)),
            pltpu.SemaphoreType.DMA((count // 2 - 1,)),
            pltpu.SemaphoreType.DMA((count // 2,)),
            pltpu.SemaphoreType.DMA((count // 2,)),
        ],
        compiler_params=pltpu.CompilerParams(collective_id=number, has_side_effects=True),
        cost_estimate=pl.CostEstimate(
            flops=0, bytes_accessed=2 * count * x.size * x.dtype.itemsize, transcendentals=0
        ),
    )(x)


def pair_sum(halves, number):
    lane = lax.rem(lax.axis_index("exp"), 2)
    both = pair_send(halves, number)
    own = lax.dynamic_index_in_dim(halves, lane, 0, keepdims=False)
    return (own.astype(jnp.float32) + both.astype(jnp.float32)).astype(jnp.bfloat16)


def pair_kernel(x_ref, out_ref, send_sem, recv_sem):
    index = lax.axis_index("exp")
    lane = lax.rem(index, 2)
    sibling = index + 1 - 2 * lane
    barrier = pltpu.get_barrier_semaphore()
    pl.semaphore_signal(barrier, inc=1, device_id={"exp": sibling}, device_id_type=MESH)
    pl.semaphore_wait(barrier, 1)
    copy = pltpu.make_async_remote_copy(
        src_ref=x_ref.at[1 - lane],
        dst_ref=out_ref,
        send_sem=send_sem,
        recv_sem=recv_sem,
        device_id={"exp": sibling},
        device_id_type=MESH,
    )
    copy.start()
    copy.wait()


def pair_send(halves, number):
    return pl.pallas_call(
        pair_kernel,
        out_shape=jax.ShapeDtypeStruct(halves.shape[1:], halves.dtype),
        in_specs=[pl.BlockSpec(memory_space=pl.ANY)],
        out_specs=pl.BlockSpec(memory_space=pl.ANY),
        scratch_shapes=[pltpu.SemaphoreType.DMA, pltpu.SemaphoreType.DMA],
        compiler_params=pltpu.CompilerParams(collective_id=number, has_side_effects=True),
        cost_estimate=pl.CostEstimate(
            flops=0, bytes_accessed=halves.size * 2, transcendentals=0
        ),
    )(halves)


def expert_kernel(x_ref, gate_ref, up_ref, down_ref, out_ref, total):
    step = pl.program_id(1)
    gate_val = jnp.dot(x_ref[...], gate_ref[...], preferred_element_type=jnp.float32)
    up_val = jnp.dot(x_ref[...], up_ref[...], preferred_element_type=jnp.float32)
    hidden = (gate_val / (1.0 + jnp.exp(-gate_val)) * up_val).astype(jnp.bfloat16)
    columns = down_ref.shape[1] // 4

    def add(first):
        for c in range(4):
            part = slice(c * columns, (c + 1) * columns)
            term = jnp.dot(hidden, down_ref[:, part], preferred_element_type=jnp.float32)
            total[:, part] = term if first else total[:, part] + term

    pl.when(step == 0)(lambda: add(True))
    pl.when(step > 0)(lambda: add(False))

    @pl.when(step == pl.num_programs(1) - 1)
    def _():
        out_ref[...] = total[...].astype(out_ref.dtype)


def expert_terms(rows, gate, up, down):
    count, width = rows.shape
    units = gate.shape[1]
    block = 256 if units % 256 == 0 else 128
    tall = 256 if count % 256 == 0 else count
    return pl.pallas_call(
        expert_kernel,
        out_shape=jax.ShapeDtypeStruct((count, width), jnp.bfloat16),
        grid=(count // tall, units // block),
        in_specs=[
            pl.BlockSpec((tall, width), lambda r, i: (r, 0)),
            pl.BlockSpec((width, block), lambda r, i: (0, i)),
            pl.BlockSpec((width, block), lambda r, i: (0, i)),
            pl.BlockSpec((block, width), lambda r, i: (i, 0)),
        ],
        out_specs=pl.BlockSpec((tall, width), lambda r, i: (r, 0)),
        scratch_shapes=[pltpu.VMEM((tall, width), jnp.float32)],
        compiler_params=pltpu.CompilerParams(vmem_limit_bytes=48 * 1024 * 1024),
        cost_estimate=pl.CostEstimate(
            flops=6 * count * width * units,
            bytes_accessed=6 * width * units,
            transcendentals=count * units,
        ),
    )(rows, gate, up, down)


def slot_tables(block_ids):
    expert_range = jnp.arange(EXPERTS, dtype=jnp.int32)
    hit_table = jnp.sum(
        (block_ids[:, :, None] == expert_range[None, None, :]).astype(jnp.int32), axis=1
    )
    lower = jnp.tril(jnp.ones((block_ids.shape[0],) * 2, jnp.bfloat16))
    ranking = (
        jnp.dot(lower, hit_table.astype(jnp.bfloat16), preferred_element_type=jnp.float32)
    ).astype(jnp.int32) - 1
    slot_range = jnp.arange(CAP, dtype=jnp.int32)
    matches = (hit_table.T[:, None, :] == 1) & (ranking.T[:, None, :] == slot_range[None, :, None])
    row_count = block_ids.shape[0]
    row_range = jnp.arange(row_count, dtype=jnp.int32)
    chosen = jnp.sum(jnp.where(matches, row_range[None, None, :], 0), axis=2)
    filled = jnp.any(matches, axis=2)
    token_of_slot = jnp.where(filled, chosen, row_count)
    pick_rank = jnp.take_along_axis(ranking, block_ids, axis=1)
    return (token_of_slot, pick_rank)


def normalize(stream_rows, moe_gain):
    values = stream_rows.astype(jnp.float32)
    scale_inv = lax.rsqrt(jnp.mean(values * values, axis=-1, keepdims=True) + EPSILON)
    return (values * scale_inv * moe_gain).astype(jnp.bfloat16)


def remote(src, dst, send_sem, recv_sem, device):
    return pltpu.make_async_remote_copy(
        src_ref=src,
        dst_ref=dst,
        send_sem=send_sem,
        recv_sem=recv_sem,
        device_id=device,
        device_id_type=MESH,
    )


def xor(a, s):
    low = lax.rem(a, 2)
    low = 1 - low if s % 2 else low
    high = a // 2
    high = 1 - high if s // 2 else high
    return high * 2 + low


TILE = 1024
SLOTS = 14


def layer_kernel(
    x_hbm,
    z_hbm,
    write_hbm,
    read_hbm,
    logit_hbm,
    decay_hbm,
    skip_hbm,
    norm_gain_hbm,
    residual_hbm,
    weight_hbm,
    ids_hbm,
    route_hbm,
    moe_gain_hbm,
    gate_hbm,
    up_hbm,
    down_hbm,
    out_ref,
    x_all,
    z_ref,
    write_all,
    read_ref,
    logit_all,
    decay_ref,
    skip_ref,
    norm_gain_ref,
    residual_ref,
    weight,
    ids_ref,
    route_ref,
    moe_gain_ref,
    weights_of,
    factor,
    entered,
    scan,
    normed,
    terms,
    paired,
    sums,
    arrived,
    rest,
    stream,
    tiles,
    gate_sum,
    up_sum,
    rows,
    hidden,
    term,
    came,
    relay,
    relayed,
    mine,
    outs,
    ids_all,
    combine,
    load_sem,
    state_send,
    state_recv,
    norm_send,
    norm_recv,
    pair_send_sem,
    pair_recv_sem,
    sum_send,
    sum_recv,
    rest_send,
    rest_recv,
    tile_sem,
    z_send,
    z_recv,
    xy_send,
    xy_recv,
    fwd_send,
    fwd_recv,
    pass_send,
    pass_recv,
    ids_send,
    ids_recv,
    term_send,
    term_recv,
    relay_send,
    relay_recv,
    out_send,
    out_recv,
    sib_send,
    sib_recv,
):
    f32, bf16 = jnp.float32, jnp.bfloat16
    n_ctx, n_exp = 4, 8
    groups = n_exp // 2
    ctx, e = lax.axis_index("ctx"), lax.axis_index("exp")
    group, lane = e // 2, lax.rem(e, 2)
    sibling = group * 2 + 1 - lane
    tokens, channels = x_all.shape[1:]
    heads = logit_all.shape[1]
    wide = 2 * (channels // heads)
    own_rows = tokens // n_exp
    cols = weight.shape[1]
    blocks = hidden.shape[1] // TILE
    n_rows = n_ctx * CAP
    others = [xor(ctx, s) for s in range(n_ctx)]
    chips = [lax.rem(group + d, groups) for d in range(groups)]

    back = [lax.rem(group + groups - d, groups) for d in range(groups)]
    turn = [lax.rem(group + 1 + i, groups) for i in range(groups)]
    barrier = pltpu.get_barrier_semaphore()
    peers = [{"ctx": others[s], "exp": e} for s in range(1, n_ctx)] + [
        {"ctx": ctx, "exp": lax.rem(e + d, n_exp)} for d in range(1, n_exp)
    ]
    for peer in peers:
        pl.semaphore_signal(barrier, inc=1, device_id=peer, device_id_type=MESH)

    loads = [
        pltpu.make_async_copy(src, dst, load_sem.at[i])
        for i, (src, dst) in enumerate(
            (
                (logit_hbm, logit_all.at[ctx]),
                (decay_hbm, decay_ref),
                (write_hbm, write_all.at[ctx]),
                (x_hbm, x_all.at[ctx]),
                (read_hbm, read_ref),
                (skip_hbm, skip_ref),
                (z_hbm, z_ref),
                (norm_gain_hbm, norm_gain_ref),
                (ids_hbm, ids_ref),
                (route_hbm, route_ref),
                (moe_gain_hbm, moe_gain_ref),
                (residual_hbm.at[pl.ds(pl.multiple_of(e * own_rows, 16), own_rows)], residual_ref),
                (weight_hbm, weight),
            )
        )
    ]
    for load in loads:
        load.start()

    order = [
        (kind, s, n) for s in range(n_ctx) for n in range(blocks) for kind in ("gate", "up")
    ] + [("down", m, f) for m in range(groups) for f in range(blocks)]

    def tile_copy(i):
        kind, outer, inner = order[i]
        fixed = pl.ds(inner * TILE, TILE)
        if kind == "down":
            moving = pl.ds(pl.multiple_of(turn[outer] * TILE, TILE), TILE)
            src = down_hbm.at[0, fixed, moving]
        else:
            moving = pl.ds(pl.multiple_of(others[outer] * TILE, TILE), TILE)
            src = (gate_hbm if kind == "gate" else up_hbm).at[0, moving, fixed]
        return pltpu.make_async_copy(src, tiles.at[i % SLOTS], tile_sem.at[i % SLOTS])

    def use_tile(i):
        tile_copy(i).wait()
        return tiles.at[i % SLOTS]

    def done_tile(i):
        if i + SLOTS < len(order):
            tile_copy(i + SLOTS).start()

    halves = [pl.ds(h * NORM_GROUP, NORM_GROUP) for h in range(2)]

    def block_copy(d, device_ctx, slot, i):
        src, dst = (
            (logit_hbm, logit_all.at[slot]),
            (write_hbm, write_all.at[slot]),
            (x_hbm.at[:, halves[0]], x_all.at[slot, :, halves[0]]),
            (x_hbm.at[:, halves[1]], x_all.at[slot, :, halves[1]]),
        )[i]
        return remote(
            src,
            dst,
            state_send.at[d - 1, i],
            state_recv.at[d - 1, i],
            {"ctx": device_ctx, "exp": e},
        )

    pl.semaphore_wait(barrier, len(peers))
    for some in ((0, 1, 2), (3,)):
        for d in range(1, n_ctx):

            @pl.when(ctx + d < n_ctx)
            def _(d=d, some=some):
                for i in some:
                    block_copy(d, ctx + d, ctx, i).start()

    for load in loads[:-1]:
        load.wait()

    x_ref = x_all.at[ctx]
    write_ref = write_all.at[ctx]
    diagonal = lax.broadcasted_iota(jnp.int32, (heads, heads), 0) == lax.broadcasted_iota(
        jnp.int32, (heads, heads), 1
    )

    def column(row):
        return jnp.sum(
            jnp.where(diagonal, jnp.broadcast_to(row, (heads, heads)), 0.0), axis=1, keepdims=True
        )

    head_of = lax.broadcasted_iota(jnp.int32, (heads, channels), 1) // (channels // heads)
    own_head = head_of == lax.broadcasted_iota(jnp.int32, (heads, channels), 0)

    def spread_row(col):
        return jnp.sum(
            jnp.where(own_head, jnp.broadcast_to(col, (heads, channels)), 0.0),
            axis=0,
            keepdims=True,
        )

    rate = -jnp.exp(column(decay_ref[...]))
    row_i = lax.broadcasted_iota(jnp.int32, (tokens, tokens), 0)
    col_i = lax.broadcasted_iota(jnp.int32, (tokens, tokens), 1)
    upper = (row_i <= col_i).astype(f32)

    def running(logits):
        step = jnp.maximum(logits, 0.0) + jnp.log1p(jnp.exp(-jnp.abs(logits)))
        total = jnp.dot(
            step * rate, upper, precision=lax.Precision.HIGHEST, preferred_element_type=f32
        )
        return step, total, total[:, tokens - 1 : tokens]

    step, cumulative, last = running(logit_all[ctx])
    stacked = jnp.concatenate(
        [cumulative, jnp.exp(cumulative), jnp.zeros((tokens - 2 * heads, tokens), f32)], axis=0
    ).T
    first_half = lax.broadcasted_iota(jnp.int32, (tokens, wide), 1) < wide // 2

    def pair_columns(table, first, q):
        return jnp.where(
            first_half,
            table[:, first + 2 * q : first + 2 * q + 1],
            table[:, first + 2 * q + 1 : first + 2 * q + 2],
        )

    rest_copies = [
        remote(
            residual_ref.at[:, pl.ds(pl.multiple_of(others[s] * cols, cols), cols)],
            rest.at[s],
            rest_send.at[s - 1],
            rest_recv.at[s - 1],
            {"ctx": others[s], "exp": e},
        )
        for s in range(1, n_ctx)
    ]
    for copy in rest_copies:
        copy.start()
    rest[0] = residual_ref[:, pl.ds(pl.multiple_of(ctx * cols, cols), cols)]

    for i in range(SLOTS):
        tile_copy(i).start()

    causal = row_i >= col_i
    scores = lax.dot_general(
        read_ref[...], write_ref[...], (((1,), (1,)), ((), ())), preferred_element_type=f32
    )
    for q in range(heads // 2):
        part = slice(q * wide, (q + 1) * wide)
        x_pair = x_ref[:, part]
        pair_outs = []
        for h in (2 * q, 2 * q + 1):
            gap = stacked[:, h : h + 1] - cumulative[h : h + 1, :]
            decayed = jnp.exp(jnp.where(causal, gap, 0.0)) * step[h : h + 1, :]
            mixing = jnp.where(causal, scores * decayed, 0.0).astype(bf16)
            pair_outs.append(jnp.dot(mixing, x_pair, preferred_element_type=f32))
        scan[:, part] = jnp.where(first_half, pair_outs[0], pair_outs[1])

    entered[...] = jnp.zeros_like(entered)
    factor[...] = jnp.ones_like(factor)
    for d in range(1, n_ctx):

        @pl.when(ctx >= d)
        def _(d=d):
            block_copy(d, ctx, ctx - d, 0).wait_recv()
            steps, total, end = running(logit_all[ctx - d])
            weight_rows = jnp.exp(end - total) * steps * factor[...]
            factor[...] = factor[...] * jnp.exp(end)
            weights_of[d - 1] = jnp.concatenate(
                [weight_rows, jnp.zeros((tokens - heads, tokens), f32)], axis=0
            ).T

    def norm_copy(s, source, h, number):
        where = normed.at[source, :, pl.ds(h * NORM_GROUP, NORM_GROUP)]
        return remote(
            where, where, norm_send.at[number], norm_recv.at[number], {"ctx": others[s], "exp": e}
        )

    reads = read_ref[...]
    skip = spread_row(column(skip_ref[...]))
    for n in range(channels // NORM_GROUP):
        pairs = range(n * NORM_GROUP // wide, (n + 1) * NORM_GROUP // wide)
        for d in range(1, n_ctx):

            @pl.when(ctx >= d)
            def _(d=d, n=n, pairs=pairs):
                if n == 0:
                    block_copy(d, ctx, ctx - d, 1).wait_recv()
                block_copy(d, ctx, ctx - d, 2 + n).wait_recv()
                table = weights_of[d - 1]
                write_t = write_all[ctx - d].astype(f32).T.astype(bf16)
                for q in pairs:
                    part = slice(q * wide, (q + 1) * wide)
                    weighted = pair_columns(table, 0, q) * x_all[ctx - d, :, part].astype(f32)
                    entered[:, part] += jnp.dot(
                        write_t, weighted.astype(bf16), preferred_element_type=f32
                    )

        for q in pairs:
            part = slice(q * wide, (q + 1) * wide)
            state = entered[:, part]
            high = state.astype(bf16)
            low = (state - high.astype(f32)).astype(bf16)
            inter = jnp.dot(reads, high, preferred_element_type=f32) + jnp.dot(
                reads, low, preferred_element_type=f32
            )
            value = (
                scan[:, part]
                + pair_columns(stacked, heads, q) * inter
                + skip[:, part] * x_ref[:, part].astype(f32)
            )
            gate = z_ref[:, part].astype(f32)
            scan[:, part] = value * (gate / (1.0 + jnp.exp(-gate)))
        part = slice(n * NORM_GROUP, (n + 1) * NORM_GROUP)
        value = scan[:, part]
        scale = lax.rsqrt(jnp.mean(value * value, axis=1, keepdims=True) + EPSILON)
        normed[ctx, :, part] = (value * scale * norm_gain_ref[:, part]).astype(bf16)
        norm_copy(1, ctx, n, n).start()
        norm_copy(2, ctx, n, 2 + n).start()
    loads[-1].wait()

    def project(s):
        value = jnp.dot(
            normed[others[s]], weight[...], preferred_element_type=f32
        ).astype(bf16)
        for owner in range(n_exp):
            terms[s, owner % 2, owner // 2] = value[owner * own_rows : (owner + 1) * own_rows]

    def pair_copy(s):
        return remote(
            terms.at[s, 1 - lane],
            paired.at[s],
            pair_send_sem.at[s],
            pair_recv_sem.at[s],
            {"ctx": ctx, "exp": sibling},
        )

    def sum_copy(s, d):
        return remote(
            sums.at[s, chips[d]],
            arrived.at[s, d - 1],
            sum_send.at[s, d - 1],
            sum_recv.at[s, d - 1],
            {"ctx": ctx, "exp": chips[d] * 2 + lane},
        )

    def add_pair(s):
        pair_copy(s).wait_recv()
        sums[s] = (terms[s, lane].astype(f32) + paired[s].astype(f32)).astype(bf16)
        for d in range(1, groups):
            sum_copy(s, d).start()

    ids_rows = [jnp.broadcast_to(ids_ref[k : k + 1, :].astype(f32), (CAP, tokens)) for k in range(2)]
    ids_all[ctx] = jnp.where(row_i[:8] == 0, ids_rows[0][:8], ids_rows[1][:8])

    near = lax.rem(group, 3) > 0
    mate = group + 1 - 2 * lax.rem(group, 2)
    across = 2 - group // 2
    beyond = 3 * across - 3
    number_here = jnp.where(near, 1, 2)

    def z_copy(s, number):
        where = stream.at[ctx, s, group, lane]
        return remote(
            where,
            where,
            z_send.at[s, number],
            z_recv.at[s, 0 if number == 0 else number_here],
            {"ctx": ctx, "exp": (mate if number == 0 else across) * 2 + lane},
        )

    def z_pass(s, number):
        where = stream.at[ctx, s, across if number == 1 else beyond, lane]
        return remote(
            where,
            where,
            z_send.at[s, 1 + number],
            z_recv.at[s, number],
            {"ctx": ctx, "exp": mate * 2 + lane},
        )

    def xy_copy(to, s, source):
        where = stream.at[source, s, :, lane]
        return remote(
            where,
            where,
            xy_send.at[to - 1, s],
            xy_recv.at[to - 1, s],
            {"ctx": others[to], "exp": e},
        )

    half = cols // 2

    def fwd_copy(to, s, source):
        where = stream.at[source, s, :, lane, :, pl.ds((2 - to) * half, half)]
        return remote(
            where,
            where,
            fwd_send.at[to - 1, s],
            fwd_recv.at[to - 1, s],
            {"ctx": others[to], "exp": e},
        )

    def pass_copy(k, s, which=None):
        where = stream.at[others[k], s, :, lane if which is None else which]
        return remote(
            where, where, pass_send.at[k, s], pass_recv.at[k, s], {"ctx": ctx, "exp": sibling}
        )

    def ids_copy(s, source):
        where = ids_all.at[source]
        return remote(
            where, where, ids_send.at[s - 1], ids_recv.at[s - 1], {"ctx": others[s], "exp": e}
        )

    def gathered(s):
        for number in (1, 2):
            z_pass(s, number).wait_recv()

            @pl.when(near)
            def _(number=number):
                z_pass(s, number).start()

        z_copy(s, 0).wait_recv()
        for to in (1, 2):
            xy_copy(to, s, ctx).start()
        pass_copy(0, s).start()

    def forward(s):
        xy_copy(1, s, others[1]).wait_recv()
        fwd_copy(2, s, others[1]).start()
        pass_copy(1, s).start()
        xy_copy(2, s, others[2]).wait_recv()
        fwd_copy(1, s, others[2]).start()
        pass_copy(2, s).start()

    def diagonal_came(s):
        fwd_copy(1, s, others[3]).wait_recv()
        fwd_copy(2, s, others[3]).wait_recv()
        pass_copy(3, s).start()

    def sum_stage(s):
        total = sums[s, group].astype(f32)
        for d in range(1, groups):
            sum_copy(s, d).wait_recv()
            total = total + arrived[s, d - 1].astype(f32)
        total = total.astype(bf16).astype(f32) + rest[s].astype(f32)
        stream[ctx, s, group, lane] = total.astype(bf16)
        for number in range(2):
            z_copy(s, number).start()

    def norm_came(number):
        to = 1 + number // 2
        norm_copy(to, others[to], number % 2, number).wait_recv()

    project(0)
    pair_copy(0).start()
    for copy in rest_copies:
        copy.wait_recv()
    for s in range(1, n_ctx):
        ids_copy(s, ctx).start()
    add_pair(0)
    norm_came(0)
    norm_copy(2, others[1], 0, 4).start()
    norm_came(3)
    norm_copy(1, others[2], 1, 5).start()
    sum_stage(0)
    norm_came(1)
    project(1)
    pair_copy(1).start()
    norm_came(2)
    project(2)
    pair_copy(2).start()
    add_pair(1)
    add_pair(2)
    norm_copy(2, others[3], 0, 4).wait_recv()
    norm_copy(1, others[3], 1, 5).wait_recv()
    project(3)
    pair_copy(3).start()
    add_pair(3)

    upper = upper.astype(bf16)
    slot_i = lax.broadcasted_iota(jnp.int32, (CAP, 128), 0).astype(f32)

    def slots_of(first, second, expert):
        hit = jnp.where((first == expert) | (second == expert), 1.0, 0.0)
        rank = jnp.dot(hit.astype(bf16), upper, preferred_element_type=f32) - 1.0
        return jnp.where((hit > 0.0) & (rank == slot_i), 1.0, 0.0)

    own_ids = ids_rows
    own_route = [jnp.broadcast_to(route_ref[k : k + 1, :], (CAP, tokens)) for k in range(2)]
    for pair in range(n_exp // 2):
        both = []
        for x in (2 * pair, 2 * pair + 1):
            weight = jnp.where(own_ids[0] == float(x), own_route[0], own_route[1])
            both.append(slots_of(own_ids[0], own_ids[1], float(x)) * weight)
        back_table = jnp.concatenate(both, axis=0).T
        high = back_table.astype(bf16)
        part = slice(pair * 128, (pair + 1) * 128)
        combine[0, :, part] = high
        combine[1, :, part] = (back_table - high.astype(f32)).astype(bf16)

    for s in range(1, n_ctx):
        ids_copy(s, others[s]).wait_recv()
    my_expert = e.astype(f32)
    picks = []
    for j in range(n_ctx):
        first = jnp.broadcast_to(ids_all[j][0:1], (CAP, 128))
        second = jnp.broadcast_to(ids_all[j][1:2], (CAP, 128))
        picks.append(slots_of(first, second, my_expert).astype(bf16))

    gathered(0)
    sum_stage(1)
    sum_stage(2)
    forward(0)
    sum_stage(3)
    gathered(1)
    diagonal_came(0)
    forward(1)
    gathered(2)
    diagonal_came(1)
    forward(2)
    gathered(3)
    squares = jnp.zeros((n_rows, 1), f32)
    own = own_rows

    for s in range(n_ctx):
        if s == 1:
            forward(3)
            diagonal_came(2)
        if s == 2:
            diagonal_came(3)
        for stage in range(n_ctx):
            pass_copy(s, stage, 1 - lane).wait_recv()
        source = others[s]
        added = []
        gain = moe_gain_ref[:, pl.ds(pl.multiple_of(source * TILE, TILE), TILE)]
        for j in range(n_ctx):
            dense = stream[source, xor(source, j)].reshape(n_exp * own, TILE)
            picked = jnp.dot(picks[j], dense, preferred_element_type=f32)
            added.append(jnp.sum(picked * picked, axis=1, keepdims=True))
            rows[j * CAP : (j + 1) * CAP, :] = (picked * gain).astype(bf16)
        squares = squares + jnp.concatenate(added, axis=0)
        if s == n_ctx - 1:
            scale = lax.rsqrt(squares / float(n_ctx * TILE) + EPSILON)
        for n in range(blocks):
            to = slice(n * TILE, (n + 1) * TILE)
            for kind, total in (("gate", gate_sum), ("up", up_sum)):
                number = order.index((kind, s, n))
                tile = use_tile(number)
                value = jnp.dot(rows[...], tile[...], preferred_element_type=f32)
                done_tile(number)
                if s == 0:
                    total[:, to] = value
                elif s < n_ctx - 1 or kind == "gate":
                    total[:, to] = total[:, to] + value
                else:
                    gate = gate_sum[:, to] * scale
                    up = (total[:, to] + value) * scale
                    hidden[:, to] = (gate / (1.0 + jnp.exp(-gate)) * up).astype(bf16)

    def term_copy(i, to, far):
        h = to - 1
        return remote(
            term.at[i, h, others[3] if far else others[to]],
            came.at[i, h, far],
            term_send.at[i, h, far],
            term_recv.at[i, h, far],
            {"ctx": others[to], "exp": e},
        )

    def relay_copy(i, h):
        return remote(
            relay.at[i, h],
            relayed.at[i, h],
            relay_send.at[i, h],
            relay_recv.at[i, h],
            {"ctx": others[2 - h], "exp": e},
        )

    def relay_on(i):
        for h in range(2):
            term_copy(i, h + 1, 1).wait_recv()
            relay[i, h] = (
                term[i, h, others[2 - h]].astype(f32) + came[i, h, 1].astype(f32)
            ).astype(bf16)
            relay_copy(i, h).start()

    width = TILE // 2

    def out_copy(i, to, number):
        return remote(
            mine.at[i, to],
            outs.at[e],
            out_send.at[i, to],
            out_recv.at[i, number],
            {"ctx": ctx, "exp": turn[i] * 2 + to},
        )

    def sib_copy():
        return remote(
            mine.at[groups - 1, 1 - lane],
            outs.at[e],
            sib_send,
            sib_recv,
            {"ctx": ctx, "exp": sibling},
        )

    def reduce(i):
        for h in range(2):
            term_copy(i, h + 1, 0).wait_recv()
            relay_copy(i, h).wait_recv()
            mine[i, h] = (
                term[i, h, ctx].astype(f32)
                + came[i, h, 0].astype(f32)
                + relayed[i, h].astype(f32)
            ).astype(bf16)
        if i < groups - 1:
            for to in range(2):
                out_copy(i, to, lane).start()
        else:
            sib_copy().start()
            outs[e] = mine[i, lane]

    for i in range(groups):
        value = None
        for f in range(blocks):
            tile = use_tile(order.index(("down", i, f)))
            more = jnp.dot(
                hidden[:, f * TILE : (f + 1) * TILE], tile[...], preferred_element_type=f32
            )
            value = more if value is None else value + more
        for j in range(n_ctx):
            for h in range(2):
                term[i, h, j] = value[j * CAP : (j + 1) * CAP, h * width : (h + 1) * width].astype(
                    bf16
                )
        for f in range(blocks):
            done_tile(order.index(("down", i, f)))
        for far in (1, 0):
            for to in (1, 2):
                term_copy(i, to, far).start()
        if i > 0:
            relay_on(i - 1)
        if i > 1:
            reduce(i - 2)
    relay_on(groups - 1)
    reduce(groups - 2)
    reduce(groups - 1)

    for i in range(groups - 1):
        for number in range(2):
            out_copy(i, 0, number).wait_recv()
    sib_copy().wait_recv()
    lot = outs[...].reshape(n_exp * CAP, width)
    value = jnp.dot(combine[0], lot, preferred_element_type=f32) + jnp.dot(
        combine[1], lot, preferred_element_type=f32
    )
    stage = lax.rem(lax.rem(group, 2) + lax.rem(ctx, 2), 2) + 2 * lax.rem(
        group // 2 + ctx // 2, 2
    )
    base = stream[
        group, stage, :, :, :, pl.ds(pl.multiple_of(lane * width, 128), width)
    ].reshape(n_exp * own, width)
    out_ref[...] = (base.astype(f32) + value).astype(bf16)

    for s in range(1, n_ctx):
        ids_copy(s, ctx).wait_send()
    for i in range(groups):
        for to in (1, 2):
            for far in range(2):
                term_copy(i, to, far).wait_send()
            relay_copy(i, to - 1).wait_send()
    for s in range(n_ctx):
        for number in range(2):
            z_copy(s, number).wait_send()

        @pl.when(near)
        def _(s=s):
            for number in (1, 2):
                z_pass(s, number).wait_send()

        for to in (1, 2):
            xy_copy(to, s, ctx).wait_send()
            fwd_copy(to, s, others[3 - to]).wait_send()
        for k in range(n_ctx):
            pass_copy(k, s).wait_send()
    for i in range(groups - 1):
        for to in range(2):
            out_copy(i, to, lane).wait_send()
    sib_copy().wait_send()


    for number in range(4):
        norm_copy(1 + number // 2, ctx, number % 2, number).wait_send()
    norm_copy(2, others[1], 0, 4).wait_send()
    norm_copy(1, others[2], 1, 5).wait_send()
    for copy in rest_copies:
        copy.wait_send()
    for s in range(n_ctx):
        pair_copy(s).wait_send()
        for d in range(1, groups):
            sum_copy(s, d).wait_send()
    for d in range(1, n_ctx):

        @pl.when(ctx + d < n_ctx)
        def _(d=d):
            for i in range(4):
                block_copy(d, ctx + d, ctx, i).wait_send()


def layer(
    x, z, write, read, logits, decay_log, skip_gain, norm_gain, residual, out_weight, ids, route,
    moe_gain, gate, up, down, number,
):
    n_ctx, n_exp = lax.axis_size("ctx"), lax.axis_size("exp")
    tokens, channels = x.shape
    heads = logits.shape[0]
    cols = out_weight.shape[1]
    own_rows = tokens // n_exp
    groups = n_exp // 2
    units = gate.shape[2]
    width = cols // 2
    n_rows = n_ctx * CAP
    size = write.shape[1]
    f32, bf16, dma = jnp.float32, jnp.bfloat16, pltpu.SemaphoreType.DMA
    vmem = pltpu.VMEM
    inputs = (
        x,
        z,
        write,
        read,
        logits,
        decay_log.reshape(1, -1),
        skip_gain.reshape(1, -1),
        norm_gain.reshape(1, -1),
        residual,
        out_weight,
        ids.T,
        route.T,
        moe_gain.reshape(1, -1),
        gate,
        up,
        down,
    )
    held = [vmem(a.shape, a.dtype) for a in inputs[:13]]
    for i in (0, 2, 4):
        held[i] = vmem((n_ctx,) + inputs[i].shape, inputs[i].dtype)
    held[8] = vmem((own_rows, residual.shape[1]), bf16)
    return pl.pallas_call(
        layer_kernel,
        out_shape=jax.ShapeDtypeStruct((tokens, width), bf16),
        in_specs=[pl.BlockSpec(memory_space=pl.ANY)] * len(inputs),
        out_specs=pl.BlockSpec(memory_space=pltpu.VMEM),
        scratch_shapes=held
        + [
            vmem((n_ctx - 1, tokens, 128), f32),
            vmem((heads, tokens), f32),
            vmem((size, channels), f32),
            vmem((tokens, channels), f32),
            vmem((n_ctx, tokens, channels), bf16),
            vmem((n_ctx, 2, groups, own_rows, cols), bf16),
            vmem((n_ctx, groups, own_rows, cols), bf16),
            vmem((n_ctx, groups, own_rows, cols), bf16),
            vmem((n_ctx, groups - 1, own_rows, cols), bf16),
            vmem((n_ctx, own_rows, cols), bf16),
            vmem((n_ctx, n_ctx, groups, 2, own_rows, cols), bf16),
            vmem((SLOTS, TILE, TILE), bf16),
            vmem((n_rows, units), f32),
            vmem((n_rows, units), f32),
            vmem((n_rows, TILE), bf16),
            vmem((n_rows, units), bf16),
            vmem((groups, 2, n_ctx, CAP, width), bf16),
            vmem((groups, 2, 2, CAP, width), bf16),
            vmem((groups, 2, CAP, width), bf16),
            vmem((groups, 2, CAP, width), bf16),
            vmem((groups, 2, CAP, width), bf16),
            vmem((n_exp, CAP, width), bf16),
            vmem((n_ctx, 8, 128), f32),
            vmem((2, tokens, n_exp * CAP), bf16),
            dma((13,)),
            dma((n_ctx - 1, 4)),
            dma((n_ctx - 1, 4)),
            dma((6,)),
            dma((6,)),
            dma((n_ctx,)),
            dma((n_ctx,)),
            dma((n_ctx, groups - 1)),
            dma((n_ctx, groups - 1)),
            dma((n_ctx - 1,)),
            dma((n_ctx - 1,)),
            dma((SLOTS,)),
            dma((n_ctx, 4)),
            dma((n_ctx, 3)),
            dma((2, n_ctx)),
            dma((2, n_ctx)),
            dma((2, n_ctx)),
            dma((2, n_ctx)),
            dma((n_ctx, n_ctx)),
            dma((n_ctx, n_ctx)),
            dma((n_ctx - 1,)),
            dma((n_ctx - 1,)),
            dma((groups, 2, 2)),
            dma((groups, 2, 2)),
            dma((groups, 2)),
            dma((groups, 2)),
            dma((groups - 1, 2)),
            dma((groups - 1, 2)),
            dma,
            dma,
        ],
        compiler_params=pltpu.CompilerParams(
            collective_id=number, has_side_effects=True, vmem_limit_bytes=63 * 1024 * 1024
        ),
        cost_estimate=pl.CostEstimate(
            flops=6 * n_rows * n_ctx * TILE * units,
            bytes_accessed=6 * n_ctx * TILE * units,
            transcendentals=n_rows * units,
        ),
    )(*inputs)


def body(
    residual,
    ssm_input,
    ssm_gate,
    write_vectors,
    read_vectors,
    step_logits,
    decay_log,
    skip_gain,
    norm_gain,
    out_weight,
    moe_gain,
    gate_weight,
    up_weight,
    down_weight,
    expert_ids,
    route_weight,
):
    sizes = (lax.axis_size("ctx"), lax.axis_size("exp"), step_logits.shape[1], out_weight.shape[1])
    if sizes == (4, 8, SPAN, TILE) and gate_weight.shape[2] % TILE == 0:
        return layer(
            ssm_input,
            ssm_gate,
            write_vectors,
            read_vectors,
            step_logits,
            decay_log,
            skip_gain,
            norm_gain,
            residual,
            out_weight,
            expert_ids,
            route_weight,
            moe_gain,
            gate_weight,
            up_weight,
            down_weight,
            1,
        )
    heads_dev = step_logits.shape[0]
    tok_rows = step_logits.shape[1]
    head_width = ssm_input.shape[1] // heads_dev
    span_count = tok_rows // SPAN
    step_size = jax.nn.softplus(step_logits)
    log_step = step_size * (-jnp.exp(decay_log))[:, None]
    cumulative = jnp.einsum(
        "hks,st->hkt",
        log_step.reshape(heads_dev, span_count, SPAN),
        jnp.triu(jnp.ones((SPAN, SPAN), jnp.float32)),
        precision=lax.Precision.HIGHEST,
    )
    step_blocks = step_size.reshape(heads_dev, span_count, SPAN)
    input_blocks = ssm_input.reshape(span_count, SPAN, heads_dev, head_width)
    write_blocks = write_vectors.reshape(span_count, SPAN, -1)
    read_blocks = read_vectors.reshape(span_count, SPAN, -1)
    scores = jnp.einsum(
        "ktn,ksn->kts", read_blocks, write_blocks, preferred_element_type=jnp.float32
    )
    causal = jnp.arange(SPAN)[:, None] >= jnp.arange(SPAN)[None, :]
    log_gaps = cumulative[:, :, :, None] - cumulative[:, :, None, :]
    mixing = jnp.where(
        causal,
        scores[None] * jnp.exp(jnp.where(causal, log_gaps, 0.0)) * step_blocks[:, :, None, :],
        0.0,
    ).astype(jnp.bfloat16)
    intra_out = jnp.einsum(
        "hkts,kshp->kthp", mixing, input_blocks, preferred_element_type=jnp.float32
    )
    end_weight = jnp.exp(cumulative[:, :, -1:] - cumulative) * step_blocks
    loaded = (end_weight[:, :, :, None] * write_blocks.astype(jnp.float32)[None]).astype(
        jnp.bfloat16
    )
    block_state = jnp.einsum(
        "kshp,hksn->hkpn", input_blocks, loaded, preferred_element_type=jnp.float32
    )
    block_decay = jnp.exp(cumulative[:, :, -1])
    running = jnp.zeros_like(block_state[:, 0])
    decay_run = jnp.ones_like(block_decay[:, 0])
    entering_list = [running]
    reach_list = [decay_run]
    running = block_decay[:, 0, None, None] * running + block_state[:, 0]
    decay_run = decay_run * block_decay[:, 0]
    device_state = running
    device_decay = decay_run

    all_states, all_decays = sent(
        [
            device_state.astype(jnp.bfloat16),
            jnp.broadcast_to(device_decay[:, None], (heads_dev, 128)),
        ],
        "ctx",
        1,
        True,
    )
    ctx_index = lax.axis_index("ctx")
    device_in = jnp.zeros_like(device_state)
    for j in range(lax.axis_size("ctx") - 1):
        device_in = jnp.where(
            j < ctx_index,
            all_decays[j, :, :1, None] * device_in + all_states[j].astype(jnp.float32),
            device_in,
        )
    entering = jnp.stack(entering_list, axis=1)
    reach = jnp.stack(reach_list, axis=1)
    states = entering + reach[:, :, None, None] * device_in[:, None]
    inter_out = jnp.transpose(jnp.exp(cumulative), (1, 2, 0))[:, :, :, None] * jnp.einsum(
        "ktn,hkpn->kthp", read_blocks.astype(jnp.float32), states, precision=lax.Precision.HIGHEST
    )
    scan_out = (
        intra_out + inter_out + skip_gain[None, None, :, None] * input_blocks.astype(jnp.float32)
    )
    scan_out = scan_out.reshape(tok_rows, heads_dev * head_width)
    gated_out = scan_out * jax.nn.silu(ssm_gate.astype(jnp.float32))
    grouped = gated_out.reshape(tok_rows, -1, NORM_GROUP)
    group_scale = lax.rsqrt(jnp.mean(grouped * grouped, axis=2, keepdims=True) + EPSILON)
    normed = ((grouped * group_scale).reshape(tok_rows, -1) * norm_gain).astype(jnp.bfloat16)
    ctx_count = lax.axis_size("ctx")
    exp_count = lax.axis_size("exp")
    exp_index = lax.axis_index("exp")
    width = residual.shape[1]
    slice_width = width // exp_count
    split_count = exp_count // EXPERTS
    own_rows = tok_rows // exp_count
    normed_all = sent([normed], "ctx", 2, True)[0].reshape(ctx_count * tok_rows, -1)
    ssm_terms = jnp.dot(normed_all, out_weight, preferred_element_type=jnp.float32).astype(
        jnp.bfloat16
    )
    groups = exp_count // 2
    by_owner = jnp.transpose(
        ssm_terms.reshape(ctx_count, groups, 2, own_rows, -1), (2, 1, 0, 3, 4)
    ).reshape(2, groups * ctx_count * own_rows, -1)
    halves = pair_sum(by_owner, 3)
    chips = sent([halves.reshape(groups, ctx_count * own_rows, -1)], "exp", 4, False, 2)[0]
    ssm_part = jnp.sum(chips.astype(jnp.float32), axis=0).astype(jnp.bfloat16)
    ssm_rows = sent([ssm_part.reshape(ctx_count, own_rows, -1)], "ctx", 5, False)[0]
    ssm_rows = jnp.transpose(ssm_rows, (1, 0, 2)).reshape(own_rows, width)
    own_residual = lax.dynamic_slice_in_dim(residual, exp_index * own_rows, own_rows, 0)
    stream_rows = (own_residual.astype(jnp.float32) + ssm_rows.astype(jnp.float32)).astype(
        jnp.bfloat16
    )
    token_of_slot, pick_rank = slot_tables(expert_ids)
    stream_full = gather_pairs(stream_rows, "exp", 6).reshape(tok_rows, width)
    stream_slice = lax.dynamic_slice_in_dim(stream_full, exp_index * slice_width, slice_width, 1)
    padded = jnp.concatenate(
        [stream_full, jnp.zeros((1, stream_full.shape[1]), jnp.bfloat16)], axis=0
    )
    my_slots = lax.dynamic_index_in_dim(token_of_slot, exp_index // split_count, 0, keepdims=False)
    picked = normalize(jnp.take(padded, my_slots, axis=0), moe_gain)
    normed_rows = sent([picked], "ctx", 7, True)[0].reshape(ctx_count * CAP, width)
    terms = expert_terms(normed_rows, gate_weight[0], up_weight[0], down_weight[0])
    arrived_terms = sent([terms.reshape(ctx_count, CAP, width)], "ctx", 8, False)[0]
    sums_mine = jnp.sum(arrived_terms.astype(jnp.float32), axis=0).astype(jnp.bfloat16)
    by_slice = jnp.transpose(sums_mine.reshape(CAP, exp_count, slice_width), (1, 0, 2))
    arrived = sent([by_slice], "exp", 9, False)[0].reshape(exp_count * CAP, slice_width)
    piece_expert = jnp.arange(exp_count, dtype=jnp.int32) // split_count
    slot_range = jnp.arange(CAP, dtype=jnp.int32)
    moe_slice = jnp.zeros((tok_rows, slice_width), jnp.float32)
    for k in range(expert_ids.shape[1]):
        hit_expert = expert_ids[:, k, None] == piece_expert[None, :]
        hit_slot = pick_rank[:, k, None] == slot_range[None, :]
        hits = (hit_expert[:, :, None] & hit_slot[:, None, :]).astype(jnp.bfloat16)
        picked_out = jnp.dot(
            hits.reshape(tok_rows, exp_count * CAP), arrived, preferred_element_type=jnp.float32
        )
        moe_slice = moe_slice + route_weight[:, k, None] * picked_out
    return (stream_slice.astype(jnp.float32) + moe_slice).astype(jnp.bfloat16)


def solution(mesh):
    placed = (
        P("ctx", None),
        P("ctx", "exp"),
        P("ctx", "exp"),
        P("ctx", None),
        P("ctx", None),
        P("exp", "ctx"),
        P("exp"),
        P("exp"),
        P("exp"),
        P("exp", "ctx"),
        P(),
        P("exp", None, "ctx"),
        P("exp", None, "ctx"),
        P("exp", "ctx", None),
        P("ctx", None),
        P("ctx", None),
    )
    return jax.shard_map(
        body, mesh=mesh, in_specs=placed, out_specs=P("ctx", "exp"), check_vma=False
    )
```

```python
import functools
import math

import jax
import jax.numpy as jnp
from jax import lax
from jax.experimental import pallas as pl
from jax.experimental.pallas import tpu as pltpu
from jax.sharding import PartitionSpec as P

SPAN = 128
NORM_GROUP = 512
EXPERTS = 8
CAP = 64


EPSILON = 1e-05


MESH = pl.DeviceIdType.MESH


def send_kernel(axis, count, pair, spread, n_arrays, *refs):
    sources, targets = refs[:n_arrays], refs[n_arrays : 2 * n_arrays]
    local_sem, send_sem, recv_sem = refs[2 * n_arrays :]
    index = lax.axis_index(axis)
    group, lane = index // pair, lax.rem(index, pair)
    barrier = pltpu.get_barrier_semaphore()
    peers = [lax.rem(group + d, count) for d in range(1, count)]
    for peer in peers:
        pl.semaphore_signal(
            barrier, inc=1, device_id={axis: peer * pair + lane}, device_id_type=MESH
        )
    pl.semaphore_wait(barrier, count - 1)
    copies = []
    for d, peer in enumerate(peers):
        for i in range(n_arrays):
            copy = pltpu.make_async_remote_copy(
                src_ref=sources[i] if spread else sources[i].at[peer],
                dst_ref=targets[i].at[group],
                send_sem=send_sem.at[d, i],
                recv_sem=recv_sem.at[d, i],
                device_id={axis: peer * pair + lane},
                device_id_type=MESH,
            )
            copy.start()
            copies.append(copy)
    for i in range(n_arrays):
        own = pltpu.make_async_copy(
            sources[i] if spread else sources[i].at[group],
            targets[i].at[group],
            local_sem.at[i],
        )
        own.start()
        copies.append(own)
    for copy in copies:
        copy.wait()


def sent(arrays, axis, number, spread, pair=1):
    count = lax.axis_size(axis) // pair
    n_arrays = len(arrays)
    shapes = [
        jax.ShapeDtypeStruct((count,) + a.shape if spread else a.shape, a.dtype) for a in arrays
    ]
    size = sum(math.prod(shape.shape) * shape.dtype.itemsize for shape in shapes)
    return pl.pallas_call(
        functools.partial(send_kernel, axis, count, pair, spread, n_arrays),
        out_shape=shapes,
        in_specs=[pl.BlockSpec(memory_space=pl.ANY)] * n_arrays,
        out_specs=[pl.BlockSpec(memory_space=pl.ANY)] * n_arrays,
        scratch_shapes=[
            pltpu.SemaphoreType.DMA((n_arrays,)),
            pltpu.SemaphoreType.DMA((count - 1, n_arrays)),
            pltpu.SemaphoreType.DMA((count - 1, n_arrays)),
        ],
        compiler_params=pltpu.CompilerParams(collective_id=number, has_side_effects=True),
        cost_estimate=pl.CostEstimate(flops=0, bytes_accessed=2 * size, transcendentals=0),
    )(*arrays)


def gather_pairs_kernel(axis, groups, x_ref, out_ref, local_sem, send_sem, recv_sem, pass_send, pass_recv):
    index = lax.axis_index(axis)
    group, lane = index // 2, lax.rem(index, 2)
    sibling = group * 2 + 1 - lane
    barrier = pltpu.get_barrier_semaphore()
    peers = [lax.rem(group + d, groups) for d in range(1, groups)]
    for peer in [p * 2 + lane for p in peers] + [sibling]:
        pl.semaphore_signal(barrier, inc=1, device_id={axis: peer}, device_id_type=MESH)
    pl.semaphore_wait(barrier, groups)
    copies = []
    for d, peer in enumerate(peers):
        copy = pltpu.make_async_remote_copy(
            src_ref=x_ref,
            dst_ref=out_ref.at[index],
            send_sem=send_sem.at[d],
            recv_sem=recv_sem.at[d],
            device_id={axis: peer * 2 + lane},
            device_id_type=MESH,
        )
        copy.start()
        copies.append(copy)
    own = pltpu.make_async_copy(x_ref, out_ref.at[index], local_sem)
    own.start()
    passed = [
        pltpu.make_async_remote_copy(
            src_ref=x_ref,
            dst_ref=out_ref.at[index],
            send_sem=pass_send.at[0],
            recv_sem=pass_recv.at[0],
            device_id={axis: sibling},
            device_id_type=MESH,
        )
    ]
    passed[0].start()
    for d in range(1, groups):
        copies[d - 1].wait_recv()
        block = lax.rem(group + groups - d, groups) * 2 + lane
        copy = pltpu.make_async_remote_copy(
            src_ref=out_ref.at[block],
            dst_ref=out_ref.at[block],
            send_sem=pass_send.at[d],
            recv_sem=pass_recv.at[d],
            device_id={axis: sibling},
            device_id_type=MESH,
        )
        copy.start()
        passed.append(copy)
    for copy in copies:
        copy.wait_send()
    own.wait()
    for copy in passed:
        copy.wait()


def gather_pairs(x, axis, number):
    count = lax.axis_size(axis)
    return pl.pallas_call(
        functools.partial(gather_pairs_kernel, axis, count // 2),
        out_shape=jax.ShapeDtypeStruct((count,) + x.shape, x.dtype),
        in_specs=[pl.BlockSpec(memory_space=pl.ANY)],
        out_specs=pl.BlockSpec(memory_space=pl.ANY),
        scratch_shapes=[
            pltpu.SemaphoreType.DMA,
            pltpu.SemaphoreType.DMA((count // 2 - 1,)),
            pltpu.SemaphoreType.DMA((count // 2 - 1,)),
            pltpu.SemaphoreType.DMA((count // 2,)),
            pltpu.SemaphoreType.DMA((count // 2,)),
        ],
        compiler_params=pltpu.CompilerParams(collective_id=number, has_side_effects=True),
        cost_estimate=pl.CostEstimate(
            flops=0, bytes_accessed=2 * count * x.size * x.dtype.itemsize, transcendentals=0
        ),
    )(x)


def pair_sum(halves, number):
    lane = lax.rem(lax.axis_index("exp"), 2)
    both = pair_send(halves, number)
    own = lax.dynamic_index_in_dim(halves, lane, 0, keepdims=False)
    return (own.astype(jnp.float32) + both.astype(jnp.float32)).astype(jnp.bfloat16)


def pair_kernel(x_ref, out_ref, send_sem, recv_sem):
    index = lax.axis_index("exp")
    lane = lax.rem(index, 2)
    sibling = index + 1 - 2 * lane
    barrier = pltpu.get_barrier_semaphore()
    pl.semaphore_signal(barrier, inc=1, device_id={"exp": sibling}, device_id_type=MESH)
    pl.semaphore_wait(barrier, 1)
    copy = pltpu.make_async_remote_copy(
        src_ref=x_ref.at[1 - lane],
        dst_ref=out_ref,
        send_sem=send_sem,
        recv_sem=recv_sem,
        device_id={"exp": sibling},
        device_id_type=MESH,
    )
    copy.start()
    copy.wait()


def pair_send(halves, number):
    return pl.pallas_call(
        pair_kernel,
        out_shape=jax.ShapeDtypeStruct(halves.shape[1:], halves.dtype),
        in_specs=[pl.BlockSpec(memory_space=pl.ANY)],
        out_specs=pl.BlockSpec(memory_space=pl.ANY),
        scratch_shapes=[pltpu.SemaphoreType.DMA, pltpu.SemaphoreType.DMA],
        compiler_params=pltpu.CompilerParams(collective_id=number, has_side_effects=True),
        cost_estimate=pl.CostEstimate(
            flops=0, bytes_accessed=halves.size * 2, transcendentals=0
        ),
    )(halves)


def expert_kernel(x_ref, gate_ref, up_ref, down_ref, out_ref, total):
    step = pl.program_id(1)
    gate_val = jnp.dot(x_ref[...], gate_ref[...], preferred_element_type=jnp.float32)
    up_val = jnp.dot(x_ref[...], up_ref[...], preferred_element_type=jnp.float32)
    hidden = (gate_val / (1.0 + jnp.exp(-gate_val)) * up_val).astype(jnp.bfloat16)
    columns = down_ref.shape[1] // 4

    def add(first):
        for c in range(4):
            part = slice(c * columns, (c + 1) * columns)
            term = jnp.dot(hidden, down_ref[:, part], preferred_element_type=jnp.float32)
            total[:, part] = term if first else total[:, part] + term

    pl.when(step == 0)(lambda: add(True))
    pl.when(step > 0)(lambda: add(False))

    @pl.when(step == pl.num_programs(1) - 1)
    def _():
        out_ref[...] = total[...].astype(out_ref.dtype)


def expert_terms(rows, gate, up, down):
    count, width = rows.shape
    units = gate.shape[1]
    block = 256 if units % 256 == 0 else 128
    tall = 256 if count % 256 == 0 else count
    return pl.pallas_call(
        expert_kernel,
        out_shape=jax.ShapeDtypeStruct((count, width), jnp.bfloat16),
        grid=(count // tall, units // block),
        in_specs=[
            pl.BlockSpec((tall, width), lambda r, i: (r, 0)),
            pl.BlockSpec((width, block), lambda r, i: (0, i)),
            pl.BlockSpec((width, block), lambda r, i: (0, i)),
            pl.BlockSpec((block, width), lambda r, i: (i, 0)),
        ],
        out_specs=pl.BlockSpec((tall, width), lambda r, i: (r, 0)),
        scratch_shapes=[pltpu.VMEM((tall, width), jnp.float32)],
        compiler_params=pltpu.CompilerParams(vmem_limit_bytes=48 * 1024 * 1024),
        cost_estimate=pl.CostEstimate(
            flops=6 * count * width * units,
            bytes_accessed=6 * width * units,
            transcendentals=count * units,
        ),
    )(rows, gate, up, down)


def slot_tables(block_ids):
    expert_range = jnp.arange(EXPERTS, dtype=jnp.int32)
    hit_table = jnp.sum(
        (block_ids[:, :, None] == expert_range[None, None, :]).astype(jnp.int32), axis=1
    )
    lower = jnp.tril(jnp.ones((block_ids.shape[0],) * 2, jnp.bfloat16))
    ranking = (
        jnp.dot(lower, hit_table.astype(jnp.bfloat16), preferred_element_type=jnp.float32)
    ).astype(jnp.int32) - 1
    slot_range = jnp.arange(CAP, dtype=jnp.int32)
    matches = (hit_table.T[:, None, :] == 1) & (ranking.T[:, None, :] == slot_range[None, :, None])
    row_count = block_ids.shape[0]
    row_range = jnp.arange(row_count, dtype=jnp.int32)
    chosen = jnp.sum(jnp.where(matches, row_range[None, None, :], 0), axis=2)
    filled = jnp.any(matches, axis=2)
    token_of_slot = jnp.where(filled, chosen, row_count)
    pick_rank = jnp.take_along_axis(ranking, block_ids, axis=1)
    return (token_of_slot, pick_rank)


def normalize(stream_rows, moe_gain):
    values = stream_rows.astype(jnp.float32)
    scale_inv = lax.rsqrt(jnp.mean(values * values, axis=-1, keepdims=True) + EPSILON)
    return (values * scale_inv * moe_gain).astype(jnp.bfloat16)


def remote(src, dst, send_sem, recv_sem, device):
    return pltpu.make_async_remote_copy(
        src_ref=src,
        dst_ref=dst,
        send_sem=send_sem,
        recv_sem=recv_sem,
        device_id=device,
        device_id_type=MESH,
    )


def xor(a, s):
    low = lax.rem(a, 2)
    low = 1 - low if s % 2 else low
    high = a // 2
    high = 1 - high if s // 2 else high
    return high * 2 + low


TILE = 1024
SLOTS = 14


def layer_kernel(
    x_hbm,
    z_hbm,
    write_hbm,
    read_hbm,
    logit_hbm,
    decay_hbm,
    skip_hbm,
    norm_gain_hbm,
    residual_hbm,
    weight_hbm,
    ids_hbm,
    route_hbm,
    moe_gain_hbm,
    gate_hbm,
    up_hbm,
    down_hbm,
    out_ref,
    x_all,
    z_ref,
    write_all,
    read_ref,
    logit_all,
    decay_ref,
    skip_ref,
    norm_gain_ref,
    residual_ref,
    weight,
    ids_ref,
    route_ref,
    moe_gain_ref,
    weights_of,
    factor,
    entered,
    scan,
    normed,
    terms,
    paired,
    sums,
    arrived,
    rest,
    stream,
    tiles,
    gate_sum,
    up_sum,
    rows,
    hidden,
    term,
    came,
    relay,
    relayed,
    mine,
    outs,
    ids_all,
    combine,
    load_sem,
    state_send,
    state_recv,
    norm_send,
    norm_recv,
    pair_send_sem,
    pair_recv_sem,
    sum_send,
    sum_recv,
    rest_send,
    rest_recv,
    tile_sem,
    z_send,
    z_recv,
    xy_send,
    xy_recv,
    fwd_send,
    fwd_recv,
    pass_send,
    pass_recv,
    ids_send,
    ids_recv,
    term_send,
    term_recv,
    relay_send,
    relay_recv,
    out_send,
    out_recv,
    sib_send,
    sib_recv,
):
    f32, bf16 = jnp.float32, jnp.bfloat16
    n_ctx, n_exp = 4, 8
    groups = n_exp // 2
    ctx, e = lax.axis_index("ctx"), lax.axis_index("exp")
    group, lane = e // 2, lax.rem(e, 2)
    sibling = group * 2 + 1 - lane
    tokens, channels = x_all.shape[1:]
    heads = logit_all.shape[1]
    wide = 2 * (channels // heads)
    own_rows = tokens // n_exp
    cols = weight.shape[1]
    blocks = hidden.shape[1] // TILE
    n_rows = n_ctx * CAP
    others = [xor(ctx, s) for s in range(n_ctx)]
    chips = [lax.rem(group + d, groups) for d in range(groups)]

    back = [lax.rem(group + groups - d, groups) for d in range(groups)]
    turn = [lax.rem(group + 1 + i, groups) for i in range(groups)]
    barrier = pltpu.get_barrier_semaphore()
    peers = [{"ctx": others[s], "exp": e} for s in range(1, n_ctx)] + [
        {"ctx": ctx, "exp": lax.rem(e + d, n_exp)} for d in range(1, n_exp)
    ]
    for peer in peers:
        pl.semaphore_signal(barrier, inc=1, device_id=peer, device_id_type=MESH)

    loads = [
        pltpu.make_async_copy(src, dst, load_sem.at[i])
        for i, (src, dst) in enumerate(
            (
                (logit_hbm, logit_all.at[ctx]),
                (decay_hbm, decay_ref),
                (write_hbm, write_all.at[ctx]),
                (x_hbm, x_all.at[ctx]),
                (read_hbm, read_ref),
                (skip_hbm, skip_ref),
                (z_hbm, z_ref),
                (norm_gain_hbm, norm_gain_ref),
                (ids_hbm, ids_ref),
                (route_hbm, route_ref),
                (moe_gain_hbm, moe_gain_ref),
                (residual_hbm.at[pl.ds(pl.multiple_of(e * own_rows, 16), own_rows)], residual_ref),
                (weight_hbm, weight),
            )
        )
    ]
    for load in loads:
        load.start()

    order = [
        (kind, s, n) for s in range(n_ctx) for n in range(blocks) for kind in ("gate", "up")
    ] + [("down", m, f) for m in range(groups) for f in range(blocks)]

    def tile_copy(i):
        kind, outer, inner = order[i]
        fixed = pl.ds(inner * TILE, TILE)
        if kind == "down":
            moving = pl.ds(pl.multiple_of(turn[outer] * TILE, TILE), TILE)
            src = down_hbm.at[0, fixed, moving]
        else:
            moving = pl.ds(pl.multiple_of(others[outer] * TILE, TILE), TILE)
            src = (gate_hbm if kind == "gate" else up_hbm).at[0, moving, fixed]
        return pltpu.make_async_copy(src, tiles.at[i % SLOTS], tile_sem.at[i % SLOTS])

    def use_tile(i):
        tile_copy(i).wait()
        return tiles.at[i % SLOTS]

    def done_tile(i):
        if i + SLOTS < len(order):
            tile_copy(i + SLOTS).start()

    halves = [pl.ds(h * NORM_GROUP, NORM_GROUP) for h in range(2)]

    def block_copy(d, device_ctx, slot, i):
        src, dst = (
            (logit_hbm, logit_all.at[slot]),
            (write_hbm, write_all.at[slot]),
            (x_hbm.at[:, halves[0]], x_all.at[slot, :, halves[0]]),
            (x_hbm.at[:, halves[1]], x_all.at[slot, :, halves[1]]),
        )[i]
        return remote(
            src,
            dst,
            state_send.at[d - 1, i],
            state_recv.at[d - 1, i],
            {"ctx": device_ctx, "exp": e},
        )

    pl.semaphore_wait(barrier, len(peers))
    for some in ((0, 1, 2), (3,)):
        for d in range(1, n_ctx):

            @pl.when(ctx + d < n_ctx)
            def _(d=d, some=some):
                for i in some:
                    block_copy(d, ctx + d, ctx, i).start()

    for load in loads[:-1]:
        load.wait()

    x_ref = x_all.at[ctx]
    write_ref = write_all.at[ctx]
    diagonal = lax.broadcasted_iota(jnp.int32, (heads, heads), 0) == lax.broadcasted_iota(
        jnp.int32, (heads, heads), 1
    )

    def column(row):
        return jnp.sum(
            jnp.where(diagonal, jnp.broadcast_to(row, (heads, heads)), 0.0), axis=1, keepdims=True
        )

    head_of = lax.broadcasted_iota(jnp.int32, (heads, channels), 1) // (channels // heads)
    own_head = head_of == lax.broadcasted_iota(jnp.int32, (heads, channels), 0)

    def spread_row(col):
        return jnp.sum(
            jnp.where(own_head, jnp.broadcast_to(col, (heads, channels)), 0.0),
            axis=0,
            keepdims=True,
        )

    rate = -jnp.exp(column(decay_ref[...]))
    row_i = lax.broadcasted_iota(jnp.int32, (tokens, tokens), 0)
    col_i = lax.broadcasted_iota(jnp.int32, (tokens, tokens), 1)
    upper = (row_i <= col_i).astype(f32)

    def running(logits):
        step = jnp.maximum(logits, 0.0) + jnp.log1p(jnp.exp(-jnp.abs(logits)))
        total = jnp.dot(
            step * rate, upper, precision=lax.Precision.HIGHEST, preferred_element_type=f32
        )
        return step, total, total[:, tokens - 1 : tokens]

    step, cumulative, last = running(logit_all[ctx])
    stacked = jnp.concatenate(
        [cumulative, jnp.exp(cumulative), jnp.zeros((tokens - 2 * heads, tokens), f32)], axis=0
    ).T
    first_half = lax.broadcasted_iota(jnp.int32, (tokens, wide), 1) < wide // 2

    def pair_columns(table, first, q):
        return jnp.where(
            first_half,
            table[:, first + 2 * q : first + 2 * q + 1],
            table[:, first + 2 * q + 1 : first + 2 * q + 2],
        )

    rest_copies = [
        remote(
            residual_ref.at[:, pl.ds(pl.multiple_of(others[s] * cols, cols), cols)],
            rest.at[s],
            rest_send.at[s - 1],
            rest_recv.at[s - 1],
            {"ctx": others[s], "exp": e},
        )
        for s in range(1, n_ctx)
    ]
    for copy in rest_copies:
        copy.start()
    rest[0] = residual_ref[:, pl.ds(pl.multiple_of(ctx * cols, cols), cols)]

    for i in range(SLOTS):
        tile_copy(i).start()

    causal = row_i >= col_i
    scores = lax.dot_general(
        read_ref[...], write_ref[...], (((1,), (1,)), ((), ())), preferred_element_type=f32
    )
    for q in range(heads // 2):
        part = slice(q * wide, (q + 1) * wide)
        x_pair = x_ref[:, part]
        pair_outs = []
        for h in (2 * q, 2 * q + 1):
            gap = stacked[:, h : h + 1] - cumulative[h : h + 1, :]
            decayed = jnp.exp(jnp.where(causal, gap, 0.0)) * step[h : h + 1, :]
            mixing = jnp.where(causal, scores * decayed, 0.0).astype(bf16)
            pair_outs.append(jnp.dot(mixing, x_pair, preferred_element_type=f32))
        scan[:, part] = jnp.where(first_half, pair_outs[0], pair_outs[1])

    entered[...] = jnp.zeros_like(entered)
    factor[...] = jnp.ones_like(factor)
    for d in range(1, n_ctx):

        @pl.when(ctx >= d)
        def _(d=d):
            block_copy(d, ctx, ctx - d, 0).wait_recv()
            steps, total, end = running(logit_all[ctx - d])
            weight_rows = jnp.exp(end - total) * steps * factor[...]
            factor[...] = factor[...] * jnp.exp(end)
            weights_of[d - 1] = jnp.concatenate(
                [weight_rows, jnp.zeros((tokens - heads, tokens), f32)], axis=0
            ).T

    def norm_copy(s, source, h, number):
        where = normed.at[source, :, pl.ds(h * NORM_GROUP, NORM_GROUP)]
        return remote(
            where, where, norm_send.at[number], norm_recv.at[number], {"ctx": others[s], "exp": e}
        )

    reads = read_ref[...]
    skip = spread_row(column(skip_ref[...]))
    for n in range(channels // NORM_GROUP):
        pairs = range(n * NORM_GROUP // wide, (n + 1) * NORM_GROUP // wide)
        for d in range(1, n_ctx):

            @pl.when(ctx >= d)
            def _(d=d, n=n, pairs=pairs):
                if n == 0:
                    block_copy(d, ctx, ctx - d, 1).wait_recv()
                block_copy(d, ctx, ctx - d, 2 + n).wait_recv()
                table = weights_of[d - 1]
                write_t = write_all[ctx - d].astype(f32).T.astype(bf16)
                for q in pairs:
                    part = slice(q * wide, (q + 1) * wide)
                    weighted = pair_columns(table, 0, q) * x_all[ctx - d, :, part].astype(f32)
                    entered[:, part] += jnp.dot(
                        write_t, weighted.astype(bf16), preferred_element_type=f32
                    )

        for q in pairs:
            part = slice(q * wide, (q + 1) * wide)
            state = entered[:, part]
            high = state.astype(bf16)
            low = (state - high.astype(f32)).astype(bf16)
            inter = jnp.dot(reads, high, preferred_element_type=f32) + jnp.dot(
                reads, low, preferred_element_type=f32
            )
            value = (
                scan[:, part]
                + pair_columns(stacked, heads, q) * inter
                + skip[:, part] * x_ref[:, part].astype(f32)
            )
            gate = z_ref[:, part].astype(f32)
            scan[:, part] = value * (gate / (1.0 + jnp.exp(-gate)))
        part = slice(n * NORM_GROUP, (n + 1) * NORM_GROUP)
        value = scan[:, part]
        scale = lax.rsqrt(jnp.mean(value * value, axis=1, keepdims=True) + EPSILON)
        normed[ctx, :, part] = (value * scale * norm_gain_ref[:, part]).astype(bf16)
        norm_copy(1, ctx, n, n).start()
        norm_copy(2, ctx, n, 2 + n).start()
    loads[-1].wait()

    def project(s):
        value = jnp.dot(
            normed[others[s]], weight[...], preferred_element_type=f32
        ).astype(bf16)
        for owner in range(n_exp):
            terms[s, owner % 2, owner // 2] = value[owner * own_rows : (owner + 1) * own_rows]

    def pair_copy(s):
        return remote(
            terms.at[s, 1 - lane],
            paired.at[s],
            pair_send_sem.at[s],
            pair_recv_sem.at[s],
            {"ctx": ctx, "exp": sibling},
        )

    def sum_copy(s, d):
        return remote(
            sums.at[s, chips[d]],
            arrived.at[s, d - 1],
            sum_send.at[s, d - 1],
            sum_recv.at[s, d - 1],
            {"ctx": ctx, "exp": chips[d] * 2 + lane},
        )

    def add_pair(s):
        pair_copy(s).wait_recv()
        sums[s] = (terms[s, lane].astype(f32) + paired[s].astype(f32)).astype(bf16)
        for d in range(1, groups):
            sum_copy(s, d).start()

    ids_rows = [jnp.broadcast_to(ids_ref[k : k + 1, :].astype(f32), (CAP, tokens)) for k in range(2)]
    ids_all[ctx] = jnp.where(row_i[:8] == 0, ids_rows[0][:8], ids_rows[1][:8])

    near = lax.rem(group, 3) > 0
    mate = group + 1 - 2 * lax.rem(group, 2)
    across = 2 - group // 2
    beyond = 3 * across - 3
    number_here = jnp.where(near, 1, 2)

    def z_copy(s, number):
        where = stream.at[ctx, s, group, lane]
        return remote(
            where,
            where,
            z_send.at[s, number],
            z_recv.at[s, 0 if number == 0 else number_here],
            {"ctx": ctx, "exp": (mate if number == 0 else across) * 2 + lane},
        )

    def z_pass(s, number):
        where = stream.at[ctx, s, across if number == 1 else beyond, lane]
        return remote(
            where,
            where,
            z_send.at[s, 1 + number],
            z_recv.at[s, number],
            {"ctx": ctx, "exp": mate * 2 + lane},
        )

    def xy_copy(to, s, source):
        where = stream.at[source, s, :, lane]
        return remote(
            where,
            where,
            xy_send.at[to - 1, s],
            xy_recv.at[to - 1, s],
            {"ctx": others[to], "exp": e},
        )

    half = cols // 2

    def fwd_copy(to, s, source):
        where = stream.at[source, s, :, lane, :, pl.ds((2 - to) * half, half)]
        return remote(
            where,
            where,
            fwd_send.at[to - 1, s],
            fwd_recv.at[to - 1, s],
            {"ctx": others[to], "exp": e},
        )

    def pass_copy(k, s, which=None):
        where = stream.at[others[k], s, :, lane if which is None else which]
        return remote(
            where, where, pass_send.at[k, s], pass_recv.at[k, s], {"ctx": ctx, "exp": sibling}
        )

    def ids_copy(s, source):
        where = ids_all.at[source]
        return remote(
            where, where, ids_send.at[s - 1], ids_recv.at[s - 1], {"ctx": others[s], "exp": e}
        )

    def gathered(s):
        for number in (1, 2):
            z_pass(s, number).wait_recv()

            @pl.when(near)
            def _(number=number):
                z_pass(s, number).start()

        z_copy(s, 0).wait_recv()
        for to in (1, 2):
            xy_copy(to, s, ctx).start()
        pass_copy(0, s).start()

    def forward(s):
        xy_copy(1, s, others[1]).wait_recv()
        fwd_copy(2, s, others[1]).start()
        pass_copy(1, s).start()
        xy_copy(2, s, others[2]).wait_recv()
        fwd_copy(1, s, others[2]).start()
        pass_copy(2, s).start()

    def diagonal_came(s):
        fwd_copy(1, s, others[3]).wait_recv()
        fwd_copy(2, s, others[3]).wait_recv()
        pass_copy(3, s).start()

    def sum_stage(s):
        total = sums[s, group].astype(f32)
        for d in range(1, groups):
            sum_copy(s, d).wait_recv()
            total = total + arrived[s, d - 1].astype(f32)
        total = total.astype(bf16).astype(f32) + rest[s].astype(f32)
        stream[ctx, s, group, lane] = total.astype(bf16)
        for number in range(2):
            z_copy(s, number).start()

    def norm_came(number):
        to = 1 + number // 2
        norm_copy(to, others[to], number % 2, number).wait_recv()

    project(0)
    pair_copy(0).start()
    for copy in rest_copies:
        copy.wait_recv()
    for s in range(1, n_ctx):
        ids_copy(s, ctx).start()
    add_pair(0)
    norm_came(0)
    norm_copy(2, others[1], 0, 4).start()
    norm_came(3)
    norm_copy(1, others[2], 1, 5).start()
    sum_stage(0)
    norm_came(1)
    project(1)
    pair_copy(1).start()
    norm_came(2)
    project(2)
    pair_copy(2).start()
    add_pair(1)
    add_pair(2)
    norm_copy(2, others[3], 0, 4).wait_recv()
    norm_copy(1, others[3], 1, 5).wait_recv()
    project(3)
    pair_copy(3).start()
    add_pair(3)

    upper = upper.astype(bf16)
    slot_i = lax.broadcasted_iota(jnp.int32, (CAP, 128), 0).astype(f32)

    def slots_of(first, second, expert):
        hit = jnp.where((first == expert) | (second == expert), 1.0, 0.0)
        rank = jnp.dot(hit.astype(bf16), upper, preferred_element_type=f32) - 1.0
        return jnp.where((hit > 0.0) & (rank == slot_i), 1.0, 0.0)

    own_ids = ids_rows
    own_route = [jnp.broadcast_to(route_ref[k : k + 1, :], (CAP, tokens)) for k in range(2)]
    for pair in range(n_exp // 2):
        both = []
        for x in (2 * pair, 2 * pair + 1):
            weight = jnp.where(own_ids[0] == float(x), own_route[0], own_route[1])
            both.append(slots_of(own_ids[0], own_ids[1], float(x)) * weight)
        back_table = jnp.concatenate(both, axis=0).T
        high = back_table.astype(bf16)
        part = slice(pair * 128, (pair + 1) * 128)
        combine[0, :, part] = high
        combine[1, :, part] = (back_table - high.astype(f32)).astype(bf16)

    for s in range(1, n_ctx):
        ids_copy(s, others[s]).wait_recv()
    my_expert = e.astype(f32)
    picks = []
    for j in range(n_ctx):
        first = jnp.broadcast_to(ids_all[j][0:1], (CAP, 128))
        second = jnp.broadcast_to(ids_all[j][1:2], (CAP, 128))
        picks.append(slots_of(first, second, my_expert).astype(bf16))

    gathered(0)
    sum_stage(1)
    sum_stage(2)
    forward(0)
    sum_stage(3)
    gathered(1)
    diagonal_came(0)
    forward(1)
    gathered(2)
    diagonal_came(1)
    forward(2)
    gathered(3)
    squares = jnp.zeros((n_rows, 1), f32)
    own = own_rows

    for s in range(n_ctx):
        if s == 1:
            forward(3)
            diagonal_came(2)
        if s == 2:
            diagonal_came(3)
        for stage in range(n_ctx):
            pass_copy(s, stage, 1 - lane).wait_recv()
        source = others[s]
        added = []
        gain = moe_gain_ref[:, pl.ds(pl.multiple_of(source * TILE, TILE), TILE)]
        for j in range(n_ctx):
            dense = stream[source, xor(source, j)].reshape(n_exp * own, TILE)
            picked = jnp.dot(picks[j], dense, preferred_element_type=f32)
            added.append(jnp.sum(picked * picked, axis=1, keepdims=True))
            rows[j * CAP : (j + 1) * CAP, :] = (picked * gain).astype(bf16)
        squares = squares + jnp.concatenate(added, axis=0)
        if s == n_ctx - 1:
            scale = lax.rsqrt(squares / float(n_ctx * TILE) + EPSILON)
        for n in range(blocks):
            to = slice(n * TILE, (n + 1) * TILE)
            for kind, total in (("gate", gate_sum), ("up", up_sum)):
                number = order.index((kind, s, n))
                tile = use_tile(number)
                value = jnp.dot(rows[...], tile[...], preferred_element_type=f32)
                done_tile(number)
                if s == 0:
                    total[:, to] = value
                elif s < n_ctx - 1 or kind == "gate":
                    total[:, to] = total[:, to] + value
                else:
                    gate = gate_sum[:, to] * scale
                    up = (total[:, to] + value) * scale
                    hidden[:, to] = (gate / (1.0 + jnp.exp(-gate)) * up).astype(bf16)

    def term_copy(i, to, far):
        h = to - 1
        return remote(
            term.at[i, h, others[3] if far else others[to]],
            came.at[i, h, far],
            term_send.at[i, h, far],
            term_recv.at[i, h, far],
            {"ctx": others[to], "exp": e},
        )

    def relay_copy(i, h):
        return remote(
            relay.at[i, h],
            relayed.at[i, h],
            relay_send.at[i, h],
            relay_recv.at[i, h],
            {"ctx": others[2 - h], "exp": e},
        )

    def relay_on(i):
        for h in range(2):
            term_copy(i, h + 1, 1).wait_recv()
            relay[i, h] = (
                term[i, h, others[2 - h]].astype(f32) + came[i, h, 1].astype(f32)
            ).astype(bf16)
            relay_copy(i, h).start()

    width = TILE // 2

    def out_copy(i, to, number):
        return remote(
            mine.at[i, to],
            outs.at[e],
            out_send.at[i, to],
            out_recv.at[i, number],
            {"ctx": ctx, "exp": turn[i] * 2 + to},
        )

    def sib_copy():
        return remote(
            mine.at[groups - 1, 1 - lane],
            outs.at[e],
            sib_send,
            sib_recv,
            {"ctx": ctx, "exp": sibling},
        )

    def reduce(i):
        for h in range(2):
            term_copy(i, h + 1, 0).wait_recv()
            relay_copy(i, h).wait_recv()
            mine[i, h] = (
                term[i, h, ctx].astype(f32)
                + came[i, h, 0].astype(f32)
                + relayed[i, h].astype(f32)
            ).astype(bf16)
        if i < groups - 1:
            for to in range(2):
                out_copy(i, to, lane).start()
        else:
            sib_copy().start()
            outs[e] = mine[i, lane]

    for i in range(groups):
        for h in range(2):
            at = slice(h * width, (h + 1) * width)
            value = None
            for f in range(blocks):
                number = order.index(("down", i, f))
                tile = use_tile(number) if h == 0 else tiles.at[number % SLOTS]
                more = jnp.dot(
                    hidden[:, f * TILE : (f + 1) * TILE],
                    tile[:, at],
                    preferred_element_type=f32,
                )
                value = more if value is None else value + more
            for j in range(n_ctx):
                term[i, h, j] = value[j * CAP : (j + 1) * CAP].astype(bf16)
            for far in (1, 0):
                term_copy(i, h + 1, far).start()
        for f in range(blocks):
            done_tile(order.index(("down", i, f)))
        if i > 0:
            relay_on(i - 1)
        if i > 1:
            reduce(i - 2)
    relay_on(groups - 1)
    reduce(groups - 2)
    reduce(groups - 1)

    for i in range(groups - 1):
        for number in range(2):
            out_copy(i, 0, number).wait_recv()
    sib_copy().wait_recv()
    lot = outs[...].reshape(n_exp * CAP, width)
    value = jnp.dot(combine[0], lot, preferred_element_type=f32) + jnp.dot(
        combine[1], lot, preferred_element_type=f32
    )
    stage = lax.rem(lax.rem(group, 2) + lax.rem(ctx, 2), 2) + 2 * lax.rem(
        group // 2 + ctx // 2, 2
    )
    base = stream[
        group, stage, :, :, :, pl.ds(pl.multiple_of(lane * width, 128), width)
    ].reshape(n_exp * own, width)
    out_ref[...] = (base.astype(f32) + value).astype(bf16)

    for s in range(1, n_ctx):
        ids_copy(s, ctx).wait_send()
    for i in range(groups):
        for to in (1, 2):
            for far in range(2):
                term_copy(i, to, far).wait_send()
            relay_copy(i, to - 1).wait_send()
    for s in range(n_ctx):
        for number in range(2):
            z_copy(s, number).wait_send()

        @pl.when(near)
        def _(s=s):
            for number in (1, 2):
                z_pass(s, number).wait_send()

        for to in (1, 2):
            xy_copy(to, s, ctx).wait_send()
            fwd_copy(to, s, others[3 - to]).wait_send()
        for k in range(n_ctx):
            pass_copy(k, s).wait_send()
    for i in range(groups - 1):
        for to in range(2):
            out_copy(i, to, lane).wait_send()
    sib_copy().wait_send()


    for number in range(4):
        norm_copy(1 + number // 2, ctx, number % 2, number).wait_send()
    norm_copy(2, others[1], 0, 4).wait_send()
    norm_copy(1, others[2], 1, 5).wait_send()
    for copy in rest_copies:
        copy.wait_send()
    for s in range(n_ctx):
        pair_copy(s).wait_send()
        for d in range(1, groups):
            sum_copy(s, d).wait_send()
    for d in range(1, n_ctx):

        @pl.when(ctx + d < n_ctx)
        def _(d=d):
            for i in range(4):
                block_copy(d, ctx + d, ctx, i).wait_send()


def layer(
    x, z, write, read, logits, decay_log, skip_gain, norm_gain, residual, out_weight, ids, route,
    moe_gain, gate, up, down, number,
):
    n_ctx, n_exp = lax.axis_size("ctx"), lax.axis_size("exp")
    tokens, channels = x.shape
    heads = logits.shape[0]
    cols = out_weight.shape[1]
    own_rows = tokens // n_exp
    groups = n_exp // 2
    units = gate.shape[2]
    width = cols // 2
    n_rows = n_ctx * CAP
    size = write.shape[1]
    f32, bf16, dma = jnp.float32, jnp.bfloat16, pltpu.SemaphoreType.DMA
    vmem = pltpu.VMEM
    inputs = (
        x,
        z,
        write,
        read,
        logits,
        decay_log.reshape(1, -1),
        skip_gain.reshape(1, -1),
        norm_gain.reshape(1, -1),
        residual,
        out_weight,
        ids.T,
        route.T,
        moe_gain.reshape(1, -1),
        gate,
        up,
        down,
    )
    held = [vmem(a.shape, a.dtype) for a in inputs[:13]]
    for i in (0, 2, 4):
        held[i] = vmem((n_ctx,) + inputs[i].shape, inputs[i].dtype)
    held[8] = vmem((own_rows, residual.shape[1]), bf16)
    return pl.pallas_call(
        layer_kernel,
        out_shape=jax.ShapeDtypeStruct((tokens, width), bf16),
        in_specs=[pl.BlockSpec(memory_space=pl.ANY)] * len(inputs),
        out_specs=pl.BlockSpec(memory_space=pltpu.VMEM),
        scratch_shapes=held
        + [
            vmem((n_ctx - 1, tokens, 128), f32),
            vmem((heads, tokens), f32),
            vmem((size, channels), f32),
            vmem((tokens, channels), f32),
            vmem((n_ctx, tokens, channels), bf16),
            vmem((n_ctx, 2, groups, own_rows, cols), bf16),
            vmem((n_ctx, groups, own_rows, cols), bf16),
            vmem((n_ctx, groups, own_rows, cols), bf16),
            vmem((n_ctx, groups - 1, own_rows, cols), bf16),
            vmem((n_ctx, own_rows, cols), bf16),
            vmem((n_ctx, n_ctx, groups, 2, own_rows, cols), bf16),
            vmem((SLOTS, TILE, TILE), bf16),
            vmem((n_rows, units), f32),
            vmem((n_rows, units), f32),
            vmem((n_rows, TILE), bf16),
            vmem((n_rows, units), bf16),
            vmem((groups, 2, n_ctx, CAP, width), bf16),
            vmem((groups, 2, 2, CAP, width), bf16),
            vmem((groups, 2, CAP, width), bf16),
            vmem((groups, 2, CAP, width), bf16),
            vmem((groups, 2, CAP, width), bf16),
            vmem((n_exp, CAP, width), bf16),
            vmem((n_ctx, 8, 128), f32),
            vmem((2, tokens, n_exp * CAP), bf16),
            dma((13,)),
            dma((n_ctx - 1, 4)),
            dma((n_ctx - 1, 4)),
            dma((6,)),
            dma((6,)),
            dma((n_ctx,)),
            dma((n_ctx,)),
            dma((n_ctx, groups - 1)),
            dma((n_ctx, groups - 1)),
            dma((n_ctx - 1,)),
            dma((n_ctx - 1,)),
            dma((SLOTS,)),
            dma((n_ctx, 4)),
            dma((n_ctx, 3)),
            dma((2, n_ctx)),
            dma((2, n_ctx)),
            dma((2, n_ctx)),
            dma((2, n_ctx)),
            dma((n_ctx, n_ctx)),
            dma((n_ctx, n_ctx)),
            dma((n_ctx - 1,)),
            dma((n_ctx - 1,)),
            dma((groups, 2, 2)),
            dma((groups, 2, 2)),
            dma((groups, 2)),
            dma((groups, 2)),
            dma((groups - 1, 2)),
            dma((groups - 1, 2)),
            dma,
            dma,
        ],
        compiler_params=pltpu.CompilerParams(
            collective_id=number, has_side_effects=True, vmem_limit_bytes=63 * 1024 * 1024
        ),
        cost_estimate=pl.CostEstimate(
            flops=6 * n_rows * n_ctx * TILE * units,
            bytes_accessed=6 * n_ctx * TILE * units,
            transcendentals=n_rows * units,
        ),
    )(*inputs)


def body(
    residual,
    ssm_input,
    ssm_gate,
    write_vectors,
    read_vectors,
    step_logits,
    decay_log,
    skip_gain,
    norm_gain,
    out_weight,
    moe_gain,
    gate_weight,
    up_weight,
    down_weight,
    expert_ids,
    route_weight,
):
    sizes = (lax.axis_size("ctx"), lax.axis_size("exp"), step_logits.shape[1], out_weight.shape[1])
    if sizes == (4, 8, SPAN, TILE) and gate_weight.shape[2] % TILE == 0:
        return layer(
            ssm_input,
            ssm_gate,
            write_vectors,
            read_vectors,
            step_logits,
            decay_log,
            skip_gain,
            norm_gain,
            residual,
            out_weight,
            expert_ids,
            route_weight,
            moe_gain,
            gate_weight,
            up_weight,
            down_weight,
            1,
        )
    heads_dev = step_logits.shape[0]
    tok_rows = step_logits.shape[1]
    head_width = ssm_input.shape[1] // heads_dev
    span_count = tok_rows // SPAN
    step_size = jax.nn.softplus(step_logits)
    log_step = step_size * (-jnp.exp(decay_log))[:, None]
    cumulative = jnp.einsum(
        "hks,st->hkt",
        log_step.reshape(heads_dev, span_count, SPAN),
        jnp.triu(jnp.ones((SPAN, SPAN), jnp.float32)),
        precision=lax.Precision.HIGHEST,
    )
    step_blocks = step_size.reshape(heads_dev, span_count, SPAN)
    input_blocks = ssm_input.reshape(span_count, SPAN, heads_dev, head_width)
    write_blocks = write_vectors.reshape(span_count, SPAN, -1)
    read_blocks = read_vectors.reshape(span_count, SPAN, -1)
    scores = jnp.einsum(
        "ktn,ksn->kts", read_blocks, write_blocks, preferred_element_type=jnp.float32
    )
    causal = jnp.arange(SPAN)[:, None] >= jnp.arange(SPAN)[None, :]
    log_gaps = cumulative[:, :, :, None] - cumulative[:, :, None, :]
    mixing = jnp.where(
        causal,
        scores[None] * jnp.exp(jnp.where(causal, log_gaps, 0.0)) * step_blocks[:, :, None, :],
        0.0,
    ).astype(jnp.bfloat16)
    intra_out = jnp.einsum(
        "hkts,kshp->kthp", mixing, input_blocks, preferred_element_type=jnp.float32
    )
    end_weight = jnp.exp(cumulative[:, :, -1:] - cumulative) * step_blocks
    loaded = (end_weight[:, :, :, None] * write_blocks.astype(jnp.float32)[None]).astype(
        jnp.bfloat16
    )
    block_state = jnp.einsum(
        "kshp,hksn->hkpn", input_blocks, loaded, preferred_element_type=jnp.float32
    )
    block_decay = jnp.exp(cumulative[:, :, -1])
    running = jnp.zeros_like(block_state[:, 0])
    decay_run = jnp.ones_like(block_decay[:, 0])
    entering_list = [running]
    reach_list = [decay_run]
    running = block_decay[:, 0, None, None] * running + block_state[:, 0]
    decay_run = decay_run * block_decay[:, 0]
    device_state = running
    device_decay = decay_run

    all_states, all_decays = sent(
        [
            device_state.astype(jnp.bfloat16),
            jnp.broadcast_to(device_decay[:, None], (heads_dev, 128)),
        ],
        "ctx",
        1,
        True,
    )
    ctx_index = lax.axis_index("ctx")
    device_in = jnp.zeros_like(device_state)
    for j in range(lax.axis_size("ctx") - 1):
        device_in = jnp.where(
            j < ctx_index,
            all_decays[j, :, :1, None] * device_in + all_states[j].astype(jnp.float32),
            device_in,
        )
    entering = jnp.stack(entering_list, axis=1)
    reach = jnp.stack(reach_list, axis=1)
    states = entering + reach[:, :, None, None] * device_in[:, None]
    inter_out = jnp.transpose(jnp.exp(cumulative), (1, 2, 0))[:, :, :, None] * jnp.einsum(
        "ktn,hkpn->kthp", read_blocks.astype(jnp.float32), states, precision=lax.Precision.HIGHEST
    )
    scan_out = (
        intra_out + inter_out + skip_gain[None, None, :, None] * input_blocks.astype(jnp.float32)
    )
    scan_out = scan_out.reshape(tok_rows, heads_dev * head_width)
    gated_out = scan_out * jax.nn.silu(ssm_gate.astype(jnp.float32))
    grouped = gated_out.reshape(tok_rows, -1, NORM_GROUP)
    group_scale = lax.rsqrt(jnp.mean(grouped * grouped, axis=2, keepdims=True) + EPSILON)
    normed = ((grouped * group_scale).reshape(tok_rows, -1) * norm_gain).astype(jnp.bfloat16)
    ctx_count = lax.axis_size("ctx")
    exp_count = lax.axis_size("exp")
    exp_index = lax.axis_index("exp")
    width = residual.shape[1]
    slice_width = width // exp_count
    split_count = exp_count // EXPERTS
    own_rows = tok_rows // exp_count
    normed_all = sent([normed], "ctx", 2, True)[0].reshape(ctx_count * tok_rows, -1)
    ssm_terms = jnp.dot(normed_all, out_weight, preferred_element_type=jnp.float32).astype(
        jnp.bfloat16
    )
    groups = exp_count // 2
    by_owner = jnp.transpose(
        ssm_terms.reshape(ctx_count, groups, 2, own_rows, -1), (2, 1, 0, 3, 4)
    ).reshape(2, groups * ctx_count * own_rows, -1)
    halves = pair_sum(by_owner, 3)
    chips = sent([halves.reshape(groups, ctx_count * own_rows, -1)], "exp", 4, False, 2)[0]
    ssm_part = jnp.sum(chips.astype(jnp.float32), axis=0).astype(jnp.bfloat16)
    ssm_rows = sent([ssm_part.reshape(ctx_count, own_rows, -1)], "ctx", 5, False)[0]
    ssm_rows = jnp.transpose(ssm_rows, (1, 0, 2)).reshape(own_rows, width)
    own_residual = lax.dynamic_slice_in_dim(residual, exp_index * own_rows, own_rows, 0)
    stream_rows = (own_residual.astype(jnp.float32) + ssm_rows.astype(jnp.float32)).astype(
        jnp.bfloat16
    )
    token_of_slot, pick_rank = slot_tables(expert_ids)
    stream_full = gather_pairs(stream_rows, "exp", 6).reshape(tok_rows, width)
    stream_slice = lax.dynamic_slice_in_dim(stream_full, exp_index * slice_width, slice_width, 1)
    padded = jnp.concatenate(
        [stream_full, jnp.zeros((1, stream_full.shape[1]), jnp.bfloat16)], axis=0
    )
    my_slots = lax.dynamic_index_in_dim(token_of_slot, exp_index // split_count, 0, keepdims=False)
    picked = normalize(jnp.take(padded, my_slots, axis=0), moe_gain)
    normed_rows = sent([picked], "ctx", 7, True)[0].reshape(ctx_count * CAP, width)
    terms = expert_terms(normed_rows, gate_weight[0], up_weight[0], down_weight[0])
    arrived_terms = sent([terms.reshape(ctx_count, CAP, width)], "ctx", 8, False)[0]
    sums_mine = jnp.sum(arrived_terms.astype(jnp.float32), axis=0).astype(jnp.bfloat16)
    by_slice = jnp.transpose(sums_mine.reshape(CAP, exp_count, slice_width), (1, 0, 2))
    arrived = sent([by_slice], "exp", 9, False)[0].reshape(exp_count * CAP, slice_width)
    piece_expert = jnp.arange(exp_count, dtype=jnp.int32) // split_count
    slot_range = jnp.arange(CAP, dtype=jnp.int32)
    moe_slice = jnp.zeros((tok_rows, slice_width), jnp.float32)
    for k in range(expert_ids.shape[1]):
        hit_expert = expert_ids[:, k, None] == piece_expert[None, :]
        hit_slot = pick_rank[:, k, None] == slot_range[None, :]
        hits = (hit_expert[:, :, None] & hit_slot[:, None, :]).astype(jnp.bfloat16)
        picked_out = jnp.dot(
            hits.reshape(tok_rows, exp_count * CAP), arrived, preferred_element_type=jnp.float32
        )
        moe_slice = moe_slice + route_weight[:, k, None] * picked_out
    return (stream_slice.astype(jnp.float32) + moe_slice).astype(jnp.bfloat16)


def solution(mesh):
    placed = (
        P("ctx", None),
        P("ctx", "exp"),
        P("ctx", "exp"),
        P("ctx", None),
        P("ctx", None),
        P("exp", "ctx"),
        P("exp"),
        P("exp"),
        P("exp"),
        P("exp", "ctx"),
        P(),
        P("exp", None, "ctx"),
        P("exp", None, "ctx"),
        P("exp", "ctx", None),
        P("ctx", None),
        P("ctx", None),
    )
    return jax.shard_map(
        body, mesh=mesh, in_specs=placed, out_specs=P("ctx", "exp"), check_vma=False
    )
```
